128 devices in a mesh: gx: 16 (over x, z_lo, core), gy: 8 (over z_hi, y).
Axes of the slice: x: 4, y: 4, z: 4 (z_hi: 2, z_lo: 2; z = z_hi * 2 + z_lo), core: 2. Of those that a mesh axis runs over, the one named last changes fastest.
Arguments:
- fields: float32 [5, 256, 256, 128], P(None, 'gx', 'gy'), may hold values from -6 to 6
- patch_weight: bfloat16 [2560, 512], replicated, may hold values from -0.125 to 0.125
- trainer_of: int32 [8192, 1], P(('gx', 'gy')), may hold values from 0 to 127; in each aligned block of 64 rows (0 to 63, 64 to 127, ...) at most 2 rows name the same one
- lag_index: int32 [32, 32, 16], P('gx', 'gy'), may hold values from 0 to 1
- w_in: bfloat16 [128, 512, 2048], P(('gx', 'gy')), may hold values from -0.25 to 0.25
- b_in: float32 [128, 2048], P(('gx', 'gy')), may hold values from -3 to 3
- w_out: bfloat16 [128, 2048, 512], P(('gx', 'gy')), may hold values from -0.125 to 0.125
- b_out: float32 [128, 512], P(('gx', 'gy')), may hold values from -3 to 3
Outputs:
- new_fields: float32 [5, 256, 256, 128], P(None, 'gx', 'gy')
- patch_gradient: float32 [2560, 512], replicated
- w_in_gradient: float32 [128, 512, 2048], P(('gx', 'gy'))
- b_in_gradient: float32 [128, 2048], P(('gx', 'gy'))
- w_out_gradient: float32 [128, 2048, 512], P(('gx', 'gy'))
- b_out_gradient: float32 [128, 512], P(('gx', 'gy'))
The draws below stay inside these ranges and needn't reach their ends.
Inputs may be any that keep to these rules, and one draw needn't show every extreme that they name: `trainer_of`: among the 64 rows of one brick, no trainer is named more than 2 times.
All inputs are finite; a program needn't handle non-finite values.
Results may differ from the reference program's by a relative error of at most 0.0062.
Values may be sent and summed in bfloat16 or wider, within the bound.
No kernel may reach another device: no remote copies, remote signals or barrier semaphores. Data moves between devices by JAX's collectives and lax.ppermute only.
A program may use at most 128 MiB of HBM per device.

```python
import math
import jax
import jax.numpy as jnp
import numpy as np
from jax import lax

FIELDS = 5
PATCH = 8
CX = 16
CY = 32
CZ = 128
STEPS = 3
EMBED = 512
HIDDEN_SIZE = 2048
BLOCK_ROWS = 2
FEAT = 2560
NX = 256
NY = 256
NBLOCK = 64
TRAINERS = 128
SLOTS = 2
ROWS = 16384
N_GX = 16
N_GY = 8
DEVICES = 128


def with_ends(result, key, low, top_value):
    place = [jax.random.randint(jax.random.fold_in(key, axis), (), 0, length) for axis, length in enumerate(result.shape)]
    main_axis = result.shape.index(max(result.shape))
    beside = place[:main_axis] + [(place[main_axis] + 1) % result.shape[main_axis]] + place[main_axis + 1:]
    return result.at[tuple(place)].set(low).at[tuple(beside)].set(top_value)


def levels(rng, dims, pieces, least, high):
    gain, own = 1.0, jax.random.fold_in(rng, 6)
    for dim, parts in pieces:
        heights = jnp.exp(jax.random.uniform(jax.random.fold_in(own, dim), (parts,), jnp.float32, least / len(pieces), high / len(pieces)))
        gain = gain * jnp.repeat(heights, dims[dim] // parts).reshape([-1 if axis == dim else 1 for axis in range(len(dims))])
    return gain


def shared_out(stream_key, own, number, rows, count, top, reach, lean):
    sequence = jax.random.permutation(stream_key, count)
    heavy_load, common = shares(count, rows * top, reach, lean, True), shares(count, rows * top, reach, lean, False)
    places = jnp.arange(count)

    def named(sizes, turn):
        used = int((sizes > 0).sum())
        fixed = max(1, used // 4)
        moved = fixed + (places - fixed + turn * (used - fixed)) % max(1, count - fixed)
        return jnp.zeros((count,), jnp.int32).at[sequence[jnp.where(places < fixed, places, moved)]].set(jnp.asarray(sizes, jnp.int32))

    sizes = jnp.where(number % 4 == 0, named(heavy_load, number // 4), named(common, number - number // 4 - 1))
    mixed = jax.random.permutation(jax.random.fold_in(own, 3), count)
    donor, sink = mixed[0:count // 2 * 2:2], mixed[1:count // 2 * 2:2]
    slack = jnp.minimum(sizes[donor] - 1, reach - sizes[sink]) // 2
    slack = jnp.where((donor == sequence[0]) | (sink == sequence[0]) | (sizes[sink] == 0), 0, jnp.maximum(slack, 0))
    moved = jax.random.randint(jax.random.fold_in(own, 4), (count // 2,), 0, 1 << 20) % (slack + 1)
    sizes = sizes.at[donor].add(-moved).at[sink].add(moved)
    members = jnp.searchsorted(jnp.cumsum(sizes), jnp.arange(rows * top), side="right").astype(jnp.int32)
    listing = members.reshape(top, rows).T
    listing = listing[jax.random.permutation(jax.random.fold_in(own, 1), rows)]
    turn = jax.random.randint(jax.random.fold_in(own, 2), (rows, 1), 0, top)
    return jnp.take_along_axis(listing, (jnp.arange(top)[None, :] + turn) % top, axis=1)


def shares(number_of, total, reach, lean, full):
    portions = [(1 << 20) // math.isqrt(rank ** lean) + 1 for rank in range(1, number_of + 1)]
    largest = reach if full else min(reach, max(-(-total // number_of), total * portions[0] // sum(portions)))
    least = 1 if total - largest >= number_of - 1 else 0
    counts, spare = [largest] + [least] * (number_of - 1), total - largest - least * (number_of - 1)
    while spare > 0:
        movable = [i for i in range(1, number_of) if counts[i] < largest] or [i for i in range(1, number_of) if counts[i] < reach]
        mass, remaining = sum([portions[i] for i in movable]), spare
        for i in movable:
            more = min(reach - counts[i], max(1, remaining * portions[i] // mass), spare)
            counts[i] = counts[i] + more
            spare = spare - more
    return np.array(counts)


def centred(own_key, dims, deviation, most, shards=(), kind=jnp.bfloat16):
    entries = jax.random.normal(own_key, dims, jnp.float32) * deviation
    if len(shards) > 0:
        entries = levels(own_key, dims, shards, -0.22, 0.18) * entries
    return jnp.clip(entries, min=-most, max=most).astype(kind)


def setup_inputs(seed: int = 0) -> dict:
    splits = jax.random.split(jax.random.key(seed), 9)
    fields = centred(splits[0], (FIELDS, NX, NY, CZ), 1.0, 6.0, ((1, 16), (2, 8)), jnp.float32)
    patch_weight = centred(splits[1], (FEAT, EMBED), FEAT ** -0.5, 0.125)
    trainer_of_keys = jax.random.split(jax.random.fold_in(splits[2], 1), (TRAINERS * NBLOCK) // NBLOCK)
    trainer_of_turns = jax.random.permutation(jax.random.fold_in(splits[2], 3), (TRAINERS * NBLOCK) // NBLOCK)
    trainer_of = jax.vmap(lambda own, number: shared_out(jax.random.fold_in(splits[2], 2), own, number, NBLOCK, TRAINERS, 1, SLOTS, 2))(trainer_of_keys, trainer_of_turns).reshape((TRAINERS * NBLOCK, 1))
    lag_index = with_ends(jax.random.randint(splits[3], (NX // PATCH, NY // PATCH, CZ // PATCH), 0, STEPS - 1), jax.random.fold_in(splits[3], 1), 0, (STEPS - 1) - 1).astype(jnp.int32)
    w_in = centred(splits[4], (TRAINERS, EMBED, HIDDEN_SIZE), EMBED ** -0.5, 0.25, ((0, 128),))
    b_in = centred(splits[5], (TRAINERS, HIDDEN_SIZE), 0.5, 3.0, ((0, 128),), jnp.float32)
    w_out = centred(splits[6], (TRAINERS, HIDDEN_SIZE, EMBED), HIDDEN_SIZE ** -0.5, 0.125, ((0, 128),))
    b_out = centred(splits[7], (TRAINERS, EMBED), 0.5, 3.0, ((0, 128),), jnp.float32)
    return {"fields": fields, "patch_weight": patch_weight, "trainer_of": trainer_of, "lag_index": lag_index, "w_in": w_in, "b_in": b_in, "w_out": w_out, "b_out": b_out}


time_step = 0.2
viscosity = 0.5
drift_x = 0.6
drift_y = -0.4
drift_z = 0.3
error_weight = 0.0625


def shifted(padded, dimension, offset):
    window = [slice(None)]
    for other in (1, 2, 3):
        window.append(slice(2, padded.shape[other] - 2))
    window[dimension] = slice(2 + offset, padded.shape[dimension] - 2 + offset)
    return padded[tuple(window)]


def tendency(padded):
    gradients = []
    laplacian = 0.0
    for dimension in (1, 2, 3):
        back_two = shifted(padded, dimension, -2)
        back_one = shifted(padded, dimension, -1)
        middle = shifted(padded, dimension, 0)
        ahead_one = shifted(padded, dimension, 1)
        ahead_two = shifted(padded, dimension, 2)
        gradients.append((back_two - 8.0 * back_one + 8.0 * ahead_one - ahead_two) / 12.0)
        laplacian = laplacian + (-back_two + 16.0 * back_one - 30.0 * middle + 16.0 * ahead_one - ahead_two) / 12.0
    carried = drift_x * gradients[0] + drift_y * gradients[1] + drift_z * gradients[2]
    divergence = gradients[0][1] + gradients[1][2] + gradients[2][3]
    acoustic = jnp.stack([divergence, gradients[0][4], gradients[1][4], gradients[2][4], divergence])
    return viscosity * laplacian - carried - acoustic


def contract_rows(left, right):
    return lax.dot_general(left, right, (((0,), (0,)), ((), ())), preferred_element_type=jnp.float32)


def contract_cols(left, right):
    return lax.dot_general(left, right, (((1,), (1,)), ((), ())), preferred_element_type=jnp.float32)


def trainer_step(source, target, valid, w_first, b_first, w_second, b_second):
    pre = jnp.dot(source, w_first, preferred_element_type=jnp.float32) + b_first
    hidden = jax.nn.silu(pre).astype(jnp.bfloat16)
    predict = jnp.dot(hidden, w_second, preferred_element_type=jnp.float32) + b_second
    error = (error_weight * (predict - target.astype(jnp.float32)) * valid).astype(jnp.bfloat16)
    b_second_grad = jnp.sum(error.astype(jnp.float32), axis=0)
    w_second_grad = contract_rows(hidden, error)
    back = contract_cols(error, w_second)
    sigma = jax.nn.sigmoid(pre)
    pre_grad = (back * sigma * (1.0 + pre * (1.0 - sigma))).astype(jnp.bfloat16)
    b_first_grad = jnp.sum(pre_grad.astype(jnp.float32), axis=0)
    w_first_grad = contract_rows(source, pre_grad)
    source_grad = contract_cols(pre_grad, w_first).astype(jnp.bfloat16)
    return source_grad, w_first_grad, b_first_grad, w_second_grad, b_second_grad


def patchify(state):
    shaped = state.reshape(FIELDS, N_GX, CX // PATCH, PATCH, N_GY, CY // PATCH, PATCH, CZ // PATCH, PATCH)
    return shaped.transpose(1, 4, 2, 5, 7, 0, 3, 6, 8).reshape(ROWS, FEAT)


def one_trainer(operands):
    return trainer_step(*operands)


def reference(fields, patch_weight, trainer_of, lag_index, w_in, b_in, w_out, b_out):
    current = fields
    states = []
    for counter in range(STEPS):
        padded = jnp.pad(current, ((0, 0), (2, 2), (2, 2), (2, 2)))
        current = current + time_step * tendency(padded)
        states.append(current)
    lag_rows = lag_index.reshape(N_GX, CX // PATCH, N_GY, CY // PATCH, CZ // PATCH)
    lag_rows = lag_rows.transpose(0, 2, 1, 3, 4).reshape(ROWS, 1)
    picked = patchify(states[0].astype(jnp.bfloat16))
    for counter in range(1, STEPS - 1):
        picked = jnp.where(lag_rows == counter, patchify(states[counter].astype(jnp.bfloat16)), picked)
    source = jnp.dot(picked, patch_weight, preferred_element_type=jnp.float32).astype(jnp.bfloat16)
    target = jnp.dot(patchify(current.astype(jnp.bfloat16)), patch_weight,
                     preferred_element_type=jnp.float32).astype(jnp.bfloat16)
    owners = trainer_of[:, 0].reshape(DEVICES, NBLOCK)
    onehot = (owners[:, :, None] == jnp.arange(TRAINERS, dtype=jnp.int32)[None, None, :]).astype(jnp.int32)
    within_rank = jnp.sum((jnp.cumsum(onehot, axis=1) - onehot) * onehot, axis=2)
    senders = jnp.arange(DEVICES, dtype=jnp.int32)[:, None]
    slot_block = (owners * DEVICES + senders) * SLOTS + within_rank
    slot_row = (slot_block[:, :, None] * BLOCK_ROWS + jnp.arange(BLOCK_ROWS, dtype=jnp.int32)[None, None, :])
    slot_row = slot_row.reshape(ROWS).astype(jnp.int32)
    capacity = TRAINERS * DEVICES * SLOTS * BLOCK_ROWS
    per_trainer = DEVICES * SLOTS * BLOCK_ROWS
    packed_source = jnp.zeros((capacity, EMBED), source.dtype).at[slot_row].set(source)
    packed_target = jnp.zeros((capacity, EMBED), target.dtype).at[slot_row].set(target)
    packed_valid = jnp.zeros((capacity, 1), jnp.float32).at[slot_row].set(1.0)
    results = lax.map(one_trainer, (packed_source.reshape(TRAINERS, per_trainer, EMBED),
                                    packed_target.reshape(TRAINERS, per_trainer, EMBED),
                                    packed_valid.reshape(TRAINERS, per_trainer, 1),
                                    w_in, b_in, w_out, b_out))
    source_grad = results[0].reshape(capacity, EMBED)[slot_row]
    patch_gradient = contract_rows(picked, source_grad)
    return current, patch_gradient, results[1], results[2], results[3], results[4]
```

```python
import functools

import jax
import jax.numpy as jnp
from jax import lax
from jax.experimental import pallas as pl
from jax.experimental.pallas import tpu as pltpu
from jax.sharding import PartitionSpec as P

FIELDS = 5
PATCH = 8
STEPS = 3
EMBED = 512
BLOCK_ROWS = 2
REACH = 2 * STEPS
LIFT = 8

time_step = 0.2
viscosity = 0.5
drift_x = 0.6
drift_y = -0.4
drift_z = 0.3
error_weight = 0.0625

SLOPE = {-2: 1.0 / 12.0, -1: -8.0 / 12.0, 1: 8.0 / 12.0, 2: -1.0 / 12.0}
BEND = {-2: -1.0 / 12.0, -1: 16.0 / 12.0, 1: 16.0 / 12.0, 2: -1.0 / 12.0}
OFFSETS = (-2, -1, 1, 2)


def own_weights(drift):
    return {k: time_step * (viscosity * BEND[k] - drift * SLOPE[k]) for k in OFFSETS}


OWN_X, OWN_Y, OWN_Z = own_weights(drift_x), own_weights(drift_y), own_weights(drift_z)
MIDDLE = 1.0 - time_step * viscosity * 3.0 * 30.0 / 12.0
PUSH = {k: -time_step * SLOPE[k] for k in OFFSETS}


def rolled(value, offset, axis):
    size = value.shape[axis]
    return pltpu.roll(value, (-offset) % size, axis)


def weighted(pieces, weights):
    total = None
    for k in OFFSETS:
        term = pieces[k] * weights[k]
        total = term if total is None else total + term
    return total


def slope_of(pieces):
    return (pieces[-1] - pieces[1]) * PUSH[-1] + (pieces[2] - pieces[-2]) * PUSH[2]


def one_row(src, row, own_z, push_z, window):
    def along(field):
        middle = src[field, row]
        xs = {k: src[field, row + k] for k in OFFSETS}
        ys = {k: rolled(middle, k, 0) for k in OFFSETS}
        zs = {k: rolled(middle, k, 1) for k in OFFSETS}
        return middle, xs, ys, zs

    def own(middle, xs, ys, zs):
        return (
            middle * MIDDLE + weighted(xs, OWN_X) + weighted(ys, OWN_Y) + weighted(zs, own_z)
        )

    cut = (lambda v: v) if window is None else (lambda v: v[window[0] : window[1]])
    parts = along(4)
    pressure = cut(own(*parts))
    px, py, pz = cut(slope_of(parts[1])), cut(slope_of(parts[2])), cut(weighted(parts[3], push_z))
    parts = along(1)
    first = cut(own(*parts)) + px
    spread = cut(slope_of(parts[1]))
    parts = along(2)
    second = cut(own(*parts)) + py
    spread = spread + cut(slope_of(parts[2]))
    parts = along(3)
    third = cut(own(*parts)) + pz
    spread = spread + cut(weighted(parts[3], push_z))
    parts = along(0)
    density = cut(own(*parts)) + spread
    return density, first, second, third, pressure + spread


def slot_rows(owner_row, owner_col, patches):
    earlier_r = lax.broadcasted_iota(jnp.int32, (patches, patches), 0)
    earlier_c = lax.broadcasted_iota(jnp.int32, (patches, patches), 1)
    same = owner_row == owner_col
    half_r, half_c = earlier_r // BLOCK_ROWS, earlier_c // BLOCK_ROWS
    return same, earlier_r, earlier_c, half_r, half_c


def target_rows(owner_row, owner_col, patches, slots, along_lanes):
    same, at_r, at_c, half_r, half_c = slot_rows(owner_row, owner_col, patches)
    if along_lanes:
        hit = same & (half_r < half_c) & (at_r % BLOCK_ROWS == 0)
        rank = jnp.sum(jnp.where(hit, 1.0, 0.0), axis=0, keepdims=True).astype(jnp.int32)
        place = lax.broadcasted_iota(jnp.int32, (1, patches), 1) % BLOCK_ROWS
        owner = owner_row
    else:
        hit = same & (half_c < half_r) & (at_c % BLOCK_ROWS == 0)
        rank = jnp.sum(jnp.where(hit, 1.0, 0.0), axis=1, keepdims=True).astype(jnp.int32)
        place = lax.broadcasted_iota(jnp.int32, (patches, 1), 0) % BLOCK_ROWS
        owner = owner_col
    return (owner * slots + rank) * BLOCK_ROWS + place


def window_kernel(
    shape,
    rows,
    slots,
    edge_ref,
    f_ref,
    xlo_ref,
    xhi_ref,
    ylo_ref,
    yhi_ref,
    lag_ref,
    own_row_ref,
    own_col_ref,
    w_ref,
    new_ref,
    picked_ref,
    send_ref,
    first_ref,
    second_ref,
    shuffle_ref,
    natural_ref,
    both_ref,
):
    wide_x, wide_y, wide_z = shape
    patches = (wide_x // PATCH) * (wide_y // PATCH) * (wide_z // PATCH)
    top_x, top_y = REACH + wide_x, LIFT + wide_y
    full_x, full_y = top_x + REACH, top_y + LIFT
    lane = lax.broadcasted_iota(jnp.int32, (1, wide_z), 1)
    inside = {k: (lane + k >= 0) & (lane + k < wide_z) for k in OFFSETS}
    own_z = {k: jnp.where(inside[k], OWN_Z[k], 0.0) for k in OFFSETS}
    push_z = {k: jnp.where(inside[k], PUSH[k], 0.0) for k in OFFSETS}

    first_ref[:, :, 0:LIFT, :] = jnp.zeros((FIELDS, full_x, LIFT, wide_z), jnp.float32)
    first_ref[:, :, top_y:full_y, :] = jnp.zeros((FIELDS, full_x, LIFT, wide_z), jnp.float32)
    first_ref[:, REACH:top_x, LIFT:top_y, :] = f_ref[...]
    first_ref[:, 0:REACH, LIFT:top_y, :] = xlo_ref[...].astype(jnp.float32)
    first_ref[:, top_x:full_x, LIFT:top_y, :] = xhi_ref[...].astype(jnp.float32)
    first_ref[:, :, LIFT - REACH : LIFT, :] = ylo_ref[...].astype(jnp.float32)
    first_ref[:, :, top_y : top_y + REACH, :] = yhi_ref[...].astype(jnp.float32)

    def clear(ref, least):
        @pl.when(edge_ref[0] == 1)
        def _():
            ref[:, least:REACH] = jnp.zeros((FIELDS, REACH - least, full_y, wide_z), jnp.float32)

        @pl.when(edge_ref[1] == 1)
        def _():
            ref[:, top_x : full_x - least] = jnp.zeros(
                (FIELDS, REACH - least, full_y, wide_z), jnp.float32
            )

        @pl.when(edge_ref[2] == 1)
        def _():
            ref[:, :, 0:LIFT] = jnp.zeros((FIELDS, full_x, LIFT, wide_z), jnp.float32)

        @pl.when(edge_ref[3] == 1)
        def _():
            ref[:, :, top_y:full_y] = jnp.zeros((FIELDS, full_x, LIFT, wide_z), jnp.float32)

    def step(src, dst, least):
        def body(row, carry):
            done = one_row(src, row, own_z, push_z, None)
            for field in range(FIELDS):
                dst[field, row] = done[field]
            return carry

        lax.fori_loop(least, full_x - least, body, 0)
        clear(dst, least)

    def last_step(src):
        def body(row, carry):
            done = one_row(src, row, own_z, push_z, (LIFT, top_y))
            for field in range(FIELDS):
                new_ref[field, row - REACH] = done[field]
            return carry

        lax.fori_loop(REACH, top_x, body, 0)

    z_count = wide_z // PATCH
    lane_r = lax.broadcasted_iota(jnp.int32, (wide_z, wide_z), 0)
    lane_c = lax.broadcasted_iota(jnp.int32, (wide_z, wide_z), 1)
    swap = jnp.where(
        (lane_r // PATCH == lane_c % z_count) & (lane_r % PATCH == lane_c // z_count), 1.0, 0.0
    ).astype(jnp.bfloat16)
    group = lax.broadcasted_iota(jnp.int32, (PATCH, wide_z), 1) // z_count

    def into_patches(load, store):
        for field in range(FIELDS):
            flat = load(field).reshape(wide_x * wide_y, wide_z)
            shuffle_ref[field] = jnp.dot(
                flat.astype(jnp.bfloat16), swap, preferred_element_type=jnp.float32
            ).reshape(wide_x, wide_y, wide_z)

        def body(at, carry):
            field, inner = at // PATCH, at % PATCH
            tiles = [
                shuffle_ref[field, px * PATCH + inner, py * PATCH : (py + 1) * PATCH]
                for px in range(wide_x // PATCH)
                for py in range(wide_y // PATCH)
            ]
            for bit in (4, 2, 1):
                low = (group & bit) == 0
                fresh = list(tiles)
                for i in range(PATCH):
                    if i & bit:
                        continue
                    a, b = tiles[i], tiles[i | bit]
                    fresh[i] = jnp.where(low, a, pltpu.roll(b, bit * z_count, 1))
                    fresh[i | bit] = jnp.where(
                        low, pltpu.roll(a, wide_z - bit * z_count, 1), b
                    )
                tiles = fresh
            for inner_z in range(PATCH):
                natural_ref[at, pl.ds(inner_z, PATCH, stride=PATCH), :] = tiles[inner_z]
            return carry

        lax.fori_loop(0, FIELDS * PATCH, body, 0, unroll=2)
        for field in range(FIELDS):
            block = natural_ref[field * PATCH : (field + 1) * PATCH]
            block = block.reshape(PATCH**3, patches).astype(jnp.bfloat16)
            store(field * PATCH**3, block)

    def keep_picked(at, block):
        picked_ref[at : at + PATCH**3, :] = block
        both_ref[at : at + PATCH**3, 0:patches] = block

    def keep_target(at, block):
        both_ref[at : at + PATCH**3, patches : 2 * patches] = block

    def chosen(field):
        one = second_ref[field, REACH:top_x, LIFT:top_y]
        two = first_ref[field, REACH:top_x, LIFT:top_y]
        one = one.reshape(wide_x // PATCH, PATCH, wide_y, wide_z)
        two = two.reshape(wide_x // PATCH, PATCH, wide_y, wide_z)
        return jnp.where(lag_ref[...][:, None] == 1.0, two, one)

    step(first_ref, second_ref, 2)
    step(second_ref, first_ref, 4)
    last_step(first_ref)
    into_patches(chosen, keep_picked)
    into_patches(lambda field: new_ref[field], keep_target)

    embedded = lax.dot_general(
        both_ref[...], w_ref[...], (((0,), (0,)), ((), ())), preferred_element_type=jnp.float32
    ).astype(jnp.bfloat16)
    at = target_rows(own_row_ref[...], own_col_ref[...], patches, slots, True)
    chosen_rows = lax.broadcasted_iota(jnp.int32, (rows, patches), 0) == at
    select = jnp.where(chosen_rows, 1.0, 0.0).astype(jnp.bfloat16)
    for half in range(2):
        send_ref[:, half * EMBED : (half + 1) * EMBED] = jnp.dot(
            select,
            embedded[half * patches : (half + 1) * patches],
            preferred_element_type=jnp.float32,
        ).astype(jnp.bfloat16)


def closing_kernel(rows, slots, own_row_ref, own_col_ref, picked_ref, back_ref, part_ref):
    patches = picked_ref.shape[1]
    at = target_rows(own_row_ref[...], own_col_ref[...], patches, slots, False)
    chosen_rows = lax.broadcasted_iota(jnp.int32, (patches, rows), 1) == at
    select = jnp.where(chosen_rows, 1.0, 0.0).astype(jnp.bfloat16)
    gradient = jnp.dot(select, back_ref[...], preferred_element_type=jnp.float32)
    part_ref[...] = jnp.dot(
        picked_ref[...], gradient.astype(jnp.bfloat16), preferred_element_type=jnp.float32
    ).astype(part_ref.dtype)


def neighbours(low_piece, high_piece, axis):
    count = lax.axis_size(axis)
    up = [(i, i + 1) for i in range(count - 1)]
    down = [(b, a) for a, b in up]
    return lax.ppermute(high_piece, axis, up), lax.ppermute(low_piece, axis, down)


def contract_rows(left, right):
    return lax.dot_general(
        left, right, (((0,), (0,)), ((), ())), preferred_element_type=jnp.float32
    )


def contract_cols(left, right):
    return lax.dot_general(
        left, right, (((1,), (1,)), ((), ())), preferred_element_type=jnp.float32
    )


def trainer_step(source, target, valid, w_first, b_first, w_second, b_second):
    pre = jnp.dot(source, w_first, preferred_element_type=jnp.float32) + b_first
    hidden = jax.nn.silu(pre).astype(jnp.bfloat16)
    predict = jnp.dot(hidden, w_second, preferred_element_type=jnp.float32) + b_second
    error = (error_weight * (predict - target.astype(jnp.float32)) * valid).astype(jnp.bfloat16)
    b_second_grad = jnp.sum(error.astype(jnp.float32), axis=0)
    w_second_grad = contract_rows(hidden, error)
    back = contract_cols(error, w_second)
    sigma = jax.nn.sigmoid(pre)
    pre_grad = (back * sigma * (1.0 + pre * (1.0 - sigma))).astype(jnp.bfloat16)
    b_first_grad = jnp.sum(pre_grad.astype(jnp.float32), axis=0)
    w_first_grad = contract_rows(source, pre_grad)
    source_grad = contract_cols(pre_grad, w_first).astype(jnp.bfloat16)
    return (source_grad, w_first_grad, b_first_grad, w_second_grad, b_second_grad)


def per_device(fields, patch_weight, trainer_of, lag_index, w_in, b_in, w_out, b_out):
    axes = ("gx", "gy")
    n_x, n_y = lax.axis_size("gx"), lax.axis_size("gy")
    devices = n_x * n_y
    _, wide_x, wide_y, wide_z = fields.shape
    patches = (wide_x // PATCH) * (wide_y // PATCH) * (wide_z // PATCH)
    blocks = patches // BLOCK_ROWS
    slots = max(2, 2 * blocks // devices)
    rows = devices * slots * BLOCK_ROWS

    everyone = lax.all_gather(trainer_of[:, 0], axes)
    xlo, xhi = neighbours(fields[:, :REACH], fields[:, wide_x - REACH :], "gx")
    y_first = jnp.concatenate([p[:, :, :REACH] for p in (xlo, fields, xhi)], axis=1)
    y_last = jnp.concatenate([p[:, :, wide_y - REACH :] for p in (xlo, fields, xhi)], axis=1)
    ylo, yhi = neighbours(y_first, y_last, "gy")

    at_x, at_y = lax.axis_index("gx"), lax.axis_index("gy")
    edges = jnp.stack([at_x == 0, at_x == n_x - 1, at_y == 0, at_y == n_y - 1]).astype(jnp.int32)
    lag = jnp.repeat(jnp.repeat(lag_index.astype(jnp.float32), PATCH, axis=1), PATCH, axis=2)
    own_patch = jnp.repeat(trainer_of[:, 0], BLOCK_ROWS)
    own_row, own_col = own_patch[None, :], own_patch[:, None]

    vmem = pl.BlockSpec(memory_space=pltpu.VMEM)
    full = (FIELDS, wide_x + 2 * REACH, wide_y + 2 * LIFT, wide_z)
    new_fields, picked, send = pl.pallas_call(
        functools.partial(window_kernel, (wide_x, wide_y, wide_z), rows, slots),
        out_shape=(
            jax.ShapeDtypeStruct(fields.shape, jnp.float32),
            jax.ShapeDtypeStruct((FIELDS * PATCH**3, patches), jnp.bfloat16),
            jax.ShapeDtypeStruct((rows, 2 * EMBED), jnp.bfloat16),
        ),
        in_specs=[pl.BlockSpec(memory_space=pltpu.SMEM)] + [vmem] * 9,
        out_specs=(vmem, vmem, vmem),
        scratch_shapes=[
            pltpu.VMEM(full, jnp.float32),
            pltpu.VMEM(full, jnp.float32),
            pltpu.VMEM((FIELDS, wide_x, wide_y, wide_z), jnp.float32),
            pltpu.VMEM((FIELDS * PATCH, PATCH * PATCH, patches), jnp.float32),
            pltpu.VMEM((FIELDS * PATCH**3, 2 * patches), jnp.bfloat16),
        ],
        compiler_params=pltpu.CompilerParams(vmem_limit_bytes=48 * 1024 * 1024),
        name="window",
    )(edges, fields, xlo, xhi, ylo, yhi, lag, own_row, own_col, patch_weight)

    got = lax.all_to_all(send.reshape(devices, -1), axes, 0, 0, tiled=True)
    got = got.reshape(rows, 2 * EMBED)
    me = at_x * n_y + at_y
    counts = jnp.sum((everyone == me).astype(jnp.int32), axis=1)
    place = lax.broadcasted_iota(jnp.int32, (devices, slots * BLOCK_ROWS), 1) // BLOCK_ROWS
    valid = (place < counts[:, None]).astype(jnp.float32).reshape(rows, 1)
    source_grad, w_in_grad, b_in_grad, w_out_grad, b_out_grad = trainer_step(
        got[:, :EMBED], got[:, EMBED:], valid, w_in[0], b_in[0], w_out[0], b_out[0]
    )
    back = lax.all_to_all(source_grad.reshape(devices, -1), axes, 0, 0, tiled=True)
    part = pl.pallas_call(
        functools.partial(closing_kernel, rows, slots),
        out_shape=jax.ShapeDtypeStruct((FIELDS * PATCH**3, EMBED), jnp.float32),
        in_specs=[vmem] * 4,
        out_specs=vmem,
        compiler_params=pltpu.CompilerParams(vmem_limit_bytes=32 * 1024 * 1024),
        name="closing",
    )(own_row, own_col, picked, back.reshape(rows, EMBED))
    patch_gradient = lax.psum(part, axes)
    return (
        new_fields,
        patch_gradient,
        w_in_grad[None],
        b_in_grad[None],
        w_out_grad[None],
        b_out_grad[None],
    )


def solution(mesh):
    in_specs = (
        P(None, "gx", "gy", None),
        P(),
        P(("gx", "gy"), None),
        P("gx", "gy", None),
        P(("gx", "gy"), None, None),
        P(("gx", "gy"), None),
        P(("gx", "gy"), None, None),
        P(("gx", "gy"), None),
    )
    out_specs = (
        P(None, "gx", "gy", None),
        P(),
        P(("gx", "gy"), None, None),
        P(("gx", "gy"), None),
        P(("gx", "gy"), None, None),
        P(("gx", "gy"), None),
    )
    return jax.shard_map(
        per_device, mesh=mesh, in_specs=in_specs, out_specs=out_specs, check_vma=False
    )
```

```python
import functools

import jax
import jax.numpy as jnp
from jax import lax
from jax.experimental import pallas as pl
from jax.experimental.pallas import tpu as pltpu
from jax.sharding import PartitionSpec as P

FIELDS = 5
PATCH = 8
STEPS = 3
EMBED = 512
BLOCK_ROWS = 2
REACH = 2 * STEPS
LIFT = 8
EMPTY = 1.0e30
FULL_BELOW = 1.0e29

time_step = 0.2
viscosity = 0.5
drift_x = 0.6
drift_y = -0.4
drift_z = 0.3
error_weight = 0.0625

SLOPE = {-2: 1.0 / 12.0, -1: -8.0 / 12.0, 1: 8.0 / 12.0, 2: -1.0 / 12.0}
BEND = {-2: -1.0 / 12.0, -1: 16.0 / 12.0, 1: 16.0 / 12.0, 2: -1.0 / 12.0}
OFFSETS = (-2, -1, 1, 2)


def own_weights(drift):
    return {k: time_step * (viscosity * BEND[k] - drift * SLOPE[k]) for k in OFFSETS}


OWN_X, OWN_Y, OWN_Z = own_weights(drift_x), own_weights(drift_y), own_weights(drift_z)
MIDDLE = 1.0 - time_step * viscosity * 3.0 * 30.0 / 12.0
PUSH = {k: -time_step * SLOPE[k] for k in OFFSETS}


def rolled(value, offset, axis):
    size = value.shape[axis]
    return pltpu.roll(value, (-offset) % size, axis)


def weighted(pieces, weights):
    total = None
    for k in OFFSETS:
        term = pieces[k] * weights[k]
        total = term if total is None else total + term
    return total


def slope_of(pieces):
    return (pieces[-1] - pieces[1]) * PUSH[-1] + (pieces[2] - pieces[-2]) * PUSH[2]


def one_row(src, row, own_z, push_z, window):
    def along(field):
        middle = src[field, row]
        xs = {k: src[field, row + k] for k in OFFSETS}
        ys = {k: rolled(middle, k, 0) for k in OFFSETS}
        zs = {k: rolled(middle, k, 1) for k in OFFSETS}
        return middle, xs, ys, zs

    def own(middle, xs, ys, zs):
        return (
            middle * MIDDLE + weighted(xs, OWN_X) + weighted(ys, OWN_Y) + weighted(zs, own_z)
        )

    cut = (lambda v: v) if window is None else (lambda v: v[window[0] : window[1]])
    parts = along(4)
    pressure = cut(own(*parts))
    px, py, pz = cut(slope_of(parts[1])), cut(slope_of(parts[2])), cut(weighted(parts[3], push_z))
    parts = along(1)
    first = cut(own(*parts)) + px
    spread = cut(slope_of(parts[1]))
    parts = along(2)
    second = cut(own(*parts)) + py
    spread = spread + cut(slope_of(parts[2]))
    parts = along(3)
    third = cut(own(*parts)) + pz
    spread = spread + cut(weighted(parts[3], push_z))
    parts = along(0)
    density = cut(own(*parts)) + spread
    return density, first, second, third, pressure + spread


def slot_rows(owner_row, owner_col, patches):
    earlier_r = lax.broadcasted_iota(jnp.int32, (patches, patches), 0)
    earlier_c = lax.broadcasted_iota(jnp.int32, (patches, patches), 1)
    same = owner_row == owner_col
    half_r, half_c = earlier_r // BLOCK_ROWS, earlier_c // BLOCK_ROWS
    return same, earlier_r, earlier_c, half_r, half_c


def target_rows(owner_row, owner_col, patches, slots, along_lanes):
    same, at_r, at_c, half_r, half_c = slot_rows(owner_row, owner_col, patches)
    if along_lanes:
        hit = same & (half_r < half_c) & (at_r % BLOCK_ROWS == 0)
        rank = jnp.sum(jnp.where(hit, 1.0, 0.0), axis=0, keepdims=True).astype(jnp.int32)
        place = lax.broadcasted_iota(jnp.int32, (1, patches), 1) % BLOCK_ROWS
        owner = owner_row
    else:
        hit = same & (half_c < half_r) & (at_c % BLOCK_ROWS == 0)
        rank = jnp.sum(jnp.where(hit, 1.0, 0.0), axis=1, keepdims=True).astype(jnp.int32)
        place = lax.broadcasted_iota(jnp.int32, (patches, 1), 0) % BLOCK_ROWS
        owner = owner_col
    return owner, rank * BLOCK_ROWS + place


def window_kernel(
    shape,
    rows,
    slots,
    edge_ref,
    f_ref,
    xlo_ref,
    xhi_ref,
    ylo_ref,
    yhi_ref,
    lag_ref,
    own_row_ref,
    own_col_ref,
    w_ref,
    new_ref,
    keep_ref,
    give_ref,
    send_ref,
    first_ref,
    second_ref,
    shuffle_ref,
    natural_ref,
    both_ref,
):
    wide_x, wide_y, wide_z = shape
    patches = (wide_x // PATCH) * (wide_y // PATCH) * (wide_z // PATCH)
    top_x, top_y = REACH + wide_x, LIFT + wide_y
    full_x, full_y = top_x + REACH, top_y + LIFT
    lane = lax.broadcasted_iota(jnp.int32, (1, wide_z), 1)
    inside = {k: (lane + k >= 0) & (lane + k < wide_z) for k in OFFSETS}
    own_z = {k: jnp.where(inside[k], OWN_Z[k], 0.0) for k in OFFSETS}
    push_z = {k: jnp.where(inside[k], PUSH[k], 0.0) for k in OFFSETS}

    first_ref[:, REACH:top_x, LIFT:top_y, :] = f_ref[...]
    first_ref[:, 0:REACH, LIFT:top_y, :] = xlo_ref[...].astype(jnp.float32)
    first_ref[:, top_x:full_x, LIFT:top_y, :] = xhi_ref[...].astype(jnp.float32)
    first_ref[:, :, 0:LIFT, :] = ylo_ref[...].astype(jnp.float32)
    first_ref[:, :, top_y:full_y, :] = yhi_ref[...].astype(jnp.float32)

    def clear(ref, least):
        @pl.when(edge_ref[0] == 1)
        def _():
            ref[:, least:REACH] = jnp.zeros((FIELDS, REACH - least, full_y, wide_z), jnp.float32)

        @pl.when(edge_ref[1] == 1)
        def _():
            ref[:, top_x : full_x - least] = jnp.zeros(
                (FIELDS, REACH - least, full_y, wide_z), jnp.float32
            )

        @pl.when(edge_ref[2] == 1)
        def _():
            ref[:, :, 0:LIFT] = jnp.zeros((FIELDS, full_x, LIFT, wide_z), jnp.float32)

        @pl.when(edge_ref[3] == 1)
        def _():
            ref[:, :, top_y:full_y] = jnp.zeros((FIELDS, full_x, LIFT, wide_z), jnp.float32)

    def step(src, dst, least):
        def body(row, carry):
            done = one_row(src, row, own_z, push_z, None)
            for field in range(FIELDS):
                dst[field, row] = done[field]
            return carry

        lax.fori_loop(least, full_x - least, body, 0)
        clear(dst, least)

    def last_step(src):
        def body(row, carry):
            done = one_row(src, row, own_z, push_z, (LIFT, top_y))
            for field in range(FIELDS):
                new_ref[field, row - REACH] = done[field]
            return carry

        lax.fori_loop(REACH, top_x, body, 0)

    z_count = wide_z // PATCH
    lane_r = lax.broadcasted_iota(jnp.int32, (wide_z, wide_z), 0)
    lane_c = lax.broadcasted_iota(jnp.int32, (wide_z, wide_z), 1)
    swap = jnp.where(
        (lane_r // PATCH == lane_c % z_count) & (lane_r % PATCH == lane_c // z_count), 1.0, 0.0
    ).astype(jnp.bfloat16)
    group = lax.broadcasted_iota(jnp.int32, (PATCH, wide_z), 1) // z_count

    def into_patches(load, store):
        for field in range(FIELDS):
            flat = load(field).reshape(wide_x * wide_y, wide_z)
            shuffle_ref[field] = jnp.dot(
                flat.astype(jnp.bfloat16), swap, preferred_element_type=jnp.float32
            ).reshape(wide_x, wide_y, wide_z)

        def body(at, carry):
            field, inner = at // PATCH, at % PATCH
            tiles = [
                shuffle_ref[field, px * PATCH + inner, py * PATCH : (py + 1) * PATCH]
                for px in range(wide_x // PATCH)
                for py in range(wide_y // PATCH)
            ]
            for bit in (4, 2, 1):
                low = (group & bit) == 0
                fresh = list(tiles)
                for i in range(PATCH):
                    if i & bit:
                        continue
                    a, b = tiles[i], tiles[i | bit]
                    fresh[i] = jnp.where(low, a, pltpu.roll(b, bit * z_count, 1))
                    fresh[i | bit] = jnp.where(
                        low, pltpu.roll(a, wide_z - bit * z_count, 1), b
                    )
                tiles = fresh
            for inner_z in range(PATCH):
                natural_ref[at, pl.ds(inner_z, PATCH, stride=PATCH), :] = tiles[inner_z]
            return carry

        lax.fori_loop(0, FIELDS * PATCH, body, 0, unroll=2)
        for field in range(FIELDS):
            block = natural_ref[field * PATCH : (field + 1) * PATCH]
            block = block.reshape(PATCH**3, patches).astype(jnp.bfloat16)
            store(field * PATCH**3, block)

    def keep_picked(at, block):
        both_ref[at : at + PATCH**3, 0:patches] = block

    def keep_target(at, block):
        both_ref[at : at + PATCH**3, patches : 2 * patches] = block

    def chosen(field):
        one = second_ref[field, REACH:top_x, LIFT:top_y]
        two = first_ref[field, REACH:top_x, LIFT:top_y]
        one = one.reshape(wide_x // PATCH, PATCH, wide_y, wide_z)
        two = two.reshape(wide_x // PATCH, PATCH, wide_y, wide_z)
        return jnp.where(lag_ref[...][:, None] == 1.0, two, one)

    step(first_ref, second_ref, 2)
    step(second_ref, first_ref, 4)
    last_step(first_ref)
    into_patches(chosen, keep_picked)
    into_patches(lambda field: new_ref[field], keep_target)

    embedded = lax.dot_general(
        both_ref[...], w_ref[...], (((0,), (0,)), ((), ())), preferred_element_type=jnp.float32
    ).astype(jnp.bfloat16)
    half = both_ref.shape[0] // 2
    mine = pl.multiple_of(edge_ref[4] * half, half)
    keep_ref[...] = both_ref[pl.ds(mine, half), 0:patches]
    give_ref[...] = both_ref[pl.ds(half - mine, half), 0:patches]
    owner, slot = target_rows(own_row_ref[...], own_col_ref[...], patches, slots, True)
    per = slots * BLOCK_ROWS
    row = lax.broadcasted_iota(jnp.int32, (rows, patches), 0)
    source_at = owner * (2 * per) + slot
    is_source = row == source_at
    is_target = row == source_at + per
    source_pick = jnp.where(is_source, 1.0, 0.0).astype(jnp.bfloat16)
    target_pick = jnp.where(is_target, 1.0, 0.0)
    filled = jnp.sum(target_pick, axis=1, keepdims=True)
    target_half = (lax.broadcasted_iota(jnp.int32, (rows, 1), 0) // per) % 2 == 1
    marker = jnp.where(target_half & (filled == 0.0), EMPTY, 0.0)
    placed = jnp.dot(source_pick, embedded[0:patches], preferred_element_type=jnp.float32)
    placed = placed + jnp.dot(
        target_pick.astype(jnp.bfloat16),
        embedded[patches : 2 * patches],
        preferred_element_type=jnp.float32,
    )
    send_ref[...] = (placed + marker).astype(jnp.bfloat16)


def gather_kernel(rows, slots, own_row_ref, own_col_ref, back_ref, out_ref):
    patches = own_row_ref.shape[1]
    owner, slot = target_rows(own_row_ref[...], own_col_ref[...], patches, slots, False)
    at = owner * (slots * BLOCK_ROWS) + slot
    chosen_rows = lax.broadcasted_iota(jnp.int32, (patches, rows), 1) == at
    select = jnp.where(chosen_rows, 1.0, 0.0).astype(jnp.bfloat16)
    out_ref[...] = jnp.dot(
        select, back_ref[...], preferred_element_type=jnp.float32
    ).astype(jnp.bfloat16)


def part_kernel(keep_ref, got_ref, own_grad_ref, other_grad_ref, part_ref):
    half = keep_ref.shape[0]
    width = part_ref.shape[1]
    total = jnp.dot(keep_ref[...], own_grad_ref[...], preferred_element_type=jnp.float32)
    total = total + jnp.dot(
        got_ref[...], other_grad_ref[...], preferred_element_type=jnp.float32
    )
    for side in range(EMBED // width):
        part_ref[side * half : (side + 1) * half, :] = total[
            :, side * width : (side + 1) * width
        ].astype(jnp.bfloat16)


def sum_kernel(parts_ref, copies_ref):
    total = jnp.sum(parts_ref[...].astype(jnp.float32), axis=0).astype(jnp.bfloat16)
    copies_ref[...] = jnp.broadcast_to(total[None], copies_ref.shape)


def spread_kernel(core_ref, own_ref, other_ref, out_ref):
    half, width = out_ref.shape[0] // 2, own_ref.shape[1]
    mine = pl.multiple_of(core_ref[0] * half, half)
    for side in range(EMBED // width):
        lanes = slice(side * width, (side + 1) * width)
        rows = slice(side * half, (side + 1) * half)
        out_ref[pl.ds(mine, half), lanes] = own_ref[rows].astype(jnp.float32)
        out_ref[pl.ds(half - mine, half), lanes] = other_ref[rows].astype(jnp.float32)


def neighbours(low_piece, high_piece, axis):
    count = lax.axis_size(axis)
    up = [(i, i + 1) for i in range(count - 1)]
    down = [(b, a) for a, b in up]
    return lax.ppermute(high_piece, axis, up), lax.ppermute(low_piece, axis, down)


def contract_rows(left, right):
    return lax.dot_general(
        left, right, (((0,), (0,)), ((), ())), preferred_element_type=jnp.float32
    )


def contract_cols(left, right):
    return lax.dot_general(
        left, right, (((1,), (1,)), ((), ())), preferred_element_type=jnp.float32
    )


def trainer_step(source, target, w_first, b_first, w_second, b_second):
    pre = jnp.dot(source, w_first, preferred_element_type=jnp.float32) + b_first
    hidden = jax.nn.silu(pre).astype(jnp.bfloat16)
    predict = jnp.dot(hidden, w_second, preferred_element_type=jnp.float32) + b_second
    wanted = target.astype(jnp.float32)
    error = jnp.where(wanted < FULL_BELOW, error_weight * (predict - wanted), 0.0)
    error = error.astype(jnp.bfloat16)
    b_second_grad = jnp.sum(error.astype(jnp.float32), axis=0)
    w_second_grad = contract_rows(hidden, error)
    back = contract_cols(error, w_second)
    sigma = jax.nn.sigmoid(pre)
    pre_grad = (back * sigma * (1.0 + pre * (1.0 - sigma))).astype(jnp.bfloat16)
    b_first_grad = jnp.sum(pre_grad.astype(jnp.float32), axis=0)
    w_first_grad = contract_rows(source, pre_grad)
    source_grad = contract_cols(pre_grad, w_first).astype(jnp.bfloat16)
    return (source_grad, w_first_grad, b_first_grad, w_second_grad, b_second_grad)


def per_device(fields, patch_weight, trainer_of, lag_index, w_in, b_in, w_out, b_out):
    axes = ("gx", "gy")
    n_x, n_y = lax.axis_size("gx"), lax.axis_size("gy")
    devices = n_x * n_y
    _, wide_x, wide_y, wide_z = fields.shape
    patches = (wide_x // PATCH) * (wide_y // PATCH) * (wide_z // PATCH)
    blocks = patches // BLOCK_ROWS
    slots = max(2, 2 * blocks // devices)
    per = slots * BLOCK_ROWS
    features = FIELDS * PATCH**3

    narrow = fields.astype(jnp.bfloat16)
    xlo, xhi = neighbours(narrow[:, :REACH], narrow[:, wide_x - REACH :], "gx")
    y_first = jnp.concatenate([p[:, :, :LIFT] for p in (xlo, narrow, xhi)], axis=1)
    y_last = jnp.concatenate([p[:, :, wide_y - LIFT :] for p in (xlo, narrow, xhi)], axis=1)
    ylo, yhi = neighbours(y_first, y_last, "gy")

    at_x, at_y = lax.axis_index("gx"), lax.axis_index("gy")
    core = at_x % 2
    edges = jnp.stack(
        [at_x == 0, at_x == n_x - 1, at_y == 0, at_y == n_y - 1, core == 1]
    ).astype(jnp.int32)
    lag = jnp.repeat(jnp.repeat(lag_index.astype(jnp.float32), PATCH, axis=1), PATCH, axis=2)
    own_patch = jnp.repeat(trainer_of[:, 0], BLOCK_ROWS)
    own_row, own_col = own_patch[None, :], own_patch[:, None]

    vmem = pl.BlockSpec(memory_space=pltpu.VMEM)
    smem = pl.BlockSpec(memory_space=pltpu.SMEM)
    grant = pltpu.CompilerParams(vmem_limit_bytes=32 * 1024 * 1024)
    full = (FIELDS, wide_x + 2 * REACH, wide_y + 2 * LIFT, wide_z)
    new_fields, keep, give, send = pl.pallas_call(
        functools.partial(window_kernel, (wide_x, wide_y, wide_z), 2 * devices * per, slots),
        out_shape=(
            jax.ShapeDtypeStruct(fields.shape, jnp.float32),
            jax.ShapeDtypeStruct((features // 2, patches), jnp.bfloat16),
            jax.ShapeDtypeStruct((features // 2, patches), jnp.bfloat16),
            jax.ShapeDtypeStruct((2 * devices * per, EMBED), jnp.bfloat16),
        ),
        in_specs=[smem] + [vmem] * 9,
        out_specs=(vmem, vmem, vmem, vmem),
        scratch_shapes=[
            pltpu.VMEM(full, jnp.float32),
            pltpu.VMEM(full, jnp.float32),
            pltpu.VMEM((FIELDS, wide_x, wide_y, wide_z), jnp.float32),
            pltpu.VMEM((FIELDS * PATCH, PATCH * PATCH, patches), jnp.float32),
            pltpu.VMEM((features, 2 * patches), jnp.bfloat16),
        ],
        compiler_params=pltpu.CompilerParams(vmem_limit_bytes=48 * 1024 * 1024),
        name="window",
    )(edges, fields, xlo, xhi, ylo, yhi, lag, own_row, own_col, patch_weight)

    pairs = [(i, i ^ 1) for i in range(n_x)]
    groups = [
        [x * n_y + y for x in range(n_x) for y in range(n_y) if x % 2 == c] for c in range(2)
    ]
    members = devices // 2
    got_picked = lax.ppermute(give, "gx", pairs)
    got = lax.all_to_all(send.reshape(devices, 2 * per, EMBED), axes, 0, 0, tiled=True)
    source_grad, w_in_grad, b_in_grad, w_out_grad, b_out_grad = trainer_step(
        got[:, :per].reshape(devices * per, EMBED),
        got[:, per:].reshape(devices * per, EMBED),
        w_in[0],
        b_in[0],
        w_out[0],
        b_out[0],
    )
    back = lax.all_to_all(source_grad.reshape(devices, per, EMBED), axes, 0, 0, tiled=True)
    own_grad = pl.pallas_call(
        functools.partial(gather_kernel, devices * per, slots),
        out_shape=jax.ShapeDtypeStruct((patches, EMBED), jnp.bfloat16),
        in_specs=[vmem] * 3,
        out_specs=vmem,
        name="gather",
    )(own_row, own_col, back.reshape(devices * per, EMBED))
    other_grad = lax.ppermute(own_grad, "gx", pairs)
    width = EMBED // 2
    piece = features // members
    parts = pl.pallas_call(
        part_kernel,
        out_shape=jax.ShapeDtypeStruct((features, width), jnp.bfloat16),
        in_specs=[vmem] * 4,
        out_specs=vmem,
        compiler_params=grant,
        name="part",
    )(keep, got_picked, own_grad, other_grad)
    parts = lax.all_to_all(
        parts.reshape(members, piece, width), axes, 0, 0, axis_index_groups=groups, tiled=True
    )
    copies = pl.pallas_call(
        sum_kernel,
        out_shape=jax.ShapeDtypeStruct((members, piece, width), jnp.bfloat16),
        in_specs=[vmem],
        out_specs=vmem,
        compiler_params=grant,
        name="total",
    )(parts)
    own_half = lax.all_to_all(copies, axes, 0, 0, axis_index_groups=groups, tiled=True)
    own_half = own_half.reshape(features, width)
    other_half = lax.ppermute(own_half, "gx", pairs)
    patch_gradient = pl.pallas_call(
        spread_kernel,
        out_shape=jax.ShapeDtypeStruct((features, EMBED), jnp.float32),
        in_specs=[smem, vmem, vmem],
        out_specs=vmem,
        compiler_params=grant,
        name="spread",
    )(edges[4:5], own_half, other_half)
    return (
        new_fields,
        patch_gradient,
        w_in_grad[None],
        b_in_grad[None],
        w_out_grad[None],
        b_out_grad[None],
    )


def solution(mesh):
    in_specs = (
        P(None, "gx", "gy", None),
        P(),
        P(("gx", "gy"), None),
        P("gx", "gy", None),
        P(("gx", "gy"), None, None),
        P(("gx", "gy"), None),
        P(("gx", "gy"), None, None),
        P(("gx", "gy"), None),
    )
    out_specs = (
        P(None, "gx", "gy", None),
        P(),
        P(("gx", "gy"), None, None),
        P(("gx", "gy"), None),
        P(("gx", "gy"), None, None),
        P(("gx", "gy"), None),
    )
    return jax.shard_map(
        per_device, mesh=mesh, in_specs=in_specs, out_specs=out_specs, check_vma=False
    )
```

```python
import functools

import jax
import jax.numpy as jnp
from jax import lax
from jax.experimental import pallas as pl
from jax.experimental.pallas import tpu as pltpu
from jax.sharding import PartitionSpec as P

FIELDS = 5
PATCH = 8
STEPS = 3
EMBED = 512
BLOCK_ROWS = 2
REACH = 2 * STEPS
LIFT = 8
EMPTY = 1.0e30
FULL_BELOW = 1.0e29

time_step = 0.2
viscosity = 0.5
drift_x = 0.6
drift_y = -0.4
drift_z = 0.3
error_weight = 0.0625

SLOPE = {-2: 1.0 / 12.0, -1: -8.0 / 12.0, 1: 8.0 / 12.0, 2: -1.0 / 12.0}
BEND = {-2: -1.0 / 12.0, -1: 16.0 / 12.0, 1: 16.0 / 12.0, 2: -1.0 / 12.0}
OFFSETS = (-2, -1, 1, 2)


def own_weights(drift):
    return {k: time_step * (viscosity * BEND[k] - drift * SLOPE[k]) for k in OFFSETS}


OWN_X, OWN_Y, OWN_Z = own_weights(drift_x), own_weights(drift_y), own_weights(drift_z)
MIDDLE = 1.0 - time_step * viscosity * 3.0 * 30.0 / 12.0
PUSH = {k: -time_step * SLOPE[k] for k in OFFSETS}


def rolled(value, offset, axis):
    size = value.shape[axis]
    return pltpu.roll(value, (-offset) % size, axis)


def weighted(pieces, weights):
    total = None
    for k in OFFSETS:
        term = pieces[k] * weights[k]
        total = term if total is None else total + term
    return total


def slope_of(pieces):
    return (pieces[-1] - pieces[1]) * PUSH[-1] + (pieces[2] - pieces[-2]) * PUSH[2]


def one_row(src, row, own_z, push_z, window):
    def along(field):
        middle = src[field, row]
        xs = {k: src[field, row + k] for k in OFFSETS}
        ys = {k: rolled(middle, k, 0) for k in OFFSETS}
        zs = {k: rolled(middle, k, 1) for k in OFFSETS}
        return middle, xs, ys, zs

    def own(middle, xs, ys, zs):
        return (
            middle * MIDDLE + weighted(xs, OWN_X) + weighted(ys, OWN_Y) + weighted(zs, own_z)
        )

    cut = (lambda v: v) if window is None else (lambda v: v[window[0] : window[1]])
    parts = along(4)
    pressure = cut(own(*parts))
    px, py, pz = cut(slope_of(parts[1])), cut(slope_of(parts[2])), cut(weighted(parts[3], push_z))
    parts = along(1)
    first = cut(own(*parts)) + px
    spread = cut(slope_of(parts[1]))
    parts = along(2)
    second = cut(own(*parts)) + py
    spread = spread + cut(slope_of(parts[2]))
    parts = along(3)
    third = cut(own(*parts)) + pz
    spread = spread + cut(weighted(parts[3], push_z))
    parts = along(0)
    density = cut(own(*parts)) + spread
    return density, first, second, third, pressure + spread


def slots_kernel(slots, own_row_ref, own_col_ref, lag_ref, source_ref, target_ref, chosen_ref):
    rows, patches = source_ref.shape
    per = slots * BLOCK_ROWS
    at_r = lax.broadcasted_iota(jnp.int32, (patches, patches), 0)
    at_c = lax.broadcasted_iota(jnp.int32, (patches, patches), 1)
    earlier = (at_r // BLOCK_ROWS < at_c // BLOCK_ROWS) & (at_r % BLOCK_ROWS == 0)
    hit = (own_row_ref[...] == own_col_ref[...]) & earlier
    rank = jnp.sum(jnp.where(hit, 1.0, 0.0), axis=0, keepdims=True).astype(jnp.int32)
    place = lax.broadcasted_iota(jnp.int32, (1, patches), 1) % BLOCK_ROWS
    at = own_row_ref[...] * (2 * per) + rank * BLOCK_ROWS + place
    row = lax.broadcasted_iota(jnp.int32, (rows, patches), 0)
    source_ref[...] = jnp.where(row == at, 1.0, 0.0).astype(jnp.bfloat16)
    target_ref[...] = jnp.where(row == at + per, 1.0, 0.0).astype(jnp.bfloat16)
    tall, wide = chosen_ref.shape
    bricks, deep = lag_ref.shape
    along = lax.broadcasted_iota(jnp.int32, (deep, wide), 0)
    cells = lax.broadcasted_iota(jnp.int32, (deep, wide), 1)
    spread = jnp.where(along == cells // PATCH, 1.0, 0.0).astype(jnp.bfloat16)
    lanes = jnp.dot(
        lag_ref[...].astype(jnp.bfloat16), spread, preferred_element_type=jnp.float32
    )
    line = lax.broadcasted_iota(jnp.int32, (tall, bricks), 0)
    brick = lax.broadcasted_iota(jnp.int32, (tall, bricks), 1)
    lift = jnp.where(line // PATCH == brick, 1.0, 0.0).astype(jnp.bfloat16)
    chosen_ref[...] = jnp.dot(
        lift, lanes.astype(jnp.bfloat16), preferred_element_type=jnp.float32
    )


def window_kernel(
    shape,
    per,
    edge_ref,
    f_ref,
    xlo_ref,
    xhi_ref,
    ylo_ref,
    yhi_ref,
    chosen_ref,
    source_pick_ref,
    target_pick_ref,
    w_ref,
    new_ref,
    keep_ref,
    give_ref,
    send_ref,
    first_ref,
    second_ref,
    shuffle_ref,
    natural_ref,
    both_ref,
):
    wide_x, wide_y, wide_z = shape
    patches = (wide_x // PATCH) * (wide_y // PATCH) * (wide_z // PATCH)
    top_x, top_y = REACH + wide_x, LIFT + wide_y
    full_x, full_y = top_x + REACH, top_y + LIFT
    lane = lax.broadcasted_iota(jnp.int32, (1, wide_z), 1)
    inside = {k: (lane + k >= 0) & (lane + k < wide_z) for k in OFFSETS}
    own_z = {k: jnp.where(inside[k], OWN_Z[k], 0.0) for k in OFFSETS}
    push_z = {k: jnp.where(inside[k], PUSH[k], 0.0) for k in OFFSETS}

    first_ref[:, REACH:top_x, LIFT:top_y, :] = f_ref[...]
    first_ref[:, 0:REACH, LIFT:top_y, :] = xlo_ref[...].astype(jnp.float32)
    first_ref[:, top_x:full_x, LIFT:top_y, :] = xhi_ref[...].astype(jnp.float32)
    first_ref[:, :, 0:LIFT, :] = ylo_ref[...].astype(jnp.float32)
    first_ref[:, :, top_y:full_y, :] = yhi_ref[...].astype(jnp.float32)

    def clear(ref, least):
        @pl.when(edge_ref[0] == 1)
        def _():
            ref[:, least:REACH] = jnp.zeros((FIELDS, REACH - least, full_y, wide_z), jnp.float32)

        @pl.when(edge_ref[1] == 1)
        def _():
            ref[:, top_x : full_x - least] = jnp.zeros(
                (FIELDS, REACH - least, full_y, wide_z), jnp.float32
            )

        @pl.when(edge_ref[2] == 1)
        def _():
            ref[:, :, 0:LIFT] = jnp.zeros((FIELDS, full_x, LIFT, wide_z), jnp.float32)

        @pl.when(edge_ref[3] == 1)
        def _():
            ref[:, :, top_y:full_y] = jnp.zeros((FIELDS, full_x, LIFT, wide_z), jnp.float32)

    def step(src, dst, least):
        def body(row, carry):
            done = one_row(src, row, own_z, push_z, None)
            for field in range(FIELDS):
                dst[field, row] = done[field]
            return carry

        lax.fori_loop(least, full_x - least, body, 0, unroll=2)
        clear(dst, least)

    def last_step(src):
        def body(row, carry):
            done = one_row(src, row, own_z, push_z, (LIFT, top_y))
            for field in range(FIELDS):
                new_ref[field, row - REACH] = done[field]
            return carry

        lax.fori_loop(REACH, top_x, body, 0, unroll=2)

    z_count = wide_z // PATCH
    lane_r = lax.broadcasted_iota(jnp.int32, (wide_z, wide_z), 0)
    lane_c = lax.broadcasted_iota(jnp.int32, (wide_z, wide_z), 1)
    swap = jnp.where(
        (lane_r // PATCH == lane_c % z_count) & (lane_r % PATCH == lane_c // z_count), 1.0, 0.0
    ).astype(jnp.bfloat16)
    group = lax.broadcasted_iota(jnp.int32, (PATCH, wide_z), 1) // z_count

    def into_patches(load, store):
        for field in range(FIELDS):
            flat = load(field).reshape(wide_x * wide_y, wide_z)
            shuffle_ref[field] = jnp.dot(
                flat.astype(jnp.bfloat16), swap, preferred_element_type=jnp.float32
            ).reshape(wide_x, wide_y, wide_z)

        for field in range(FIELDS):
            tiles = [
                shuffle_ref[
                    field, px * PATCH : (px + 1) * PATCH, py * PATCH : (py + 1) * PATCH
                ]
                for px in range(wide_x // PATCH)
                for py in range(wide_y // PATCH)
            ]
            for bit in (4, 2, 1):
                low = ((group & bit) == 0)[None]
                fresh = list(tiles)
                for i in range(PATCH):
                    if i & bit:
                        continue
                    a, b = tiles[i], tiles[i | bit]
                    fresh[i] = jnp.where(low, a, pltpu.roll(b, bit * z_count, 2))
                    fresh[i | bit] = jnp.where(
                        low, pltpu.roll(a, wide_z - bit * z_count, 2), b
                    )
                tiles = fresh
            for inner_z in range(PATCH):
                natural_ref[
                    field * PATCH : (field + 1) * PATCH, pl.ds(inner_z, PATCH, stride=PATCH), :
                ] = tiles[inner_z]

        for field in range(FIELDS):
            block = natural_ref[field * PATCH : (field + 1) * PATCH]
            block = block.reshape(PATCH**3, patches).astype(jnp.bfloat16)
            store(field * PATCH**3, block)

    def keep_picked(at, block):
        both_ref[at : at + PATCH**3, 0:patches] = block

    def keep_target(at, block):
        both_ref[at : at + PATCH**3, patches : 2 * patches] = block

    def chosen(field):
        one = second_ref[field, REACH:top_x, LIFT:top_y]
        two = first_ref[field, REACH:top_x, LIFT:top_y]
        one = one.reshape(wide_x // PATCH, PATCH, wide_y, wide_z)
        two = two.reshape(wide_x // PATCH, PATCH, wide_y, wide_z)
        later = chosen_ref[...].reshape(wide_x // PATCH, 1, wide_y, wide_z)
        return jnp.where(later == 1.0, two, one)

    step(first_ref, second_ref, 2)
    step(second_ref, first_ref, 4)
    last_step(first_ref)
    into_patches(chosen, keep_picked)
    into_patches(lambda field: new_ref[field], keep_target)

    embedded = lax.dot_general(
        both_ref[...], w_ref[...], (((0,), (0,)), ((), ())), preferred_element_type=jnp.float32
    ).astype(jnp.bfloat16)
    half = both_ref.shape[0] // 2
    mine = pl.multiple_of(edge_ref[4] * half, half)
    keep_ref[...] = both_ref[pl.ds(mine, half), 0:patches]
    give_ref[...] = both_ref[pl.ds(half - mine, half), 0:patches]
    rows = send_ref.shape[0]
    filled = jnp.sum(target_pick_ref[...].astype(jnp.float32), axis=1, keepdims=True)
    target_half = (lax.broadcasted_iota(jnp.int32, (rows, 1), 0) // per) % 2 == 1
    marker = jnp.where(target_half & (filled == 0.0), EMPTY, 0.0)
    placed = jnp.dot(
        source_pick_ref[...], embedded[0:patches], preferred_element_type=jnp.float32
    )
    placed = placed + jnp.dot(
        target_pick_ref[...],
        embedded[patches : 2 * patches],
        preferred_element_type=jnp.float32,
    )
    send_ref[...] = (placed + marker).astype(jnp.bfloat16)


def trainer_kernel(
    per,
    got_ref,
    w_in_ref,
    b_in_ref,
    w_out_ref,
    b_out_ref,
    source_ref,
    hidden_ref,
    error_ref,
    pre_grad_ref,
    b_in_grad_ref,
    b_out_grad_ref,
    back_ref,
    target_ref,
    slope_ref,
):
    rows = source_ref.shape[0]
    width = back_ref.shape[1]
    small, large = 32 * per, 64 * per
    line = lax.broadcasted_iota(jnp.int32, (small, large), 0)
    taken = lax.broadcasted_iota(jnp.int32, (small, large), 1)
    first = line // per * (2 * per) + line % per
    source_pick = jnp.where(taken == first, 1.0, 0.0).astype(jnp.bfloat16)
    target_pick = jnp.where(taken == first + per, 1.0, 0.0).astype(jnp.bfloat16)
    for at in range(rows // small):
        block = got_ref[at * large : (at + 1) * large]
        lines = slice(at * small, (at + 1) * small)
        source_ref[lines] = jnp.dot(
            source_pick, block, preferred_element_type=jnp.float32
        ).astype(jnp.bfloat16)
        target_ref[lines] = jnp.dot(target_pick, block, preferred_element_type=jnp.float32)

    chunk = 512
    hidden_size = hidden_ref.shape[1]
    source = source_ref[...]
    predict = jnp.broadcast_to(b_out_ref[...], target_ref.shape)
    for start in range(0, hidden_size, chunk):
        lanes = slice(start, start + chunk)
        pre = jnp.dot(source, w_in_ref[:, lanes], preferred_element_type=jnp.float32)
        pre = pre + b_in_ref[:, lanes]
        sigma = jax.nn.sigmoid(pre)
        hidden = (pre * sigma).astype(jnp.bfloat16)
        hidden_ref[:, lanes] = hidden
        slope_ref[:, lanes] = sigma * (1.0 + pre * (1.0 - sigma))
        predict = predict + jnp.dot(
            hidden, w_out_ref[lanes], preferred_element_type=jnp.float32
        )
    wanted = target_ref[...]
    error = jnp.where(wanted < FULL_BELOW, error_weight * (predict - wanted), 0.0)
    error = error.astype(jnp.bfloat16)
    error_ref[...] = error
    b_out_grad_ref[...] = jnp.sum(error.astype(jnp.float32), axis=0, keepdims=True)
    total = jnp.zeros(target_ref.shape, jnp.float32)
    for start in range(0, hidden_size, chunk):
        lanes = slice(start, start + chunk)
        upstream = contract_cols(error, w_out_ref[lanes])
        pre_grad = (upstream * slope_ref[:, lanes]).astype(jnp.bfloat16)
        pre_grad_ref[:, lanes] = pre_grad
        b_in_grad_ref[:, lanes] = jnp.sum(
            pre_grad.astype(jnp.float32), axis=0, keepdims=True
        )
        total = total + contract_cols(pre_grad, w_in_ref[:, lanes])
    gradient = total.astype(jnp.bfloat16)
    out = lax.broadcasted_iota(jnp.int32, (large, small), 0)
    origin = lax.broadcasted_iota(jnp.int32, (large, small), 1)
    fits = origin == out // (2 * per) * per + out % per
    side = out // per % 2
    for at in range(rows // small):
        lines = slice(at * small, (at + 1) * small)
        block = jnp.zeros((large, width), jnp.float32)
        for half in range(2):
            move = jnp.where(fits & (side == half), 1.0, 0.0).astype(jnp.bfloat16)
            block = block + jnp.dot(
                move,
                gradient[lines, half * width : (half + 1) * width],
                preferred_element_type=jnp.float32,
            )
        back_ref[at * large : (at + 1) * large] = block.astype(jnp.bfloat16)


def gather_kernel(source_pick_ref, target_pick_ref, back_ref, out_ref):
    width = back_ref.shape[1]
    for half, pick_ref in enumerate((source_pick_ref, target_pick_ref)):
        out_ref[:, half * width : (half + 1) * width] = contract_rows(
            pick_ref[...], back_ref[...]
        ).astype(jnp.bfloat16)


def part_kernel(keep_ref, got_ref, own_grad_ref, other_grad_ref, part_ref):
    half = keep_ref.shape[0]
    width = part_ref.shape[1]
    total = jnp.dot(keep_ref[...], own_grad_ref[...], preferred_element_type=jnp.float32)
    total = total + jnp.dot(
        got_ref[...], other_grad_ref[...], preferred_element_type=jnp.float32
    )
    for side in range(EMBED // width):
        part_ref[side * half : (side + 1) * half, :] = total[
            :, side * width : (side + 1) * width
        ].astype(jnp.bfloat16)


def sum_kernel(parts_ref, copies_ref):
    total = jnp.sum(parts_ref[...].astype(jnp.float32), axis=0).astype(jnp.bfloat16)
    copies_ref[...] = jnp.broadcast_to(total[None], copies_ref.shape)


def spread_kernel(core_ref, own_ref, other_ref, out_ref):
    half, width = out_ref.shape[0] // 2, own_ref.shape[1]
    mine = pl.multiple_of(core_ref[0] * half, half)
    for side in range(EMBED // width):
        lanes = slice(side * width, (side + 1) * width)
        rows = slice(side * half, (side + 1) * half)
        out_ref[pl.ds(mine, half), lanes] = own_ref[rows].astype(jnp.float32)
        out_ref[pl.ds(half - mine, half), lanes] = other_ref[rows].astype(jnp.float32)


def neighbours(low_piece, high_piece, axis):
    count = lax.axis_size(axis)
    up = [(i, i + 1) for i in range(count - 1)]
    down = [(b, a) for a, b in up]
    return lax.ppermute(high_piece, axis, up), lax.ppermute(low_piece, axis, down)


def contract_rows(left, right):
    return lax.dot_general(
        left, right, (((0,), (0,)), ((), ())), preferred_element_type=jnp.float32
    )


def contract_cols(left, right):
    return lax.dot_general(
        left, right, (((1,), (1,)), ((), ())), preferred_element_type=jnp.float32
    )


def per_device(fields, patch_weight, trainer_of, lag_index, w_in, b_in, w_out, b_out):
    axes = ("gx", "gy")
    n_x, n_y = lax.axis_size("gx"), lax.axis_size("gy")
    devices = n_x * n_y
    _, wide_x, wide_y, wide_z = fields.shape
    patches = (wide_x // PATCH) * (wide_y // PATCH) * (wide_z // PATCH)
    blocks = patches // BLOCK_ROWS
    slots = max(2, 2 * blocks // devices)
    per = slots * BLOCK_ROWS
    features = FIELDS * PATCH**3

    def narrow(piece):
        return piece.astype(jnp.bfloat16)

    xlo, xhi = neighbours(narrow(fields[:, :REACH]), narrow(fields[:, wide_x - REACH :]), "gx")
    y_first = jnp.concatenate(
        [xlo[:, :, :LIFT], narrow(fields[:, :, :LIFT]), xhi[:, :, :LIFT]], axis=1
    )
    at = wide_y - LIFT
    y_last = jnp.concatenate(
        [xlo[:, :, at:], narrow(fields[:, :, at:]), xhi[:, :, at:]], axis=1
    )
    ylo, yhi = neighbours(y_first, y_last, "gy")

    at_x, at_y = lax.axis_index("gx"), lax.axis_index("gy")
    core = at_x % 2
    edges = jnp.stack(
        [at_x == 0, at_x == n_x - 1, at_y == 0, at_y == n_y - 1, core == 1]
    ).astype(jnp.int32)
    own_patch = jnp.repeat(trainer_of[:, 0], BLOCK_ROWS)
    lag = lag_index.reshape(-1, lag_index.shape[2]).astype(jnp.float32)

    vmem = pl.BlockSpec(memory_space=pltpu.VMEM)
    smem = pl.BlockSpec(memory_space=pltpu.SMEM)

    def grant(mebibytes):
        return pltpu.CompilerParams(vmem_limit_bytes=mebibytes * 1024 * 1024)

    def shape(dims, kind):
        return jax.ShapeDtypeStruct(dims, kind)

    send_rows = 2 * devices * per
    source_pick, target_pick, chosen = pl.pallas_call(
        functools.partial(slots_kernel, slots),
        out_shape=(
            shape((send_rows, patches), jnp.bfloat16),
            shape((send_rows, patches), jnp.bfloat16),
            shape(((wide_x // PATCH) * wide_y, wide_z), jnp.float32),
        ),
        in_specs=[vmem] * 3,
        out_specs=(vmem,) * 3,
        compiler_params=grant(8),
        name="slots",
    )(own_patch[None, :], own_patch[:, None], lag)

    full = (FIELDS, wide_x + 2 * REACH, wide_y + 2 * LIFT, wide_z)
    new_fields, keep, give, send = pl.pallas_call(
        functools.partial(window_kernel, (wide_x, wide_y, wide_z), per),
        out_shape=(
            shape(fields.shape, jnp.float32),
            shape((features // 2, patches), jnp.bfloat16),
            shape((features // 2, patches), jnp.bfloat16),
            shape((send_rows, EMBED), jnp.bfloat16),
        ),
        in_specs=[smem] + [vmem] * 9,
        out_specs=(vmem,) * 4,
        scratch_shapes=[
            pltpu.VMEM(full, jnp.float32),
            pltpu.VMEM(full, jnp.float32),
            pltpu.VMEM((FIELDS, wide_x, wide_y, wide_z), jnp.float32),
            pltpu.VMEM((FIELDS * PATCH, PATCH * PATCH, patches), jnp.float32),
            pltpu.VMEM((features, 2 * patches), jnp.bfloat16),
        ],
        compiler_params=grant(32),
        name="window",
    )(
        edges, fields, xlo, xhi, ylo, yhi, chosen, source_pick, target_pick, patch_weight
    )

    pairs = [(i, i ^ 1) for i in range(n_x)]
    groups = [
        [x * n_y + y for x in range(n_x) for y in range(n_y) if x % 2 == c] for c in range(2)
    ]
    members = devices // 2
    got_picked = lax.ppermute(give, "gx", pairs)
    got = lax.all_to_all(send.reshape(devices, 2 * per, EMBED), axes, 0, 0, tiled=True)
    rows = devices * per
    hidden_size = w_in.shape[2]
    width = EMBED // 2
    source, hidden, error, pre_grad, b_in_grad, b_out_grad, back = pl.pallas_call(
        functools.partial(trainer_kernel, per),
        out_shape=(
            shape((rows, EMBED), jnp.bfloat16),
            shape((rows, hidden_size), jnp.bfloat16),
            shape((rows, EMBED), jnp.bfloat16),
            shape((rows, hidden_size), jnp.bfloat16),
            shape((1, hidden_size), jnp.float32),
            shape((1, EMBED), jnp.float32),
            shape((2 * rows, width), jnp.bfloat16),
        ),
        in_specs=[vmem] * 5,
        out_specs=(vmem,) * 7,
        scratch_shapes=[
            pltpu.VMEM((rows, EMBED), jnp.float32),
            pltpu.VMEM((rows, hidden_size), jnp.float32),
        ],
        compiler_params=grant(32),
        name="trainer",
    )(got.reshape(send_rows, EMBED), w_in[0], b_in, w_out[0], b_out)
    back = lax.all_to_all(back.reshape(devices, 2 * per, width), axes, 0, 0, tiled=True)
    w_in_grad = contract_rows(source, pre_grad)
    w_out_grad = contract_rows(hidden, error)
    back, w_in_grad, w_out_grad = lax.optimization_barrier((back, w_in_grad, w_out_grad))
    own_grad = pl.pallas_call(
        gather_kernel,
        out_shape=shape((patches, EMBED), jnp.bfloat16),
        in_specs=[vmem] * 3,
        out_specs=vmem,
        compiler_params=grant(8),
        name="gather",
    )(source_pick, target_pick, back.reshape(send_rows, width))
    other_grad = lax.ppermute(own_grad, "gx", pairs)
    piece = features // members
    parts = pl.pallas_call(
        part_kernel,
        out_shape=jax.ShapeDtypeStruct((features, width), jnp.bfloat16),
        in_specs=[vmem] * 4,
        out_specs=vmem,
        compiler_params=grant(16),
        name="part",
    )(keep, got_picked, own_grad, other_grad)
    parts = lax.all_to_all(
        parts.reshape(members, piece, width), axes, 0, 0, axis_index_groups=groups, tiled=True
    )
    copies = pl.pallas_call(
        sum_kernel,
        out_shape=jax.ShapeDtypeStruct((members, piece, width), jnp.bfloat16),
        in_specs=[vmem],
        out_specs=vmem,
        compiler_params=grant(16),
        name="total",
    )(parts)
    own_half = lax.all_to_all(copies, axes, 0, 0, axis_index_groups=groups, tiled=True)
    own_half = own_half.reshape(features, width)
    other_half = lax.ppermute(own_half, "gx", pairs)
    patch_gradient = pl.pallas_call(
        spread_kernel,
        out_shape=jax.ShapeDtypeStruct((features, EMBED), jnp.float32),
        in_specs=[smem, vmem, vmem],
        out_specs=vmem,
        compiler_params=grant(16),
        name="spread",
    )(edges[4:5], own_half, other_half)
    return (
        new_fields,
        patch_gradient,
        w_in_grad[None],
        b_in_grad,
        w_out_grad[None],
        b_out_grad,
    )


def solution(mesh):
    in_specs = (
        P(None, "gx", "gy", None),
        P(),
        P(("gx", "gy"), None),
        P("gx", "gy", None),
        P(("gx", "gy"), None, None),
        P(("gx", "gy"), None),
        P(("gx", "gy"), None, None),
        P(("gx", "gy"), None),
    )
    out_specs = (
        P(None, "gx", "gy", None),
        P(),
        P(("gx", "gy"), None, None),
        P(("gx", "gy"), None),
        P(("gx", "gy"), None, None),
        P(("gx", "gy"), None),
    )
    return jax.shard_map(
        per_device, mesh=mesh, in_specs=in_specs, out_specs=out_specs, check_vma=False
    )
```

```python
import functools

import jax
import jax.numpy as jnp
from jax import lax
from jax.experimental import pallas as pl
from jax.experimental.pallas import tpu as pltpu
from jax.sharding import PartitionSpec as P

FIELDS = 5
PATCH = 8
STEPS = 3
EMBED = 512
BLOCK_ROWS = 2
REACH = 2 * STEPS
LIFT = 8
EMPTY = 1.0e30
FULL_BELOW = 1.0e29

time_step = 0.2
viscosity = 0.5
drift_x = 0.6
drift_y = -0.4
drift_z = 0.3
error_weight = 0.0625

SLOPE = {-2: 1.0 / 12.0, -1: -8.0 / 12.0, 1: 8.0 / 12.0, 2: -1.0 / 12.0}
BEND = {-2: -1.0 / 12.0, -1: 16.0 / 12.0, 1: 16.0 / 12.0, 2: -1.0 / 12.0}
OFFSETS = (-2, -1, 1, 2)


def own_weights(drift):
    return {k: time_step * (viscosity * BEND[k] - drift * SLOPE[k]) for k in OFFSETS}


OWN_X, OWN_Y, OWN_Z = own_weights(drift_x), own_weights(drift_y), own_weights(drift_z)
MIDDLE = 1.0 - time_step * viscosity * 3.0 * 30.0 / 12.0
PUSH = {k: -time_step * SLOPE[k] for k in OFFSETS}


def rolled(value, offset, axis):
    size = value.shape[axis]
    return pltpu.roll(value, (-offset) % size, axis)


def weighted(pieces, weights):
    total = None
    for k in OFFSETS:
        term = pieces[k] * weights[k]
        total = term if total is None else total + term
    return total


def slope_of(pieces):
    return (pieces[-1] - pieces[1]) * PUSH[-1] + (pieces[2] - pieces[-2]) * PUSH[2]


def one_row(src, row, own_z, push_z, window):
    def along(field):
        middle = src[field, row]
        xs = {k: src[field, row + k] for k in OFFSETS}
        ys = {k: rolled(middle, k, 0) for k in OFFSETS}
        zs = {k: rolled(middle, k, 1) for k in OFFSETS}
        return middle, xs, ys, zs

    def own(middle, xs, ys, zs):
        return (
            middle * MIDDLE + weighted(xs, OWN_X) + weighted(ys, OWN_Y) + weighted(zs, own_z)
        )

    cut = (lambda v: v) if window is None else (lambda v: v[window[0] : window[1]])
    parts = along(4)
    pressure = cut(own(*parts))
    px, py, pz = cut(slope_of(parts[1])), cut(slope_of(parts[2])), cut(weighted(parts[3], push_z))
    parts = along(1)
    first = cut(own(*parts)) + px
    spread = cut(slope_of(parts[1]))
    parts = along(2)
    second = cut(own(*parts)) + py
    spread = spread + cut(slope_of(parts[2]))
    parts = along(3)
    third = cut(own(*parts)) + pz
    spread = spread + cut(weighted(parts[3], push_z))
    parts = along(0)
    density = cut(own(*parts)) + spread
    return density, first, second, third, pressure + spread


def slots_kernel(slots, own_row_ref, own_col_ref, lag_ref, source_ref, target_ref, chosen_ref):
    rows, patches = source_ref.shape
    per = slots * BLOCK_ROWS
    at_r = lax.broadcasted_iota(jnp.int32, (patches, patches), 0)
    at_c = lax.broadcasted_iota(jnp.int32, (patches, patches), 1)
    earlier = (at_r // BLOCK_ROWS < at_c // BLOCK_ROWS) & (at_r % BLOCK_ROWS == 0)
    hit = (own_row_ref[...] == own_col_ref[...]) & earlier
    rank = jnp.sum(jnp.where(hit, 1.0, 0.0), axis=0, keepdims=True).astype(jnp.int32)
    place = lax.broadcasted_iota(jnp.int32, (1, patches), 1) % BLOCK_ROWS
    at = own_row_ref[...] * (2 * per) + rank * BLOCK_ROWS + place
    row = lax.broadcasted_iota(jnp.int32, (rows, patches), 0)
    source_ref[...] = jnp.where(row == at, 1.0, 0.0).astype(jnp.bfloat16)
    target_ref[...] = jnp.where(row == at + per, 1.0, 0.0).astype(jnp.bfloat16)
    tall, wide = chosen_ref.shape
    bricks, deep = lag_ref.shape
    along = lax.broadcasted_iota(jnp.int32, (deep, wide), 0)
    cells = lax.broadcasted_iota(jnp.int32, (deep, wide), 1)
    spread = jnp.where(along == cells // PATCH, 1.0, 0.0).astype(jnp.bfloat16)
    lanes = jnp.dot(
        lag_ref[...].astype(jnp.bfloat16), spread, preferred_element_type=jnp.float32
    )
    line = lax.broadcasted_iota(jnp.int32, (tall, bricks), 0)
    brick = lax.broadcasted_iota(jnp.int32, (tall, bricks), 1)
    lift = jnp.where(line // PATCH == brick, 1.0, 0.0).astype(jnp.bfloat16)
    chosen_ref[...] = jnp.dot(
        lift, lanes.astype(jnp.bfloat16), preferred_element_type=jnp.float32
    )


def strip_layers(wide_x):
    layers, place = [], 0
    for layer in range(REACH):
        beside = REACH - LIFT // 4 if layer < 4 else 0
        rows = wide_x + 2 * beside
        layers.append((layer, beside, rows, place))
        place += rows
    return layers, place


def strips_kernel(f_ref, xlo_ref, xhi_ref, first_ref, last_ref, lines_ref):
    wide_x, wide_y = f_ref.shape[1], f_ref.shape[2]
    layers, _ = strip_layers(wide_x)
    beside = layers[0][1]
    for at, out_ref in ((0, first_ref), (wide_y - LIFT, last_ref)):
        tile = slice(at, at + LIFT)
        for row in range(wide_x + 2 * beside):
            place = slice(row * LIFT, (row + 1) * LIFT)
            if row < beside:
                piece = xlo_ref[:, REACH - beside + row, tile].astype(jnp.float32)
            elif row < beside + wide_x:
                piece = f_ref[:, row - beside, tile]
            else:
                piece = xhi_ref[:, row - beside - wide_x, tile].astype(jnp.float32)
            lines_ref[:, place] = piece
        for field in range(FIELDS):
            for layer, near, rows, place in layers:
                line = layer if at == 0 else LIFT - 1 - layer
                start = (beside - near) * LIFT + line
                out_ref[field, place : place + rows] = lines_ref[
                    field, pl.ds(start, rows, stride=LIFT), :
                ].astype(jnp.bfloat16)


def window_kernel(
    shape,
    per,
    edge_ref,
    f_ref,
    xlo_ref,
    xhi_ref,
    ylo_ref,
    yhi_ref,
    chosen_ref,
    source_pick_ref,
    target_pick_ref,
    w_hbm,
    new_hbm,
    keep_hbm,
    give_hbm,
    send_hbm,
    first_ref,
    second_ref,
    shuffle_ref,
    natural_ref,
    both_ref,
    w_ref,
    new_ref,
    send_ref,
    done,
):
    load_w = pltpu.make_async_copy(w_hbm, w_ref, done.at[0])
    load_w.start()
    wide_x, wide_y, wide_z = shape
    patches = (wide_x // PATCH) * (wide_y // PATCH) * (wide_z // PATCH)
    top_x, top_y = REACH + wide_x, LIFT + wide_y
    full_x, full_y = top_x + REACH, top_y + LIFT
    lane = lax.broadcasted_iota(jnp.int32, (1, wide_z), 1)
    inside = {k: (lane + k >= 0) & (lane + k < wide_z) for k in OFFSETS}
    own_z = {k: jnp.where(inside[k], OWN_Z[k], 0.0) for k in OFFSETS}
    push_z = {k: jnp.where(inside[k], PUSH[k], 0.0) for k in OFFSETS}

    first_ref[:, REACH:top_x, LIFT:top_y, :] = f_ref[...]
    first_ref[:, 0:REACH, LIFT:top_y, :] = xlo_ref[...].astype(jnp.float32)
    first_ref[:, top_x:full_x, LIFT:top_y, :] = xhi_ref[...].astype(jnp.float32)
    for field in range(FIELDS):
        for layer, beside, lines, place in strip_layers(wide_x)[0]:
            rows = slice(REACH - beside, REACH - beside + lines)
            packed = slice(place, place + lines)
            first_ref[field, rows, LIFT - 1 - layer, :] = ylo_ref[field, packed].astype(
                jnp.float32
            )
            first_ref[field, rows, top_y + layer, :] = yhi_ref[field, packed].astype(
                jnp.float32
            )

    def clear(ref, least):
        @pl.when(edge_ref[0] == 1)
        def _():
            ref[:, least:REACH] = jnp.zeros((FIELDS, REACH - least, full_y, wide_z), jnp.float32)

        @pl.when(edge_ref[1] == 1)
        def _():
            ref[:, top_x : full_x - least] = jnp.zeros(
                (FIELDS, REACH - least, full_y, wide_z), jnp.float32
            )

        @pl.when(edge_ref[2] == 1)
        def _():
            ref[:, :, 0:LIFT] = jnp.zeros((FIELDS, full_x, LIFT, wide_z), jnp.float32)

        @pl.when(edge_ref[3] == 1)
        def _():
            ref[:, :, top_y:full_y] = jnp.zeros((FIELDS, full_x, LIFT, wide_z), jnp.float32)

    def step(src, dst, least):
        def body(row, carry):
            done = one_row(src, row, own_z, push_z, None)
            for field in range(FIELDS):
                dst[field, row] = done[field]
            return carry

        lax.fori_loop(least, full_x - least, body, 0, unroll=2)
        clear(dst, least)

    def last_step(src):
        def body(row, carry):
            done = one_row(src, row, own_z, push_z, (LIFT, top_y))
            for field in range(FIELDS):
                new_ref[field, row - REACH] = done[field]
            return carry

        lax.fori_loop(REACH, top_x, body, 0, unroll=2)

    z_count = wide_z // PATCH
    lane_r = lax.broadcasted_iota(jnp.int32, (wide_z, wide_z), 0)
    lane_c = lax.broadcasted_iota(jnp.int32, (wide_z, wide_z), 1)
    swap = jnp.where(
        (lane_r // PATCH == lane_c % z_count) & (lane_r % PATCH == lane_c // z_count), 1.0, 0.0
    ).astype(jnp.bfloat16)
    group = lax.broadcasted_iota(jnp.int32, (PATCH, wide_z), 1) // z_count

    def into_patches(load, store):
        for field in range(FIELDS):
            flat = load(field).reshape(wide_x * wide_y, wide_z)
            shuffle_ref[field] = jnp.dot(
                flat.astype(jnp.bfloat16), swap, preferred_element_type=jnp.float32
            ).reshape(wide_x, wide_y, wide_z)

        for field in range(FIELDS):
            tiles = [
                shuffle_ref[
                    field, px * PATCH : (px + 1) * PATCH, py * PATCH : (py + 1) * PATCH
                ]
                for px in range(wide_x // PATCH)
                for py in range(wide_y // PATCH)
            ]
            for bit in (4, 2, 1):
                low = ((group & bit) == 0)[None]
                fresh = list(tiles)
                for i in range(PATCH):
                    if i & bit:
                        continue
                    a, b = tiles[i], tiles[i | bit]
                    fresh[i] = jnp.where(low, a, pltpu.roll(b, bit * z_count, 2))
                    fresh[i | bit] = jnp.where(
                        low, pltpu.roll(a, wide_z - bit * z_count, 2), b
                    )
                tiles = fresh
            for inner_z in range(PATCH):
                natural_ref[
                    field * PATCH : (field + 1) * PATCH, pl.ds(inner_z, PATCH, stride=PATCH), :
                ] = tiles[inner_z]

        for field in range(FIELDS):
            block = natural_ref[field * PATCH : (field + 1) * PATCH]
            block = block.reshape(PATCH**3, patches).astype(jnp.bfloat16)
            store(field * PATCH**3, block)

    def keep_picked(at, block):
        both_ref[at : at + PATCH**3, 0:patches] = block

    def keep_target(at, block):
        both_ref[at : at + PATCH**3, patches : 2 * patches] = block

    def chosen(field):
        one = second_ref[field, REACH:top_x, LIFT:top_y]
        two = first_ref[field, REACH:top_x, LIFT:top_y]
        one = one.reshape(wide_x // PATCH, PATCH, wide_y, wide_z)
        two = two.reshape(wide_x // PATCH, PATCH, wide_y, wide_z)
        later = chosen_ref[...].reshape(wide_x // PATCH, 1, wide_y, wide_z)
        return jnp.where(later == 1.0, two, one)

    step(first_ref, second_ref, 2)
    step(second_ref, first_ref, 4)
    last_step(first_ref)
    store_new = pltpu.make_async_copy(new_ref, new_hbm, done.at[1])
    store_new.start()
    into_patches(chosen, keep_picked)
    into_patches(lambda field: new_ref[field], keep_target)

    half = both_ref.shape[0] // 2
    mine = pl.multiple_of(edge_ref[4] * half, half)
    lanes = slice(0, patches)
    store_keep = pltpu.make_async_copy(both_ref.at[pl.ds(mine, half), lanes], keep_hbm, done.at[2])
    store_give = pltpu.make_async_copy(
        both_ref.at[pl.ds(half - mine, half), lanes], give_hbm, done.at[3]
    )
    store_give.start()
    store_keep.start()
    load_w.wait()
    embedded = contract_rows(both_ref[...], w_ref[...]).astype(jnp.bfloat16)
    rows = send_ref.shape[0]
    pieces = 4
    stores = []
    for piece in range(pieces):
        lines = slice(piece * rows // pieces, (piece + 1) * rows // pieces)
        wanted = target_pick_ref[lines]
        filled = jnp.sum(wanted.astype(jnp.float32), axis=1, keepdims=True)
        line = lax.broadcasted_iota(jnp.int32, (rows // pieces, 1), 0)
        marker = jnp.where((line // per % 2 == 1) & (filled == 0.0), EMPTY, 0.0)
        placed = jnp.dot(
            source_pick_ref[lines], embedded[0:patches], preferred_element_type=jnp.float32
        )
        placed = placed + jnp.dot(
            wanted, embedded[patches : 2 * patches], preferred_element_type=jnp.float32
        )
        send_ref[lines] = (placed + marker).astype(jnp.bfloat16)
        store = pltpu.make_async_copy(send_ref.at[lines], send_hbm.at[lines], done.at[4 + piece])
        store.start()
        stores.append(store)
    for store in [store_new, store_keep, store_give] + stores:
        store.wait()


def trainer_kernel(
    per,
    got_ref,
    w_in_hbm,
    b_in_ref,
    w_out_hbm,
    b_out_ref,
    source_hbm,
    hidden_hbm,
    error_hbm,
    pre_grad_hbm,
    b_in_grad_ref,
    b_out_grad_ref,
    back_hbm,
    target_ref,
    slope_ref,
    source_ref,
    hidden_ref,
    error_ref,
    pre_grad_ref,
    back_ref,
    w_in_ref,
    w_out_ref,
    loaded,
    stored,
):
    chunk = 512
    hidden_size = hidden_ref.shape[1]
    starts = range(0, hidden_size, chunk)
    loads = []
    for at, start in enumerate(starts):
        lanes = slice(start, start + chunk)
        pair = (
            pltpu.make_async_copy(w_in_hbm.at[:, lanes], w_in_ref.at[:, lanes], loaded.at[2 * at]),
            pltpu.make_async_copy(w_out_hbm.at[lanes], w_out_ref.at[lanes], loaded.at[2 * at + 1]),
        )
        for load in pair:
            load.start()
        loads.append(pair)
    stores = []

    def store(src, dst):
        copy = pltpu.make_async_copy(src, dst, stored.at[len(stores)])
        copy.start()
        stores.append(copy)

    rows = source_ref.shape[0]
    width = back_hbm.shape[1]
    small, large = 32 * per, 64 * per
    line = lax.broadcasted_iota(jnp.int32, (small, large), 0)
    taken = lax.broadcasted_iota(jnp.int32, (small, large), 1)
    first = line // per * (2 * per) + line % per
    source_pick = jnp.where(taken == first, 1.0, 0.0).astype(jnp.bfloat16)
    target_pick = jnp.where(taken == first + per, 1.0, 0.0).astype(jnp.bfloat16)
    for at in range(rows // small):
        block = got_ref[at * large : (at + 1) * large]
        lines = slice(at * small, (at + 1) * small)
        source_ref[lines] = jnp.dot(
            source_pick, block, preferred_element_type=jnp.float32
        ).astype(jnp.bfloat16)
        target_ref[lines] = jnp.dot(target_pick, block, preferred_element_type=jnp.float32)

    store(source_ref, source_hbm)
    source = source_ref[...]
    predict = jnp.broadcast_to(b_out_ref[...], target_ref.shape)
    for at, start in enumerate(starts):
        lanes = slice(start, start + chunk)
        for load in loads[at]:
            load.wait()
        pre = jnp.dot(source, w_in_ref[:, lanes], preferred_element_type=jnp.float32)
        pre = pre + b_in_ref[:, lanes]
        sigma = jax.nn.sigmoid(pre)
        hidden = (pre * sigma).astype(jnp.bfloat16)
        hidden_ref[:, lanes] = hidden
        store(hidden_ref.at[:, lanes], hidden_hbm.at[:, lanes])
        slope_ref[:, lanes] = sigma * (1.0 + pre * (1.0 - sigma))
        predict = predict + jnp.dot(
            hidden, w_out_ref[lanes], preferred_element_type=jnp.float32
        )
    wanted = target_ref[...]
    error = jnp.where(wanted < FULL_BELOW, error_weight * (predict - wanted), 0.0)
    error = error.astype(jnp.bfloat16)
    error_ref[...] = error
    store(error_ref, error_hbm)
    b_out_grad_ref[...] = jnp.sum(error.astype(jnp.float32), axis=0, keepdims=True)
    total = jnp.zeros(target_ref.shape, jnp.float32)
    for start in starts:
        lanes = slice(start, start + chunk)
        upstream = contract_cols(error, w_out_ref[lanes])
        pre_grad = (upstream * slope_ref[:, lanes]).astype(jnp.bfloat16)
        pre_grad_ref[:, lanes] = pre_grad
        store(pre_grad_ref.at[:, lanes], pre_grad_hbm.at[:, lanes])
        b_in_grad_ref[:, lanes] = jnp.sum(
            pre_grad.astype(jnp.float32), axis=0, keepdims=True
        )
        total = total + contract_cols(pre_grad, w_in_ref[:, lanes])
    gradient = total.astype(jnp.bfloat16)
    out = lax.broadcasted_iota(jnp.int32, (large, small), 0)
    origin = lax.broadcasted_iota(jnp.int32, (large, small), 1)
    fits = origin == out // (2 * per) * per + out % per
    side = out // per % 2
    for at in range(rows // small):
        lines = slice(at * small, (at + 1) * small)
        block = jnp.zeros((large, width), jnp.float32)
        for half in range(2):
            move = jnp.where(fits & (side == half), 1.0, 0.0).astype(jnp.bfloat16)
            block = block + jnp.dot(
                move,
                gradient[lines, half * width : (half + 1) * width],
                preferred_element_type=jnp.float32,
            )
        lines = slice(at * large, (at + 1) * large)
        back_ref[lines] = block.astype(jnp.bfloat16)
        store(back_ref.at[lines], back_hbm.at[lines])
    for copy in stores:
        copy.wait()


def gather_kernel(source_pick_ref, target_pick_ref, back_ref, out_ref):
    width = back_ref.shape[1]
    for half, pick_ref in enumerate((source_pick_ref, target_pick_ref)):
        out_ref[:, half * width : (half + 1) * width] = contract_rows(
            pick_ref[...], back_ref[...]
        ).astype(jnp.bfloat16)


def part_kernel(
    keep_hbm, got_hbm, own_grad_ref, other_grad_ref, part_ref, keep_ref, got_ref, loaded
):
    loads = (
        pltpu.make_async_copy(keep_hbm, keep_ref, loaded.at[0]),
        pltpu.make_async_copy(got_hbm, got_ref, loaded.at[1]),
    )
    for load in loads:
        load.start()
    half = keep_ref.shape[0]
    width = part_ref.shape[1]
    loads[0].wait()
    total = jnp.dot(keep_ref[...], own_grad_ref[...], preferred_element_type=jnp.float32)
    loads[1].wait()
    total = total + jnp.dot(
        got_ref[...], other_grad_ref[...], preferred_element_type=jnp.float32
    )
    for side in range(EMBED // width):
        part_ref[side * half : (side + 1) * half, :] = total[
            :, side * width : (side + 1) * width
        ].astype(jnp.bfloat16)


def sum_kernel(parts_ref, copies_ref):
    total = jnp.sum(parts_ref[...].astype(jnp.float32), axis=0).astype(jnp.bfloat16)
    copies_ref[...] = jnp.broadcast_to(total[None], copies_ref.shape)


def spread_kernel(other, edge_ref, half_ref, *rest):
    out_hbm, wide_ref, done = rest[-3:]
    half, width = wide_ref.shape[0], half_ref.shape[1]
    core = 1 - edge_ref[4] if other else edge_ref[4]
    begin = core * half
    pieces = 4
    stores = []
    for piece in range(pieces):
        lines = slice(piece * half // pieces, (piece + 1) * half // pieces)
        for side in range(EMBED // width):
            lanes = slice(side * width, (side + 1) * width)
            rows = slice(side * half + lines.start, side * half + lines.stop)
            wide_ref[lines, lanes] = half_ref[rows].astype(jnp.float32)
        at = pl.multiple_of(begin + lines.start, half // pieces)
        store = pltpu.make_async_copy(
            wide_ref.at[lines], out_hbm.at[pl.ds(at, half // pieces)], done.at[piece]
        )
        store.start()
        stores.append(store)
    for store in stores:
        store.wait()


def neighbours(low_piece, high_piece, axis):
    count = lax.axis_size(axis)
    up = [(i, i + 1) for i in range(count - 1)]
    down = [(b, a) for a, b in up]
    return lax.ppermute(high_piece, axis, up), lax.ppermute(low_piece, axis, down)


def contract_rows(left, right):
    return lax.dot_general(
        left, right, (((0,), (0,)), ((), ())), preferred_element_type=jnp.float32
    )


def contract_cols(left, right):
    return lax.dot_general(
        left, right, (((1,), (1,)), ((), ())), preferred_element_type=jnp.float32
    )


def per_device(fields, patch_weight, trainer_of, lag_index, w_in, b_in, w_out, b_out):
    axes = ("gx", "gy")
    n_x, n_y = lax.axis_size("gx"), lax.axis_size("gy")
    devices = n_x * n_y
    _, wide_x, wide_y, wide_z = fields.shape
    patches = (wide_x // PATCH) * (wide_y // PATCH) * (wide_z // PATCH)
    blocks = patches // BLOCK_ROWS
    slots = max(2, 2 * blocks // devices)
    per = slots * BLOCK_ROWS
    features = FIELDS * PATCH**3

    def narrow(piece):
        return piece.astype(jnp.bfloat16)

    xlo, xhi = neighbours(narrow(fields[:, :REACH]), narrow(fields[:, wide_x - REACH :]), "gx")
    at_x, at_y = lax.axis_index("gx"), lax.axis_index("gy")
    core = at_x % 2
    edges = jnp.stack(
        [at_x == 0, at_x == n_x - 1, at_y == 0, at_y == n_y - 1, core == 1]
    ).astype(jnp.int32)
    own_patch = jnp.repeat(trainer_of[:, 0], BLOCK_ROWS)
    lag = lag_index.reshape(-1, lag_index.shape[2]).astype(jnp.float32)

    vmem = pl.BlockSpec(memory_space=pltpu.VMEM)
    smem = pl.BlockSpec(memory_space=pltpu.SMEM)
    hbm = pl.BlockSpec(memory_space=pltpu.HBM)

    def grant(mebibytes):
        return pltpu.CompilerParams(vmem_limit_bytes=mebibytes * 1024 * 1024)

    def shape(dims, kind):
        return jax.ShapeDtypeStruct(dims, kind)

    layers, strip = strip_layers(wide_x)
    y_first, y_last = pl.pallas_call(
        strips_kernel,
        out_shape=(shape((FIELDS, strip, wide_z), jnp.bfloat16),) * 2,
        in_specs=[vmem] * 3,
        out_specs=(vmem,) * 2,
        scratch_shapes=[pltpu.VMEM((FIELDS, layers[0][2] * LIFT, wide_z), jnp.float32)],
        compiler_params=grant(8),
        name="strips",
    )(fields, xlo, xhi)
    ylo, yhi = neighbours(y_first, y_last, "gy")

    send_rows = 2 * devices * per
    source_pick, target_pick, chosen = pl.pallas_call(
        functools.partial(slots_kernel, slots),
        out_shape=(
            shape((send_rows, patches), jnp.bfloat16),
            shape((send_rows, patches), jnp.bfloat16),
            shape(((wide_x // PATCH) * wide_y, wide_z), jnp.float32),
        ),
        in_specs=[vmem] * 3,
        out_specs=(vmem,) * 3,
        compiler_params=grant(8),
        name="slots",
    )(own_patch[None, :], own_patch[:, None], lag)

    full = (FIELDS, wide_x + 2 * REACH, wide_y + 2 * LIFT, wide_z)
    new_fields, keep, give, send = pl.pallas_call(
        functools.partial(window_kernel, (wide_x, wide_y, wide_z), per),
        out_shape=(
            shape(fields.shape, jnp.float32),
            shape((features // 2, patches), jnp.bfloat16),
            shape((features // 2, patches), jnp.bfloat16),
            shape((send_rows, EMBED), jnp.bfloat16),
        ),
        in_specs=[smem] + [vmem] * 8 + [hbm],
        out_specs=(hbm,) * 4,
        scratch_shapes=[
            pltpu.VMEM(full, jnp.float32),
            pltpu.VMEM(full, jnp.float32),
            pltpu.VMEM((FIELDS, wide_x, wide_y, wide_z), jnp.float32),
            pltpu.VMEM((FIELDS * PATCH, PATCH * PATCH, patches), jnp.float32),
            pltpu.VMEM((features, 2 * patches), jnp.bfloat16),
            pltpu.VMEM((features, EMBED), jnp.bfloat16),
            pltpu.VMEM((FIELDS, wide_x, wide_y, wide_z), jnp.float32),
            pltpu.VMEM((send_rows, EMBED), jnp.bfloat16),
            pltpu.SemaphoreType.DMA((8,)),
        ],
        compiler_params=grant(32),
        name="window",
    )(
        edges, fields, xlo, xhi, ylo, yhi, chosen, source_pick, target_pick, patch_weight
    )

    pairs = [(i, i ^ 1) for i in range(n_x)]
    groups = [
        [x * n_y + y for x in range(n_x) for y in range(n_y) if x % 2 == c] for c in range(2)
    ]
    members = devices // 2
    got_picked = lax.ppermute(give, "gx", pairs)
    got = lax.all_to_all(send.reshape(devices, 2 * per, EMBED), axes, 0, 0, tiled=True)
    rows = devices * per
    hidden_size = w_in.shape[2]
    width = EMBED // 2
    source, hidden, error, pre_grad, b_in_grad, b_out_grad, back = pl.pallas_call(
        functools.partial(trainer_kernel, per),
        out_shape=(
            shape((rows, EMBED), jnp.bfloat16),
            shape((rows, hidden_size), jnp.bfloat16),
            shape((rows, EMBED), jnp.bfloat16),
            shape((rows, hidden_size), jnp.bfloat16),
            shape((1, hidden_size), jnp.float32),
            shape((1, EMBED), jnp.float32),
            shape((2 * rows, width), jnp.bfloat16),
        ),
        in_specs=[vmem, hbm, vmem, hbm, vmem],
        out_specs=(hbm, hbm, hbm, hbm, vmem, vmem, hbm),
        scratch_shapes=[
            pltpu.VMEM((rows, EMBED), jnp.float32),
            pltpu.VMEM((rows, hidden_size), jnp.float32),
            pltpu.VMEM((rows, EMBED), jnp.bfloat16),
            pltpu.VMEM((rows, hidden_size), jnp.bfloat16),
            pltpu.VMEM((rows, EMBED), jnp.bfloat16),
            pltpu.VMEM((rows, hidden_size), jnp.bfloat16),
            pltpu.VMEM((2 * rows, width), jnp.bfloat16),
            pltpu.VMEM((EMBED, hidden_size), jnp.bfloat16),
            pltpu.VMEM((hidden_size, EMBED), jnp.bfloat16),
            pltpu.SemaphoreType.DMA((8,)),
            pltpu.SemaphoreType.DMA((16,)),
        ],
        compiler_params=grant(32),
        name="trainer",
    )(got.reshape(send_rows, EMBED), w_in[0], b_in, w_out[0], b_out)
    back = lax.all_to_all(back.reshape(devices, 2 * per, width), axes, 0, 0, tiled=True)
    w_in_grad = contract_rows(source, pre_grad)
    w_out_grad = contract_rows(hidden, error)
    back, w_in_grad, w_out_grad = lax.optimization_barrier((back, w_in_grad, w_out_grad))
    own_grad = pl.pallas_call(
        gather_kernel,
        out_shape=shape((patches, EMBED), jnp.bfloat16),
        in_specs=[vmem] * 3,
        out_specs=vmem,
        compiler_params=grant(8),
        name="gather",
    )(source_pick, target_pick, back.reshape(send_rows, width))
    other_grad = lax.ppermute(own_grad, "gx", pairs)
    piece = features // members
    parts = pl.pallas_call(
        part_kernel,
        out_shape=shape((features, width), jnp.bfloat16),
        in_specs=[hbm, hbm, vmem, vmem],
        out_specs=vmem,
        scratch_shapes=[
            pltpu.VMEM((features // 2, patches), jnp.bfloat16),
            pltpu.VMEM((features // 2, patches), jnp.bfloat16),
            pltpu.SemaphoreType.DMA((2,)),
        ],
        compiler_params=grant(16),
        name="part",
    )(keep, got_picked, own_grad, other_grad)
    parts = lax.all_to_all(
        parts.reshape(members, piece, width), axes, 0, 0, axis_index_groups=groups, tiled=True
    )
    copies = pl.pallas_call(
        sum_kernel,
        out_shape=jax.ShapeDtypeStruct((members, piece, width), jnp.bfloat16),
        in_specs=[vmem],
        out_specs=vmem,
        compiler_params=grant(16),
        name="total",
    )(parts)
    own_half = lax.all_to_all(copies, axes, 0, 0, axis_index_groups=groups, tiled=True)
    own_half = own_half.reshape(features, width)
    other_half = lax.ppermute(own_half, "gx", pairs)

    def spread(other, *operands):
        return pl.pallas_call(
            functools.partial(spread_kernel, other),
            out_shape=shape((features, EMBED), jnp.float32),
            in_specs=[smem, vmem] + [hbm] * (len(operands) - 2),
            out_specs=hbm,
            scratch_shapes=[
                pltpu.VMEM((features // 2, EMBED), jnp.float32),
                pltpu.SemaphoreType.DMA((4,)),
            ],
            input_output_aliases={2: 0} if other else {},
            compiler_params=grant(8),
            name="spread_other" if other else "spread_own",
        )(*operands)

    patch_gradient = spread(False, edges, own_half)
    patch_gradient = spread(True, edges, other_half, patch_gradient)
    return (
        new_fields,
        patch_gradient,
        w_in_grad[None],
        b_in_grad,
        w_out_grad[None],
        b_out_grad,
    )


def solution(mesh):
    in_specs = (
        P(None, "gx", "gy", None),
        P(),
        P(("gx", "gy"), None),
        P("gx", "gy", None),
        P(("gx", "gy"), None, None),
        P(("gx", "gy"), None),
        P(("gx", "gy"), None, None),
        P(("gx", "gy"), None),
    )
    out_specs = (
        P(None, "gx", "gy", None),
        P(),
        P(("gx", "gy"), None, None),
        P(("gx", "gy"), None),
        P(("gx", "gy"), None, None),
        P(("gx", "gy"), None),
    )
    return jax.shard_map(
        per_device, mesh=mesh, in_specs=in_specs, out_specs=out_specs, check_vma=False
    )
```

```python
import functools

import jax
import jax.numpy as jnp
from jax import lax
from jax.experimental import pallas as pl
from jax.experimental.pallas import tpu as pltpu
from jax.sharding import PartitionSpec as P

FIELDS = 5
PATCH = 8
STEPS = 3
EMBED = 512
BLOCK_ROWS = 2
REACH = 2 * STEPS
LIFT = 8
EMPTY = 1.0e30
FULL_BELOW = 1.0e29

time_step = 0.2
viscosity = 0.5
drift_x = 0.6
drift_y = -0.4
drift_z = 0.3
error_weight = 0.0625

SLOPE = {-2: 1.0 / 12.0, -1: -8.0 / 12.0, 1: 8.0 / 12.0, 2: -1.0 / 12.0}
BEND = {-2: -1.0 / 12.0, -1: 16.0 / 12.0, 1: 16.0 / 12.0, 2: -1.0 / 12.0}
OFFSETS = (-2, -1, 1, 2)


def own_weights(drift):
    return {k: time_step * (viscosity * BEND[k] - drift * SLOPE[k]) for k in OFFSETS}


OWN_X, OWN_Y, OWN_Z = own_weights(drift_x), own_weights(drift_y), own_weights(drift_z)
MIDDLE = 1.0 - time_step * viscosity * 3.0 * 30.0 / 12.0
PUSH = {k: -time_step * SLOPE[k] for k in OFFSETS}


def rolled(value, offset, axis):
    size = value.shape[axis]
    return pltpu.roll(value, (-offset) % size, axis)


def weighted(pieces, weights):
    total = None
    for k in OFFSETS:
        term = pieces[k] * weights[k]
        total = term if total is None else total + term
    return total


def slope_of(pieces):
    return (pieces[-1] - pieces[1]) * PUSH[-1] + (pieces[2] - pieces[-2]) * PUSH[2]


def one_row(src, row, own_z, push_z, window):
    def along(field):
        middle = src[field, row]
        xs = {k: src[field, row + k] for k in OFFSETS}
        ys = {k: rolled(middle, k, 0) for k in OFFSETS}
        zs = {k: rolled(middle, k, 1) for k in OFFSETS}
        return middle, xs, ys, zs

    def own(middle, xs, ys, zs):
        return (
            middle * MIDDLE + weighted(xs, OWN_X) + weighted(ys, OWN_Y) + weighted(zs, own_z)
        )

    cut = (lambda v: v) if window is None else (lambda v: v[window[0] : window[1]])
    parts = along(4)
    pressure = cut(own(*parts))
    px, py, pz = cut(slope_of(parts[1])), cut(slope_of(parts[2])), cut(weighted(parts[3], push_z))
    parts = along(1)
    first = cut(own(*parts)) + px
    spread = cut(slope_of(parts[1]))
    parts = along(2)
    second = cut(own(*parts)) + py
    spread = spread + cut(slope_of(parts[2]))
    parts = along(3)
    third = cut(own(*parts)) + pz
    spread = spread + cut(weighted(parts[3], push_z))
    parts = along(0)
    density = cut(own(*parts)) + spread
    return density, first, second, third, pressure + spread


def slots_kernel(slots, own_row_ref, own_col_ref, lag_ref, source_ref, target_ref, chosen_ref):
    rows, patches = source_ref.shape
    per = slots * BLOCK_ROWS
    at_r = lax.broadcasted_iota(jnp.int32, (patches, patches), 0)
    at_c = lax.broadcasted_iota(jnp.int32, (patches, patches), 1)
    earlier = (at_r // BLOCK_ROWS < at_c // BLOCK_ROWS) & (at_r % BLOCK_ROWS == 0)
    hit = (own_row_ref[...] == own_col_ref[...]) & earlier
    rank = jnp.sum(jnp.where(hit, 1.0, 0.0), axis=0, keepdims=True).astype(jnp.int32)
    place = lax.broadcasted_iota(jnp.int32, (1, patches), 1) % BLOCK_ROWS
    at = own_row_ref[...] * (2 * per) + rank * BLOCK_ROWS + place
    row = lax.broadcasted_iota(jnp.int32, (rows, patches), 0)
    source_ref[...] = jnp.where(row == at, 1.0, 0.0).astype(jnp.bfloat16)
    target_ref[...] = jnp.where(row == at + per, 1.0, 0.0).astype(jnp.bfloat16)
    tall, wide = chosen_ref.shape
    bricks, deep = lag_ref.shape
    along = lax.broadcasted_iota(jnp.int32, (deep, wide), 0)
    cells = lax.broadcasted_iota(jnp.int32, (deep, wide), 1)
    spread = jnp.where(along == cells // PATCH, 1.0, 0.0).astype(jnp.bfloat16)
    lanes = jnp.dot(
        lag_ref[...].astype(jnp.bfloat16), spread, preferred_element_type=jnp.float32
    )
    line = lax.broadcasted_iota(jnp.int32, (tall, bricks), 0)
    brick = lax.broadcasted_iota(jnp.int32, (tall, bricks), 1)
    lift = jnp.where(line // PATCH == brick, 1.0, 0.0).astype(jnp.bfloat16)
    chosen_ref[...] = jnp.dot(
        lift, lanes.astype(jnp.bfloat16), preferred_element_type=jnp.float32
    )


def strip_layers(wide_x):
    layers, place = [], 0
    for layer in range(REACH):
        beside = REACH - LIFT // 4 if layer < 4 else 0
        rows = wide_x + 2 * beside
        layers.append((layer, beside, rows, place))
        place += rows
    return layers, place


def strips_kernel(f_ref, xlo_ref, xhi_ref, first_ref, last_ref, lines_ref):
    wide_x, wide_y = f_ref.shape[1], f_ref.shape[2]
    layers, _ = strip_layers(wide_x)
    beside = layers[0][1]
    for at, out_ref in ((0, first_ref), (wide_y - LIFT, last_ref)):
        tile = slice(at, at + LIFT)
        for row in range(wide_x + 2 * beside):
            place = slice(row * LIFT, (row + 1) * LIFT)
            if row < beside:
                piece = xlo_ref[:, REACH - beside + row, tile].astype(jnp.float32)
            elif row < beside + wide_x:
                piece = f_ref[:, row - beside, tile]
            else:
                piece = xhi_ref[:, row - beside - wide_x, tile].astype(jnp.float32)
            lines_ref[:, place] = piece
        for field in range(FIELDS):
            for layer, near, rows, place in layers:
                line = layer if at == 0 else LIFT - 1 - layer
                start = (beside - near) * LIFT + line
                out_ref[field, place : place + rows] = lines_ref[
                    field, pl.ds(start, rows, stride=LIFT), :
                ].astype(jnp.bfloat16)


def window_kernel(
    shape,
    per,
    edge_ref,
    f_ref,
    xlo_ref,
    xhi_ref,
    ylo_ref,
    yhi_ref,
    chosen_ref,
    source_pick_ref,
    target_pick_ref,
    w_hbm,
    new_hbm,
    keep_hbm,
    give_hbm,
    send_hbm,
    first_ref,
    second_ref,
    shuffle_ref,
    natural_ref,
    both_ref,
    w_ref,
    new_ref,
    send_ref,
    done,
):
    load_w = pltpu.make_async_copy(w_hbm, w_ref, done.at[0])
    load_w.start()
    wide_x, wide_y, wide_z = shape
    patches = (wide_x // PATCH) * (wide_y // PATCH) * (wide_z // PATCH)
    top_x, top_y = REACH + wide_x, LIFT + wide_y
    full_x, full_y = top_x + REACH, top_y + LIFT
    lane = lax.broadcasted_iota(jnp.int32, (1, wide_z), 1)
    inside = {k: (lane + k >= 0) & (lane + k < wide_z) for k in OFFSETS}
    own_z = {k: jnp.where(inside[k], OWN_Z[k], 0.0) for k in OFFSETS}
    push_z = {k: jnp.where(inside[k], PUSH[k], 0.0) for k in OFFSETS}

    first_ref[:, REACH:top_x, LIFT:top_y, :] = f_ref[...]
    first_ref[:, 0:REACH, LIFT:top_y, :] = xlo_ref[...].astype(jnp.float32)
    first_ref[:, top_x:full_x, LIFT:top_y, :] = xhi_ref[...].astype(jnp.float32)
    for field in range(FIELDS):
        for layer, beside, lines, place in strip_layers(wide_x)[0]:
            rows = slice(REACH - beside, REACH - beside + lines)
            packed = slice(place, place + lines)
            first_ref[field, rows, LIFT - 1 - layer, :] = ylo_ref[field, packed].astype(
                jnp.float32
            )
            first_ref[field, rows, top_y + layer, :] = yhi_ref[field, packed].astype(
                jnp.float32
            )

    def clear(ref, least):
        @pl.when(edge_ref[0] == 1)
        def _():
            ref[:, least:REACH] = jnp.zeros((FIELDS, REACH - least, full_y, wide_z), jnp.float32)

        @pl.when(edge_ref[1] == 1)
        def _():
            ref[:, top_x : full_x - least] = jnp.zeros(
                (FIELDS, REACH - least, full_y, wide_z), jnp.float32
            )

        @pl.when(edge_ref[2] == 1)
        def _():
            ref[:, :, 0:LIFT] = jnp.zeros((FIELDS, full_x, LIFT, wide_z), jnp.float32)

        @pl.when(edge_ref[3] == 1)
        def _():
            ref[:, :, top_y:full_y] = jnp.zeros((FIELDS, full_x, LIFT, wide_z), jnp.float32)

    def step(src, dst, least):
        def body(row, carry):
            done = one_row(src, row, own_z, push_z, None)
            for field in range(FIELDS):
                dst[field, row] = done[field]
            return carry

        lax.fori_loop(least, full_x - least, body, 0, unroll=2)
        clear(dst, least)

    def last_step(src):
        def body(row, carry):
            done = one_row(src, row, own_z, push_z, (LIFT, top_y))
            for field in range(FIELDS):
                new_ref[field, row - REACH] = done[field]
            return carry

        lax.fori_loop(REACH, top_x, body, 0, unroll=2)

    z_count = wide_z // PATCH
    lane_r = lax.broadcasted_iota(jnp.int32, (wide_z, wide_z), 0)
    lane_c = lax.broadcasted_iota(jnp.int32, (wide_z, wide_z), 1)
    swap = jnp.where(
        (lane_r // PATCH == lane_c % z_count) & (lane_r % PATCH == lane_c // z_count), 1.0, 0.0
    ).astype(jnp.bfloat16)
    group = lax.broadcasted_iota(jnp.int32, (PATCH, wide_z), 1) // z_count

    def into_patches(load, store):
        for field in range(FIELDS):
            flat = load(field).reshape(wide_x * wide_y, wide_z)
            shuffle_ref[field] = jnp.dot(
                flat.astype(jnp.bfloat16), swap, preferred_element_type=jnp.float32
            ).reshape(wide_x, wide_y, wide_z)

        for field in range(FIELDS):
            tiles = [
                shuffle_ref[
                    field, px * PATCH : (px + 1) * PATCH, py * PATCH : (py + 1) * PATCH
                ]
                for px in range(wide_x // PATCH)
                for py in range(wide_y // PATCH)
            ]
            for bit in (4, 2, 1):
                low = ((group & bit) == 0)[None]
                fresh = list(tiles)
                for i in range(PATCH):
                    if i & bit:
                        continue
                    a, b = tiles[i], tiles[i | bit]
                    fresh[i] = jnp.where(low, a, pltpu.roll(b, bit * z_count, 2))
                    fresh[i | bit] = jnp.where(
                        low, pltpu.roll(a, wide_z - bit * z_count, 2), b
                    )
                tiles = fresh
            for inner_z in range(PATCH):
                natural_ref[
                    field * PATCH : (field + 1) * PATCH, pl.ds(inner_z, PATCH, stride=PATCH), :
                ] = tiles[inner_z]

        for field in range(FIELDS):
            block = natural_ref[field * PATCH : (field + 1) * PATCH]
            block = block.reshape(PATCH**3, patches).astype(jnp.bfloat16)
            store(field * PATCH**3, block)

    def keep_picked(at, block):
        both_ref[at : at + PATCH**3, 0:patches] = block

    def keep_target(at, block):
        both_ref[at : at + PATCH**3, patches : 2 * patches] = block

    def chosen(field):
        one = second_ref[field, REACH:top_x, LIFT:top_y]
        two = first_ref[field, REACH:top_x, LIFT:top_y]
        one = one.reshape(wide_x // PATCH, PATCH, wide_y, wide_z)
        two = two.reshape(wide_x // PATCH, PATCH, wide_y, wide_z)
        later = chosen_ref[...].reshape(wide_x // PATCH, 1, wide_y, wide_z)
        return jnp.where(later == 1.0, two, one)

    step(first_ref, second_ref, 2)
    step(second_ref, first_ref, 4)
    last_step(first_ref)
    store_new = pltpu.make_async_copy(new_ref, new_hbm, done.at[1])
    store_new.start()
    into_patches(chosen, keep_picked)
    into_patches(lambda field: new_ref[field], keep_target)

    half = both_ref.shape[0] // 2
    mine = pl.multiple_of(edge_ref[4] * half, half)
    lanes = slice(0, patches)
    store_keep = pltpu.make_async_copy(both_ref.at[pl.ds(mine, half), lanes], keep_hbm, done.at[2])
    store_give = pltpu.make_async_copy(
        both_ref.at[pl.ds(half - mine, half), lanes], give_hbm, done.at[3]
    )
    store_give.start()
    store_keep.start()
    load_w.wait()
    embedded = contract_rows(both_ref[...], w_ref[...]).astype(jnp.bfloat16)
    rows = send_ref.shape[0]
    pieces = 4
    stores = []
    for piece in range(pieces):
        lines = slice(piece * rows // pieces, (piece + 1) * rows // pieces)
        wanted = target_pick_ref[lines]
        filled = jnp.sum(wanted.astype(jnp.float32), axis=1, keepdims=True)
        line = lax.broadcasted_iota(jnp.int32, (rows // pieces, 1), 0)
        marker = jnp.where((line // per % 2 == 1) & (filled == 0.0), EMPTY, 0.0)
        placed = jnp.dot(
            source_pick_ref[lines], embedded[0:patches], preferred_element_type=jnp.float32
        )
        placed = placed + jnp.dot(
            wanted, embedded[patches : 2 * patches], preferred_element_type=jnp.float32
        )
        send_ref[lines] = (placed + marker).astype(jnp.bfloat16)
        store = pltpu.make_async_copy(send_ref.at[lines], send_hbm.at[lines], done.at[4 + piece])
        store.start()
        stores.append(store)
    for store in [store_new, store_keep, store_give] + stores:
        store.wait()


def trainer_kernel(
    per,
    got_ref,
    w_in_ref,
    b_in_ref,
    w_out_ref,
    b_out_ref,
    source_ref,
    hidden_ref,
    error_ref,
    pre_grad_ref,
    b_in_grad_ref,
    b_out_grad_ref,
    back_ref,
    target_ref,
    slope_ref,
):
    rows = source_ref.shape[0]
    width = back_ref.shape[1]
    small, large = 32 * per, 64 * per
    line = lax.broadcasted_iota(jnp.int32, (small, large), 0)
    taken = lax.broadcasted_iota(jnp.int32, (small, large), 1)
    first = line // per * (2 * per) + line % per
    source_pick = jnp.where(taken == first, 1.0, 0.0).astype(jnp.bfloat16)
    target_pick = jnp.where(taken == first + per, 1.0, 0.0).astype(jnp.bfloat16)
    for at in range(rows // small):
        block = got_ref[at * large : (at + 1) * large]
        lines = slice(at * small, (at + 1) * small)
        source_ref[lines] = jnp.dot(
            source_pick, block, preferred_element_type=jnp.float32
        ).astype(jnp.bfloat16)
        target_ref[lines] = jnp.dot(target_pick, block, preferred_element_type=jnp.float32)

    chunk = 512
    hidden_size = hidden_ref.shape[1]
    source = source_ref[...]
    predict = jnp.broadcast_to(b_out_ref[...], target_ref.shape)
    for start in range(0, hidden_size, chunk):
        lanes = slice(start, start + chunk)
        pre = jnp.dot(source, w_in_ref[:, lanes], preferred_element_type=jnp.float32)
        pre = pre + b_in_ref[:, lanes]
        sigma = jax.nn.sigmoid(pre)
        hidden = (pre * sigma).astype(jnp.bfloat16)
        hidden_ref[:, lanes] = hidden
        slope_ref[:, lanes] = sigma * (1.0 + pre * (1.0 - sigma))
        predict = predict + jnp.dot(
            hidden, w_out_ref[lanes], preferred_element_type=jnp.float32
        )
    wanted = target_ref[...]
    error = jnp.where(wanted < FULL_BELOW, error_weight * (predict - wanted), 0.0)
    error = error.astype(jnp.bfloat16)
    error_ref[...] = error
    b_out_grad_ref[...] = jnp.sum(error.astype(jnp.float32), axis=0, keepdims=True)
    total = jnp.zeros(target_ref.shape, jnp.float32)
    for start in range(0, hidden_size, chunk):
        lanes = slice(start, start + chunk)
        upstream = contract_cols(error, w_out_ref[lanes])
        pre_grad = (upstream * slope_ref[:, lanes]).astype(jnp.bfloat16)
        pre_grad_ref[:, lanes] = pre_grad
        b_in_grad_ref[:, lanes] = jnp.sum(
            pre_grad.astype(jnp.float32), axis=0, keepdims=True
        )
        total = total + contract_cols(pre_grad, w_in_ref[:, lanes])
    gradient = total.astype(jnp.bfloat16)
    out = lax.broadcasted_iota(jnp.int32, (large, small), 0)
    origin = lax.broadcasted_iota(jnp.int32, (large, small), 1)
    fits = origin == out // (2 * per) * per + out % per
    side = out // per % 2
    for at in range(rows // small):
        lines = slice(at * small, (at + 1) * small)
        block = jnp.zeros((large, width), jnp.float32)
        for half in range(2):
            move = jnp.where(fits & (side == half), 1.0, 0.0).astype(jnp.bfloat16)
            block = block + jnp.dot(
                move,
                gradient[lines, half * width : (half + 1) * width],
                preferred_element_type=jnp.float32,
            )
        back_ref[at * large : (at + 1) * large] = block.astype(jnp.bfloat16)


def gather_kernel(source_pick_ref, target_pick_ref, back_ref, out_ref):
    width = back_ref.shape[1]
    for half, pick_ref in enumerate((source_pick_ref, target_pick_ref)):
        out_ref[:, half * width : (half + 1) * width] = contract_rows(
            pick_ref[...], back_ref[...]
        ).astype(jnp.bfloat16)


def part_kernel(
    keep_hbm, got_hbm, own_grad_ref, other_grad_ref, part_ref, keep_ref, got_ref, loaded
):
    loads = (
        pltpu.make_async_copy(keep_hbm, keep_ref, loaded.at[0]),
        pltpu.make_async_copy(got_hbm, got_ref, loaded.at[1]),
    )
    for load in loads:
        load.start()
    half = keep_ref.shape[0]
    width = part_ref.shape[1]
    loads[0].wait()
    total = jnp.dot(keep_ref[...], own_grad_ref[...], preferred_element_type=jnp.float32)
    loads[1].wait()
    total = total + jnp.dot(
        got_ref[...], other_grad_ref[...], preferred_element_type=jnp.float32
    )
    for side in range(EMBED // width):
        part_ref[side * half : (side + 1) * half, :] = total[
            :, side * width : (side + 1) * width
        ].astype(jnp.bfloat16)


def sum_kernel(parts_ref, copies_ref):
    total = jnp.sum(parts_ref[...].astype(jnp.float32), axis=0).astype(jnp.bfloat16)
    copies_ref[...] = jnp.broadcast_to(total[None], copies_ref.shape)


def spread_kernel(other, edge_ref, half_ref, *rest):
    out_hbm, wide_ref, done = rest[-3:]
    half, width = wide_ref.shape[0], half_ref.shape[1]
    core = 1 - edge_ref[4] if other else edge_ref[4]
    begin = core * half
    pieces = 4
    stores = []
    for piece in range(pieces):
        lines = slice(piece * half // pieces, (piece + 1) * half // pieces)
        for side in range(EMBED // width):
            lanes = slice(side * width, (side + 1) * width)
            rows = slice(side * half + lines.start, side * half + lines.stop)
            wide_ref[lines, lanes] = half_ref[rows].astype(jnp.float32)
        at = pl.multiple_of(begin + lines.start, half // pieces)
        store = pltpu.make_async_copy(
            wide_ref.at[lines], out_hbm.at[pl.ds(at, half // pieces)], done.at[piece]
        )
        store.start()
        stores.append(store)
    for store in stores:
        store.wait()


def neighbours(low_piece, high_piece, axis):
    count = lax.axis_size(axis)
    up = [(i, i + 1) for i in range(count - 1)]
    down = [(b, a) for a, b in up]
    return lax.ppermute(high_piece, axis, up), lax.ppermute(low_piece, axis, down)


def contract_rows(left, right):
    return lax.dot_general(
        left, right, (((0,), (0,)), ((), ())), preferred_element_type=jnp.float32
    )


def contract_cols(left, right):
    return lax.dot_general(
        left, right, (((1,), (1,)), ((), ())), preferred_element_type=jnp.float32
    )


def per_device(fields, patch_weight, trainer_of, lag_index, w_in, b_in, w_out, b_out):
    axes = ("gx", "gy")
    n_x, n_y = lax.axis_size("gx"), lax.axis_size("gy")
    devices = n_x * n_y
    _, wide_x, wide_y, wide_z = fields.shape
    patches = (wide_x // PATCH) * (wide_y // PATCH) * (wide_z // PATCH)
    blocks = patches // BLOCK_ROWS
    slots = max(2, 2 * blocks // devices)
    per = slots * BLOCK_ROWS
    features = FIELDS * PATCH**3

    def narrow(piece):
        return piece.astype(jnp.bfloat16)

    xlo, xhi = neighbours(narrow(fields[:, :REACH]), narrow(fields[:, wide_x - REACH :]), "gx")
    at_x, at_y = lax.axis_index("gx"), lax.axis_index("gy")
    core = at_x % 2
    edges = jnp.stack(
        [at_x == 0, at_x == n_x - 1, at_y == 0, at_y == n_y - 1, core == 1]
    ).astype(jnp.int32)
    own_patch = jnp.repeat(trainer_of[:, 0], BLOCK_ROWS)
    lag = lag_index.reshape(-1, lag_index.shape[2]).astype(jnp.float32)

    vmem = pl.BlockSpec(memory_space=pltpu.VMEM)
    smem = pl.BlockSpec(memory_space=pltpu.SMEM)
    hbm = pl.BlockSpec(memory_space=pltpu.HBM)

    def grant(mebibytes):
        return pltpu.CompilerParams(vmem_limit_bytes=mebibytes * 1024 * 1024)

    def shape(dims, kind):
        return jax.ShapeDtypeStruct(dims, kind)

    layers, strip = strip_layers(wide_x)
    y_first, y_last = pl.pallas_call(
        strips_kernel,
        out_shape=(shape((FIELDS, strip, wide_z), jnp.bfloat16),) * 2,
        in_specs=[vmem] * 3,
        out_specs=(vmem,) * 2,
        scratch_shapes=[pltpu.VMEM((FIELDS, layers[0][2] * LIFT, wide_z), jnp.float32)],
        compiler_params=grant(8),
        name="strips",
    )(fields, xlo, xhi)
    ylo, yhi = neighbours(y_first, y_last, "gy")

    send_rows = 2 * devices * per
    source_pick, target_pick, chosen = pl.pallas_call(
        functools.partial(slots_kernel, slots),
        out_shape=(
            shape((send_rows, patches), jnp.bfloat16),
            shape((send_rows, patches), jnp.bfloat16),
            shape(((wide_x // PATCH) * wide_y, wide_z), jnp.float32),
        ),
        in_specs=[vmem] * 3,
        out_specs=(vmem,) * 3,
        compiler_params=grant(8),
        name="slots",
    )(own_patch[None, :], own_patch[:, None], lag)

    full = (FIELDS, wide_x + 2 * REACH, wide_y + 2 * LIFT, wide_z)
    new_fields, keep, give, send = pl.pallas_call(
        functools.partial(window_kernel, (wide_x, wide_y, wide_z), per),
        out_shape=(
            shape(fields.shape, jnp.float32),
            shape((features // 2, patches), jnp.bfloat16),
            shape((features // 2, patches), jnp.bfloat16),
            shape((send_rows, EMBED), jnp.bfloat16),
        ),
        in_specs=[smem] + [vmem] * 8 + [hbm],
        out_specs=(hbm,) * 4,
        scratch_shapes=[
            pltpu.VMEM(full, jnp.float32),
            pltpu.VMEM(full, jnp.float32),
            pltpu.VMEM((FIELDS, wide_x, wide_y, wide_z), jnp.float32),
            pltpu.VMEM((FIELDS * PATCH, PATCH * PATCH, patches), jnp.float32),
            pltpu.VMEM((features, 2 * patches), jnp.bfloat16),
            pltpu.VMEM((features, EMBED), jnp.bfloat16),
            pltpu.VMEM((FIELDS, wide_x, wide_y, wide_z), jnp.float32),
            pltpu.VMEM((send_rows, EMBED), jnp.bfloat16),
            pltpu.SemaphoreType.DMA((8,)),
        ],
        compiler_params=grant(50),
        name="window",
    )(
        edges, fields, xlo, xhi, ylo, yhi, chosen, source_pick, target_pick, patch_weight
    )

    pairs = [(i, i ^ 1) for i in range(n_x)]
    groups = [
        [x * n_y + y for x in range(n_x) for y in range(n_y) if x % 2 == c] for c in range(2)
    ]
    members = devices // 2
    got_picked = lax.ppermute(give, "gx", pairs)
    got = lax.all_to_all(send.reshape(devices, 2 * per, EMBED), axes, 0, 0, tiled=True)
    rows = devices * per
    hidden_size = w_in.shape[2]
    width = EMBED // 2
    source, hidden, error, pre_grad, b_in_grad, b_out_grad, back = pl.pallas_call(
        functools.partial(trainer_kernel, per),
        out_shape=(
            shape((rows, EMBED), jnp.bfloat16),
            shape((rows, hidden_size), jnp.bfloat16),
            shape((rows, EMBED), jnp.bfloat16),
            shape((rows, hidden_size), jnp.bfloat16),
            shape((1, hidden_size), jnp.float32),
            shape((1, EMBED), jnp.float32),
            shape((2 * rows, width), jnp.bfloat16),
        ),
        in_specs=[vmem] * 5,
        out_specs=(vmem,) * 7,
        scratch_shapes=[
            pltpu.VMEM((rows, EMBED), jnp.float32),
            pltpu.VMEM((rows, hidden_size), jnp.float32),
        ],
        compiler_params=grant(50),
        name="trainer",
    )(got.reshape(send_rows, EMBED), w_in[0], b_in, w_out[0], b_out)
    back = lax.all_to_all(back.reshape(devices, 2 * per, width), axes, 0, 0, tiled=True)
    w_in_grad = contract_rows(source, pre_grad)
    w_out_grad = contract_rows(hidden, error)
    back, w_in_grad, w_out_grad = lax.optimization_barrier((back, w_in_grad, w_out_grad))
    own_grad = pl.pallas_call(
        gather_kernel,
        out_shape=shape((patches, EMBED), jnp.bfloat16),
        in_specs=[vmem] * 3,
        out_specs=vmem,
        compiler_params=grant(8),
        name="gather",
    )(source_pick, target_pick, back.reshape(send_rows, width))
    other_grad = lax.ppermute(own_grad, "gx", pairs)
    piece = features // members
    parts = pl.pallas_call(
        part_kernel,
        out_shape=shape((features, width), jnp.bfloat16),
        in_specs=[hbm, hbm, vmem, vmem],
        out_specs=vmem,
        scratch_shapes=[
            pltpu.VMEM((features // 2, patches), jnp.bfloat16),
            pltpu.VMEM((features // 2, patches), jnp.bfloat16),
            pltpu.SemaphoreType.DMA((2,)),
        ],
        compiler_params=grant(24),
        name="part",
    )(keep, got_picked, own_grad, other_grad)
    parts = lax.all_to_all(
        parts.reshape(members, piece, width), axes, 0, 0, axis_index_groups=groups, tiled=True
    )
    copies = pl.pallas_call(
        sum_kernel,
        out_shape=jax.ShapeDtypeStruct((members, piece, width), jnp.bfloat16),
        in_specs=[vmem],
        out_specs=vmem,
        compiler_params=grant(16),
        name="total",
    )(parts)
    own_half = lax.all_to_all(copies, axes, 0, 0, axis_index_groups=groups, tiled=True)
    own_half = own_half.reshape(features, width)
    other_half = lax.ppermute(own_half, "gx", pairs)

    def spread(other, *operands):
        return pl.pallas_call(
            functools.partial(spread_kernel, other),
            out_shape=shape((features, EMBED), jnp.float32),
            in_specs=[smem, vmem] + [hbm] * (len(operands) - 2),
            out_specs=hbm,
            scratch_shapes=[
                pltpu.VMEM((features // 2, EMBED), jnp.float32),
                pltpu.SemaphoreType.DMA((4,)),
            ],
            input_output_aliases={2: 0} if other else {},
            compiler_params=grant(8),
            name="spread_other" if other else "spread_own",
        )(*operands)

    patch_gradient = spread(False, edges, own_half)
    patch_gradient = spread(True, edges, other_half, patch_gradient)
    return (
        new_fields,
        patch_gradient,
        w_in_grad[None],
        b_in_grad,
        w_out_grad[None],
        b_out_grad,
    )


def solution(mesh):
    in_specs = (
        P(None, "gx", "gy", None),
        P(),
        P(("gx", "gy"), None),
        P("gx", "gy", None),
        P(("gx", "gy"), None, None),
        P(("gx", "gy"), None),
        P(("gx", "gy"), None, None),
        P(("gx", "gy"), None),
    )
    out_specs = (
        P(None, "gx", "gy", None),
        P(),
        P(("gx", "gy"), None, None),
        P(("gx", "gy"), None),
        P(("gx", "gy"), None, None),
        P(("gx", "gy"), None),
    )
    return jax.shard_map(
        per_device, mesh=mesh, in_specs=in_specs, out_specs=out_specs, check_vma=False
    )
```

```python
import functools

import jax
import jax.numpy as jnp
from jax import lax
from jax.experimental import pallas as pl
from jax.experimental.pallas import tpu as pltpu
from jax.sharding import PartitionSpec as P

FIELDS = 5
PATCH = 8
STEPS = 3
EMBED = 512
BLOCK_ROWS = 2
REACH = 2 * STEPS
LIFT = 8
EMPTY = 1.0e30
FULL_BELOW = 1.0e29

time_step = 0.2
viscosity = 0.5
drift_x = 0.6
drift_y = -0.4
drift_z = 0.3
error_weight = 0.0625

SLOPE = {-2: 1.0 / 12.0, -1: -8.0 / 12.0, 1: 8.0 / 12.0, 2: -1.0 / 12.0}
BEND = {-2: -1.0 / 12.0, -1: 16.0 / 12.0, 1: 16.0 / 12.0, 2: -1.0 / 12.0}
OFFSETS = (-2, -1, 1, 2)


def own_weights(drift):
    return {k: time_step * (viscosity * BEND[k] - drift * SLOPE[k]) for k in OFFSETS}


OWN_X, OWN_Y, OWN_Z = own_weights(drift_x), own_weights(drift_y), own_weights(drift_z)
MIDDLE = 1.0 - time_step * viscosity * 3.0 * 30.0 / 12.0
PUSH = {k: -time_step * SLOPE[k] for k in OFFSETS}


def rolled(value, offset, axis):
    size = value.shape[axis]
    return pltpu.roll(value, (-offset) % size, axis)


def weighted(pieces, weights):
    total = None
    for k in OFFSETS:
        term = pieces[k] * weights[k]
        total = term if total is None else total + term
    return total


def slope_of(pieces):
    return (pieces[-1] - pieces[1]) * PUSH[-1] + (pieces[2] - pieces[-2]) * PUSH[2]


def one_row(src, row, own_z, push_z, window):
    def along(field):
        middle = src[field, row]
        xs = {k: src[field, row + k] for k in OFFSETS}
        ys = {k: rolled(middle, k, 0) for k in OFFSETS}
        zs = {k: rolled(middle, k, 1) for k in OFFSETS}
        return middle, xs, ys, zs

    def own(middle, xs, ys, zs):
        return (
            middle * MIDDLE + weighted(xs, OWN_X) + weighted(ys, OWN_Y) + weighted(zs, own_z)
        )

    cut = (lambda v: v) if window is None else (lambda v: v[window[0] : window[1]])
    parts = along(4)
    pressure = cut(own(*parts))
    px, py, pz = cut(slope_of(parts[1])), cut(slope_of(parts[2])), cut(weighted(parts[3], push_z))
    parts = along(1)
    first = cut(own(*parts)) + px
    spread = cut(slope_of(parts[1]))
    parts = along(2)
    second = cut(own(*parts)) + py
    spread = spread + cut(slope_of(parts[2]))
    parts = along(3)
    third = cut(own(*parts)) + pz
    spread = spread + cut(weighted(parts[3], push_z))
    parts = along(0)
    density = cut(own(*parts)) + spread
    return density, first, second, third, pressure + spread


def slots_kernel(slots, own_row_ref, own_col_ref, lag_ref, source_ref, target_ref, chosen_ref):
    rows, patches = source_ref.shape
    per = slots * BLOCK_ROWS
    at_r = lax.broadcasted_iota(jnp.int32, (patches, patches), 0)
    at_c = lax.broadcasted_iota(jnp.int32, (patches, patches), 1)
    earlier = (at_r // BLOCK_ROWS < at_c // BLOCK_ROWS) & (at_r % BLOCK_ROWS == 0)
    hit = (own_row_ref[...] == own_col_ref[...]) & earlier
    rank = jnp.sum(jnp.where(hit, 1.0, 0.0), axis=0, keepdims=True).astype(jnp.int32)
    place = lax.broadcasted_iota(jnp.int32, (1, patches), 1) % BLOCK_ROWS
    at = own_row_ref[...] * (2 * per) + rank * BLOCK_ROWS + place
    row = lax.broadcasted_iota(jnp.int32, (rows, patches), 0)
    source_ref[...] = jnp.where(row == at, 1.0, 0.0).astype(jnp.bfloat16)
    target_ref[...] = jnp.where(row == at + per, 1.0, 0.0).astype(jnp.bfloat16)
    tall, wide = chosen_ref.shape
    bricks, deep = lag_ref.shape
    along = lax.broadcasted_iota(jnp.int32, (deep, wide), 0)
    cells = lax.broadcasted_iota(jnp.int32, (deep, wide), 1)
    spread = jnp.where(along == cells // PATCH, 1.0, 0.0).astype(jnp.bfloat16)
    lanes = jnp.dot(
        lag_ref[...].astype(jnp.bfloat16), spread, preferred_element_type=jnp.float32
    )
    line = lax.broadcasted_iota(jnp.int32, (tall, bricks), 0)
    brick = lax.broadcasted_iota(jnp.int32, (tall, bricks), 1)
    lift = jnp.where(line // PATCH == brick, 1.0, 0.0).astype(jnp.bfloat16)
    chosen_ref[...] = jnp.dot(
        lift, lanes.astype(jnp.bfloat16), preferred_element_type=jnp.float32
    )


CORNER = 4


def faces_kernel(f_ref, x_first_ref, x_last_ref, y_first_ref, y_last_ref, lines_ref):
    wide_x, wide_y = f_ref.shape[1], f_ref.shape[2]
    x_first_ref[...] = f_ref[:, :REACH].astype(jnp.bfloat16)
    x_last_ref[...] = f_ref[:, wide_x - REACH :].astype(jnp.bfloat16)
    for at, out_ref in ((0, y_first_ref), (wide_y - LIFT, y_last_ref)):
        for field in range(FIELDS):
            for row in range(wide_x):
                lines_ref[row * LIFT : (row + 1) * LIFT] = f_ref[field, row, at : at + LIFT]
            for layer in range(REACH):
                line = layer if at == 0 else LIFT - 1 - layer
                out_ref[field, layer * wide_x : (layer + 1) * wide_x] = lines_ref[
                    pl.ds(line, wide_x, stride=LIFT), :
                ].astype(jnp.bfloat16)


def corners_kernel(xlo_ref, xhi_ref, first_ref, last_ref, lines_ref):
    wide_y = xlo_ref.shape[2]
    for at, out_ref in ((0, first_ref), (wide_y - LIFT, last_ref)):
        for field in range(FIELDS):
            for row in range(CORNER):
                for begin, ref, base in ((0, xlo_ref, REACH - CORNER), (CORNER, xhi_ref, 0)):
                    place = (begin + row) * LIFT
                    lines_ref[place : place + LIFT] = ref[
                        field, base + row, at : at + LIFT
                    ].astype(jnp.float32)
            picked = []
            for layer in range(CORNER):
                line = layer if at == 0 else LIFT - 1 - layer
                picked.append(lines_ref[pl.ds(line, 2 * CORNER, stride=LIFT), :])
            out_ref[field] = jnp.concatenate(picked, axis=0).astype(jnp.bfloat16)


def window_kernel(
    shape,
    per,
    edge_ref,
    f_ref,
    xlo_ref,
    xhi_ref,
    ylo_ref,
    yhi_ref,
    corner_lo_ref,
    corner_hi_ref,
    chosen_ref,
    source_pick_ref,
    target_pick_ref,
    w_hbm,
    new_hbm,
    keep_hbm,
    give_hbm,
    send_hbm,
    first_ref,
    second_ref,
    shuffle_ref,
    natural_ref,
    both_ref,
    w_ref,
    new_ref,
    send_ref,
    done,
):
    load_w = pltpu.make_async_copy(w_hbm, w_ref, done.at[0])
    load_w.start()
    wide_x, wide_y, wide_z = shape
    patches = (wide_x // PATCH) * (wide_y // PATCH) * (wide_z // PATCH)
    top_x, top_y = REACH + wide_x, LIFT + wide_y
    full_x, full_y = top_x + REACH, top_y + LIFT
    lane = lax.broadcasted_iota(jnp.int32, (1, wide_z), 1)
    inside = {k: (lane + k >= 0) & (lane + k < wide_z) for k in OFFSETS}
    own_z = {k: jnp.where(inside[k], OWN_Z[k], 0.0) for k in OFFSETS}
    push_z = {k: jnp.where(inside[k], PUSH[k], 0.0) for k in OFFSETS}

    first_ref[:, REACH:top_x, LIFT:top_y, :] = f_ref[...]
    first_ref[:, 0:REACH, LIFT:top_y, :] = xlo_ref[...].astype(jnp.float32)
    first_ref[:, top_x:full_x, LIFT:top_y, :] = xhi_ref[...].astype(jnp.float32)
    for field in range(FIELDS):
        for low, face_ref, corner_ref in (
            (True, ylo_ref, corner_lo_ref),
            (False, yhi_ref, corner_hi_ref),
        ):
            face = face_ref[field].astype(jnp.float32)
            corner = corner_ref[field].astype(jnp.float32)
            for layer in range(REACH):
                line = LIFT - 1 - layer if low else top_y + layer
                first_ref[field, REACH:top_x, line, :] = face[
                    layer * wide_x : (layer + 1) * wide_x
                ]
                if layer >= CORNER:
                    continue
                at = layer * 2 * CORNER
                first_ref[field, REACH - CORNER : REACH, line, :] = corner[at : at + CORNER]
                first_ref[field, top_x : top_x + CORNER, line, :] = corner[
                    at + CORNER : at + 2 * CORNER
                ]

    def clear(ref, least):
        @pl.when(edge_ref[0] == 1)
        def _():
            ref[:, least:REACH] = jnp.zeros((FIELDS, REACH - least, full_y, wide_z), jnp.float32)

        @pl.when(edge_ref[1] == 1)
        def _():
            ref[:, top_x : full_x - least] = jnp.zeros(
                (FIELDS, REACH - least, full_y, wide_z), jnp.float32
            )

        @pl.when(edge_ref[2] == 1)
        def _():
            ref[:, :, 0:LIFT] = jnp.zeros((FIELDS, full_x, LIFT, wide_z), jnp.float32)

        @pl.when(edge_ref[3] == 1)
        def _():
            ref[:, :, top_y:full_y] = jnp.zeros((FIELDS, full_x, LIFT, wide_z), jnp.float32)

    def step(src, dst, least):
        def body(row, carry):
            done = one_row(src, row, own_z, push_z, None)
            for field in range(FIELDS):
                dst[field, row] = done[field]
            return carry

        lax.fori_loop(least, full_x - least, body, 0, unroll=2)
        clear(dst, least)

    def last_step(src):
        def body(row, carry):
            done = one_row(src, row, own_z, push_z, (LIFT, top_y))
            for field in range(FIELDS):
                new_ref[field, row - REACH] = done[field]
            return carry

        lax.fori_loop(REACH, top_x, body, 0, unroll=2)

    z_count = wide_z // PATCH
    lane_r = lax.broadcasted_iota(jnp.int32, (wide_z, wide_z), 0)
    lane_c = lax.broadcasted_iota(jnp.int32, (wide_z, wide_z), 1)
    swap = jnp.where(
        (lane_r // PATCH == lane_c % z_count) & (lane_r % PATCH == lane_c // z_count), 1.0, 0.0
    ).astype(jnp.bfloat16)
    group = lax.broadcasted_iota(jnp.int32, (PATCH, wide_z), 1) // z_count

    def into_patches(load, store):
        for field in range(FIELDS):
            flat = load(field).reshape(wide_x * wide_y, wide_z)
            shuffle_ref[field] = jnp.dot(
                flat.astype(jnp.bfloat16), swap, preferred_element_type=jnp.float32
            ).reshape(wide_x, wide_y, wide_z)

        for field in range(FIELDS):
            tiles = [
                shuffle_ref[
                    field, px * PATCH : (px + 1) * PATCH, py * PATCH : (py + 1) * PATCH
                ]
                for px in range(wide_x // PATCH)
                for py in range(wide_y // PATCH)
            ]
            for bit in (4, 2, 1):
                low = ((group & bit) == 0)[None]
                fresh = list(tiles)
                for i in range(PATCH):
                    if i & bit:
                        continue
                    a, b = tiles[i], tiles[i | bit]
                    fresh[i] = jnp.where(low, a, pltpu.roll(b, bit * z_count, 2))
                    fresh[i | bit] = jnp.where(
                        low, pltpu.roll(a, wide_z - bit * z_count, 2), b
                    )
                tiles = fresh
            for inner_z in range(PATCH):
                natural_ref[
                    field * PATCH : (field + 1) * PATCH, pl.ds(inner_z, PATCH, stride=PATCH), :
                ] = tiles[inner_z]

        for field in range(FIELDS):
            block = natural_ref[field * PATCH : (field + 1) * PATCH]
            block = block.reshape(PATCH**3, patches).astype(jnp.bfloat16)
            store(field * PATCH**3, block)

    def keep_picked(at, block):
        both_ref[at : at + PATCH**3, 0:patches] = block

    def keep_target(at, block):
        both_ref[at : at + PATCH**3, patches : 2 * patches] = block

    def chosen(field):
        one = second_ref[field, REACH:top_x, LIFT:top_y]
        two = first_ref[field, REACH:top_x, LIFT:top_y]
        one = one.reshape(wide_x // PATCH, PATCH, wide_y, wide_z)
        two = two.reshape(wide_x // PATCH, PATCH, wide_y, wide_z)
        later = chosen_ref[...].reshape(wide_x // PATCH, 1, wide_y, wide_z)
        return jnp.where(later == 1.0, two, one)

    step(first_ref, second_ref, 2)
    step(second_ref, first_ref, 4)
    last_step(first_ref)
    store_new = pltpu.make_async_copy(new_ref, new_hbm, done.at[1])
    store_new.start()
    into_patches(chosen, keep_picked)
    into_patches(lambda field: new_ref[field], keep_target)

    half = both_ref.shape[0] // 2
    mine = pl.multiple_of(edge_ref[4] * half, half)
    lanes = slice(0, patches)
    store_keep = pltpu.make_async_copy(both_ref.at[pl.ds(mine, half), lanes], keep_hbm, done.at[2])
    store_give = pltpu.make_async_copy(
        both_ref.at[pl.ds(half - mine, half), lanes], give_hbm, done.at[3]
    )
    store_give.start()
    store_keep.start()
    load_w.wait()
    embedded = contract_rows(both_ref[...], w_ref[...]).astype(jnp.bfloat16)
    rows = send_ref.shape[0]
    pieces = 4
    stores = []
    for piece in range(pieces):
        lines = slice(piece * rows // pieces, (piece + 1) * rows // pieces)
        wanted = target_pick_ref[lines]
        filled = jnp.sum(wanted.astype(jnp.float32), axis=1, keepdims=True)
        line = lax.broadcasted_iota(jnp.int32, (rows // pieces, 1), 0)
        marker = jnp.where((line // per % 2 == 1) & (filled == 0.0), EMPTY, 0.0)
        placed = jnp.dot(
            source_pick_ref[lines], embedded[0:patches], preferred_element_type=jnp.float32
        )
        placed = placed + jnp.dot(
            wanted, embedded[patches : 2 * patches], preferred_element_type=jnp.float32
        )
        send_ref[lines] = (placed + marker).astype(jnp.bfloat16)
        store = pltpu.make_async_copy(send_ref.at[lines], send_hbm.at[lines], done.at[4 + piece])
        store.start()
        stores.append(store)
    for store in [store_new, store_keep, store_give] + stores:
        store.wait()


def trainer_kernel(
    per,
    got_ref,
    w_in_ref,
    b_in_ref,
    w_out_ref,
    b_out_ref,
    source_ref,
    hidden_ref,
    error_ref,
    pre_grad_ref,
    b_in_grad_ref,
    b_out_grad_ref,
    back_ref,
    target_ref,
    slope_ref,
):
    rows = source_ref.shape[0]
    width = back_ref.shape[1]
    small, large = 32 * per, 64 * per
    line = lax.broadcasted_iota(jnp.int32, (small, large), 0)
    taken = lax.broadcasted_iota(jnp.int32, (small, large), 1)
    first = line // per * (2 * per) + line % per
    source_pick = jnp.where(taken == first, 1.0, 0.0).astype(jnp.bfloat16)
    target_pick = jnp.where(taken == first + per, 1.0, 0.0).astype(jnp.bfloat16)
    for at in range(rows // small):
        block = got_ref[at * large : (at + 1) * large]
        lines = slice(at * small, (at + 1) * small)
        source_ref[lines] = jnp.dot(
            source_pick, block, preferred_element_type=jnp.float32
        ).astype(jnp.bfloat16)
        target_ref[lines] = jnp.dot(target_pick, block, preferred_element_type=jnp.float32)

    chunk = 512
    hidden_size = hidden_ref.shape[1]
    source = source_ref[...]
    predict = jnp.broadcast_to(b_out_ref[...], target_ref.shape)
    for start in range(0, hidden_size, chunk):
        lanes = slice(start, start + chunk)
        pre = jnp.dot(source, w_in_ref[:, lanes], preferred_element_type=jnp.float32)
        pre = pre + b_in_ref[:, lanes]
        sigma = jax.nn.sigmoid(pre)
        hidden = (pre * sigma).astype(jnp.bfloat16)
        hidden_ref[:, lanes] = hidden
        slope_ref[:, lanes] = sigma * (1.0 + pre * (1.0 - sigma))
        predict = predict + jnp.dot(
            hidden, w_out_ref[lanes], preferred_element_type=jnp.float32
        )
    wanted = target_ref[...]
    error = jnp.where(wanted < FULL_BELOW, error_weight * (predict - wanted), 0.0)
    error = error.astype(jnp.bfloat16)
    error_ref[...] = error
    b_out_grad_ref[...] = jnp.sum(error.astype(jnp.float32), axis=0, keepdims=True)
    total = jnp.zeros(target_ref.shape, jnp.float32)
    for start in range(0, hidden_size, chunk):
        lanes = slice(start, start + chunk)
        upstream = contract_cols(error, w_out_ref[lanes])
        pre_grad = (upstream * slope_ref[:, lanes]).astype(jnp.bfloat16)
        pre_grad_ref[:, lanes] = pre_grad
        b_in_grad_ref[:, lanes] = jnp.sum(
            pre_grad.astype(jnp.float32), axis=0, keepdims=True
        )
        total = total + contract_cols(pre_grad, w_in_ref[:, lanes])
    gradient = total.astype(jnp.bfloat16)
    out = lax.broadcasted_iota(jnp.int32, (large, small), 0)
    origin = lax.broadcasted_iota(jnp.int32, (large, small), 1)
    fits = origin == out // (2 * per) * per + out % per
    side = out // per % 2
    for at in range(rows // small):
        lines = slice(at * small, (at + 1) * small)
        block = jnp.zeros((large, width), jnp.float32)
        for half in range(2):
            move = jnp.where(fits & (side == half), 1.0, 0.0).astype(jnp.bfloat16)
            block = block + jnp.dot(
                move,
                gradient[lines, half * width : (half + 1) * width],
                preferred_element_type=jnp.float32,
            )
        back_ref[at * large : (at + 1) * large] = block.astype(jnp.bfloat16)


def gather_kernel(source_pick_ref, target_pick_ref, back_ref, out_ref):
    width = back_ref.shape[1]
    for half, pick_ref in enumerate((source_pick_ref, target_pick_ref)):
        out_ref[:, half * width : (half + 1) * width] = contract_rows(
            pick_ref[...], back_ref[...]
        ).astype(jnp.bfloat16)


def part_kernel(
    keep_hbm, got_hbm, own_grad_ref, other_grad_ref, part_ref, keep_ref, got_ref, loaded
):
    loads = (
        pltpu.make_async_copy(keep_hbm, keep_ref, loaded.at[0]),
        pltpu.make_async_copy(got_hbm, got_ref, loaded.at[1]),
    )
    for load in loads:
        load.start()
    half = keep_ref.shape[0]
    width = part_ref.shape[1]
    loads[0].wait()
    total = jnp.dot(keep_ref[...], own_grad_ref[...], preferred_element_type=jnp.float32)
    loads[1].wait()
    total = total + jnp.dot(
        got_ref[...], other_grad_ref[...], preferred_element_type=jnp.float32
    )
    for side in range(EMBED // width):
        part_ref[side * half : (side + 1) * half, :] = total[
            :, side * width : (side + 1) * width
        ].astype(jnp.bfloat16)


def sum_kernel(parts_ref, copies_ref):
    total = jnp.sum(parts_ref[...].astype(jnp.float32), axis=0).astype(jnp.bfloat16)
    copies_ref[...] = jnp.broadcast_to(total[None], copies_ref.shape)


def spread_kernel(other, edge_ref, half_ref, *rest):
    out_hbm, wide_ref, done = rest[-3:]
    half, width = wide_ref.shape[0], half_ref.shape[1]
    core = 1 - edge_ref[4] if other else edge_ref[4]
    begin = core * half
    pieces = 4
    stores = []
    for piece in range(pieces):
        lines = slice(piece * half // pieces, (piece + 1) * half // pieces)
        for side in range(EMBED // width):
            lanes = slice(side * width, (side + 1) * width)
            rows = slice(side * half + lines.start, side * half + lines.stop)
            wide_ref[lines, lanes] = half_ref[rows].astype(jnp.float32)
        at = pl.multiple_of(begin + lines.start, half // pieces)
        store = pltpu.make_async_copy(
            wide_ref.at[lines], out_hbm.at[pl.ds(at, half // pieces)], done.at[piece]
        )
        store.start()
        stores.append(store)
    for store in stores:
        store.wait()


def neighbours(low_piece, high_piece, axis):
    count = lax.axis_size(axis)
    up = [(i, i + 1) for i in range(count - 1)]
    down = [(b, a) for a, b in up]
    return lax.ppermute(high_piece, axis, up), lax.ppermute(low_piece, axis, down)


def contract_rows(left, right):
    return lax.dot_general(
        left, right, (((0,), (0,)), ((), ())), preferred_element_type=jnp.float32
    )


def contract_cols(left, right):
    return lax.dot_general(
        left, right, (((1,), (1,)), ((), ())), preferred_element_type=jnp.float32
    )


def per_device(fields, patch_weight, trainer_of, lag_index, w_in, b_in, w_out, b_out):
    axes = ("gx", "gy")
    n_x, n_y = lax.axis_size("gx"), lax.axis_size("gy")
    devices = n_x * n_y
    _, wide_x, wide_y, wide_z = fields.shape
    patches = (wide_x // PATCH) * (wide_y // PATCH) * (wide_z // PATCH)
    blocks = patches // BLOCK_ROWS
    slots = max(2, 2 * blocks // devices)
    per = slots * BLOCK_ROWS
    features = FIELDS * PATCH**3

    at_x, at_y = lax.axis_index("gx"), lax.axis_index("gy")
    core = at_x % 2
    edges = jnp.stack(
        [at_x == 0, at_x == n_x - 1, at_y == 0, at_y == n_y - 1, core == 1]
    ).astype(jnp.int32)
    own_patch = jnp.repeat(trainer_of[:, 0], BLOCK_ROWS)
    lag = lag_index.reshape(-1, lag_index.shape[2]).astype(jnp.float32)

    vmem = pl.BlockSpec(memory_space=pltpu.VMEM)
    smem = pl.BlockSpec(memory_space=pltpu.SMEM)
    hbm = pl.BlockSpec(memory_space=pltpu.HBM)

    def grant(mebibytes):
        return pltpu.CompilerParams(vmem_limit_bytes=mebibytes * 1024 * 1024)

    def shape(dims, kind):
        return jax.ShapeDtypeStruct(dims, kind)

    face = shape((FIELDS, REACH, wide_y, wide_z), jnp.bfloat16)
    side = shape((FIELDS, REACH * wide_x, wide_z), jnp.bfloat16)
    x_first, x_last, y_first, y_last = pl.pallas_call(
        faces_kernel,
        out_shape=(face, face, side, side),
        in_specs=[vmem],
        out_specs=(vmem,) * 4,
        scratch_shapes=[pltpu.VMEM((wide_x * LIFT, wide_z), jnp.float32)],
        compiler_params=grant(8),
        name="faces",
    )(fields)
    xlo, xhi = neighbours(x_first, x_last, "gx")
    ylo, yhi = neighbours(y_first, y_last, "gy")
    corner_first, corner_last = pl.pallas_call(
        corners_kernel,
        out_shape=(shape((FIELDS, 2 * CORNER * CORNER, wide_z), jnp.bfloat16),) * 2,
        in_specs=[vmem] * 2,
        out_specs=(vmem,) * 2,
        scratch_shapes=[pltpu.VMEM((2 * CORNER * LIFT, wide_z), jnp.float32)],
        compiler_params=grant(8),
        name="corners",
    )(xlo, xhi)
    corner_lo, corner_hi = neighbours(corner_first, corner_last, "gy")

    send_rows = 2 * devices * per
    source_pick, target_pick, chosen = pl.pallas_call(
        functools.partial(slots_kernel, slots),
        out_shape=(
            shape((send_rows, patches), jnp.bfloat16),
            shape((send_rows, patches), jnp.bfloat16),
            shape(((wide_x // PATCH) * wide_y, wide_z), jnp.float32),
        ),
        in_specs=[vmem] * 3,
        out_specs=(vmem,) * 3,
        compiler_params=grant(8),
        name="slots",
    )(own_patch[None, :], own_patch[:, None], lag)

    full = (FIELDS, wide_x + 2 * REACH, wide_y + 2 * LIFT, wide_z)
    new_fields, keep, give, send = pl.pallas_call(
        functools.partial(window_kernel, (wide_x, wide_y, wide_z), per),
        out_shape=(
            shape(fields.shape, jnp.float32),
            shape((features // 2, patches), jnp.bfloat16),
            shape((features // 2, patches), jnp.bfloat16),
            shape((send_rows, EMBED), jnp.bfloat16),
        ),
        in_specs=[smem] + [vmem] * 10 + [hbm],
        out_specs=(hbm,) * 4,
        scratch_shapes=[
            pltpu.VMEM(full, jnp.float32),
            pltpu.VMEM(full, jnp.float32),
            pltpu.VMEM((FIELDS, wide_x, wide_y, wide_z), jnp.float32),
            pltpu.VMEM((FIELDS * PATCH, PATCH * PATCH, patches), jnp.float32),
            pltpu.VMEM((features, 2 * patches), jnp.bfloat16),
            pltpu.VMEM((features, EMBED), jnp.bfloat16),
            pltpu.VMEM((FIELDS, wide_x, wide_y, wide_z), jnp.float32),
            pltpu.VMEM((send_rows, EMBED), jnp.bfloat16),
            pltpu.SemaphoreType.DMA((8,)),
        ],
        compiler_params=grant(50),
        name="window",
    )(
        edges,
        fields,
        xlo,
        xhi,
        ylo,
        yhi,
        corner_lo,
        corner_hi,
        chosen,
        source_pick,
        target_pick,
        patch_weight,
    )

    pairs = [(i, i ^ 1) for i in range(n_x)]
    groups = [
        [x * n_y + y for x in range(n_x) for y in range(n_y) if x % 2 == c] for c in range(2)
    ]
    members = devices // 2
    got_picked = lax.ppermute(give, "gx", pairs)
    got = lax.all_to_all(send.reshape(devices, 2 * per, EMBED), axes, 0, 0, tiled=True)
    rows = devices * per
    hidden_size = w_in.shape[2]
    width = EMBED // 2
    source, hidden, error, pre_grad, b_in_grad, b_out_grad, back = pl.pallas_call(
        functools.partial(trainer_kernel, per),
        out_shape=(
            shape((rows, EMBED), jnp.bfloat16),
            shape((rows, hidden_size), jnp.bfloat16),
            shape((rows, EMBED), jnp.bfloat16),
            shape((rows, hidden_size), jnp.bfloat16),
            shape((1, hidden_size), jnp.float32),
            shape((1, EMBED), jnp.float32),
            shape((2 * rows, width), jnp.bfloat16),
        ),
        in_specs=[vmem] * 5,
        out_specs=(vmem,) * 7,
        scratch_shapes=[
            pltpu.VMEM((rows, EMBED), jnp.float32),
            pltpu.VMEM((rows, hidden_size), jnp.float32),
        ],
        compiler_params=grant(50),
        name="trainer",
    )(got.reshape(send_rows, EMBED), w_in[0], b_in, w_out[0], b_out)
    back = lax.all_to_all(back.reshape(devices, 2 * per, width), axes, 0, 0, tiled=True)
    w_in_grad = contract_rows(source, pre_grad)
    w_out_grad = contract_rows(hidden, error)
    back, w_in_grad, w_out_grad = lax.optimization_barrier((back, w_in_grad, w_out_grad))
    own_grad = pl.pallas_call(
        gather_kernel,
        out_shape=shape((patches, EMBED), jnp.bfloat16),
        in_specs=[vmem] * 3,
        out_specs=vmem,
        compiler_params=grant(8),
        name="gather",
    )(source_pick, target_pick, back.reshape(send_rows, width))
    other_grad = lax.ppermute(own_grad, "gx", pairs)
    piece = features // members
    parts = pl.pallas_call(
        part_kernel,
        out_shape=shape((features, width), jnp.bfloat16),
        in_specs=[hbm, hbm, vmem, vmem],
        out_specs=vmem,
        scratch_shapes=[
            pltpu.VMEM((features // 2, patches), jnp.bfloat16),
            pltpu.VMEM((features // 2, patches), jnp.bfloat16),
            pltpu.SemaphoreType.DMA((2,)),
        ],
        compiler_params=grant(24),
        name="part",
    )(keep, got_picked, own_grad, other_grad)
    parts = lax.all_to_all(
        parts.reshape(members, piece, width), axes, 0, 0, axis_index_groups=groups, tiled=True
    )
    copies = pl.pallas_call(
        sum_kernel,
        out_shape=jax.ShapeDtypeStruct((members, piece, width), jnp.bfloat16),
        in_specs=[vmem],
        out_specs=vmem,
        compiler_params=grant(16),
        name="total",
    )(parts)
    own_half = lax.all_to_all(copies, axes, 0, 0, axis_index_groups=groups, tiled=True)
    own_half = own_half.reshape(features, width)
    other_half = lax.ppermute(own_half, "gx", pairs)

    def spread(other, *operands):
        return pl.pallas_call(
            functools.partial(spread_kernel, other),
            out_shape=shape((features, EMBED), jnp.float32),
            in_specs=[smem, vmem] + [hbm] * (len(operands) - 2),
            out_specs=hbm,
            scratch_shapes=[
                pltpu.VMEM((features // 2, EMBED), jnp.float32),
                pltpu.SemaphoreType.DMA((4,)),
            ],
            input_output_aliases={2: 0} if other else {},
            compiler_params=grant(8),
            name="spread_other" if other else "spread_own",
        )(*operands)

    patch_gradient = spread(False, edges, own_half)
    patch_gradient = spread(True, edges, other_half, patch_gradient)
    return (
        new_fields,
        patch_gradient,
        w_in_grad[None],
        b_in_grad,
        w_out_grad[None],
        b_out_grad,
    )


def solution(mesh):
    in_specs = (
        P(None, "gx", "gy", None),
        P(),
        P(("gx", "gy"), None),
        P("gx", "gy", None),
        P(("gx", "gy"), None, None),
        P(("gx", "gy"), None),
        P(("gx", "gy"), None, None),
        P(("gx", "gy"), None),
    )
    out_specs = (
        P(None, "gx", "gy", None),
        P(),
        P(("gx", "gy"), None, None),
        P(("gx", "gy"), None),
        P(("gx", "gy"), None, None),
        P(("gx", "gy"), None),
    )
    return jax.shard_map(
        per_device, mesh=mesh, in_specs=in_specs, out_specs=out_specs, check_vma=False
    )
```

```python
import functools

import jax
import jax.numpy as jnp
from jax import lax
from jax.experimental import pallas as pl
from jax.experimental.pallas import tpu as pltpu
from jax.sharding import PartitionSpec as P

FIELDS = 5
PATCH = 8
STEPS = 3
EMBED = 512
BLOCK_ROWS = 2
REACH = 2 * STEPS
LIFT = 8
EMPTY = 1.0e30
FULL_BELOW = 1.0e29

time_step = 0.2
viscosity = 0.5
drift_x = 0.6
drift_y = -0.4
drift_z = 0.3
error_weight = 0.0625

SLOPE = {-2: 1.0 / 12.0, -1: -8.0 / 12.0, 1: 8.0 / 12.0, 2: -1.0 / 12.0}
BEND = {-2: -1.0 / 12.0, -1: 16.0 / 12.0, 1: 16.0 / 12.0, 2: -1.0 / 12.0}
OFFSETS = (-2, -1, 1, 2)


def own_weights(drift):
    return {k: time_step * (viscosity * BEND[k] - drift * SLOPE[k]) for k in OFFSETS}


OWN_X, OWN_Y, OWN_Z = own_weights(drift_x), own_weights(drift_y), own_weights(drift_z)
MIDDLE = 1.0 - time_step * viscosity * 3.0 * 30.0 / 12.0
PUSH = {k: -time_step * SLOPE[k] for k in OFFSETS}


def rolled(value, offset, axis):
    size = value.shape[axis]
    return pltpu.roll(value, (-offset) % size, axis)


def weighted(pieces, weights):
    total = None
    for k in OFFSETS:
        term = pieces[k] * weights[k]
        total = term if total is None else total + term
    return total


def slope_of(pieces):
    return (pieces[-1] - pieces[1]) * PUSH[-1] + (pieces[2] - pieces[-2]) * PUSH[2]


def one_row(src, row, own_z, push_z, begin, end):
    def along(field):
        middle = src[field, row, begin:end]
        xs = {k: src[field, row + k, begin:end] for k in OFFSETS}
        ys = {k: src[field, row, begin + k : end + k] for k in OFFSETS}
        zs = {k: rolled(middle, k, 1) for k in OFFSETS}
        total = middle * MIDDLE + weighted(xs, OWN_X) + weighted(ys, OWN_Y)
        return total + weighted(zs, own_z), xs, ys, zs

    pressure, xs, ys, zs = along(4)
    px, py, pz = slope_of(xs), slope_of(ys), weighted(zs, push_z)
    first, xs, _, _ = along(1)
    first = first + px
    spread = slope_of(xs)
    second, _, ys, _ = along(2)
    second = second + py
    spread = spread + slope_of(ys)
    third, _, _, zs = along(3)
    third = third + pz
    spread = spread + weighted(zs, push_z)
    density = along(0)[0] + spread
    return density, first, second, third, pressure + spread


def slots_kernel(slots, own_row_ref, own_col_ref, lag_ref, source_ref, target_ref, chosen_ref):
    rows, patches = source_ref.shape
    per = slots * BLOCK_ROWS
    at_r = lax.broadcasted_iota(jnp.int32, (patches, patches), 0)
    at_c = lax.broadcasted_iota(jnp.int32, (patches, patches), 1)
    earlier = (at_r // BLOCK_ROWS < at_c // BLOCK_ROWS) & (at_r % BLOCK_ROWS == 0)
    hit = (own_row_ref[...] == own_col_ref[...]) & earlier
    rank = jnp.sum(jnp.where(hit, 1.0, 0.0), axis=0, keepdims=True).astype(jnp.int32)
    place = lax.broadcasted_iota(jnp.int32, (1, patches), 1) % BLOCK_ROWS
    at = own_row_ref[...] * (2 * per) + rank * BLOCK_ROWS + place
    row = lax.broadcasted_iota(jnp.int32, (rows, patches), 0)
    source_ref[...] = jnp.where(row == at, 1.0, 0.0).astype(jnp.bfloat16)
    target_ref[...] = jnp.where(row == at + per, 1.0, 0.0).astype(jnp.bfloat16)
    tall, wide = chosen_ref.shape
    bricks, deep = lag_ref.shape
    along = lax.broadcasted_iota(jnp.int32, (deep, wide), 0)
    cells = lax.broadcasted_iota(jnp.int32, (deep, wide), 1)
    spread = jnp.where(along == cells // PATCH, 1.0, 0.0).astype(jnp.bfloat16)
    lanes = jnp.dot(
        lag_ref[...].astype(jnp.bfloat16), spread, preferred_element_type=jnp.float32
    )
    line = lax.broadcasted_iota(jnp.int32, (tall, bricks), 0)
    brick = lax.broadcasted_iota(jnp.int32, (tall, bricks), 1)
    lift = jnp.where(line // PATCH == brick, 1.0, 0.0).astype(jnp.bfloat16)
    chosen_ref[...] = jnp.dot(
        lift, lanes.astype(jnp.bfloat16), preferred_element_type=jnp.float32
    )


CORNER = 4


def y_faces_kernel(f_ref, first_ref, last_ref, lines_ref):
    wide_x, wide_y = f_ref.shape[1], f_ref.shape[2]
    for at, out_ref in ((0, first_ref), (wide_y - LIFT, last_ref)):
        for field in range(FIELDS):
            for row in range(wide_x):
                lines_ref[row * LIFT : (row + 1) * LIFT] = f_ref[field, row, at : at + LIFT]
            for layer in range(REACH):
                line = layer if at == 0 else LIFT - 1 - layer
                out_ref[field, layer * wide_x : (layer + 1) * wide_x] = lines_ref[
                    pl.ds(line, wide_x, stride=LIFT), :
                ].astype(jnp.bfloat16)


def x_faces_kernel(f_ref, ylo_ref, yhi_ref, first_ref, last_ref, lines_ref):
    wide_x, wide_y = f_ref.shape[1], f_ref.shape[2]
    tall = wide_y + 2 * CORNER
    for at, out_ref in ((0, first_ref), (wide_x - REACH, last_ref)):
        for field in range(FIELDS):
            low = ylo_ref[field].astype(jnp.float32)
            high = yhi_ref[field].astype(jnp.float32)
            for row in range(REACH):
                begin = row * tall + CORNER
                lines_ref[begin : begin + wide_y] = f_ref[field, at + row]
            for layer in range(CORNER):
                rows = slice(layer * wide_x + at, layer * wide_x + at + REACH)
                below, above = CORNER - 1 - layer, CORNER + wide_y + layer
                lines_ref[pl.ds(below, REACH, stride=tall), :] = low[rows]
                lines_ref[pl.ds(above, REACH, stride=tall), :] = high[rows]
            for row in range(REACH):
                out_ref[field, row] = lines_ref[row * tall : (row + 1) * tall].astype(
                    jnp.bfloat16
                )


def window_kernel(
    shape,
    per,
    edge_ref,
    f_ref,
    xlo_ref,
    xhi_ref,
    ylo_ref,
    yhi_ref,
    chosen_ref,
    source_pick_ref,
    target_pick_ref,
    w_hbm,
    new_hbm,
    keep_hbm,
    give_hbm,
    send_hbm,
    first_ref,
    second_ref,
    shuffle_ref,
    natural_ref,
    both_ref,
    w_ref,
    new_ref,
    send_ref,
    done,
):
    load_w = pltpu.make_async_copy(w_hbm, w_ref, done.at[0])
    load_w.start()
    wide_x, wide_y, wide_z = shape
    patches = (wide_x // PATCH) * (wide_y // PATCH) * (wide_z // PATCH)
    top_x, top_y = REACH + wide_x, LIFT + wide_y
    full_x, full_y = top_x + REACH, top_y + LIFT
    lane = lax.broadcasted_iota(jnp.int32, (1, wide_z), 1)
    inside = {k: (lane + k >= 0) & (lane + k < wide_z) for k in OFFSETS}
    own_z = {k: jnp.where(inside[k], OWN_Z[k], 0.0) for k in OFFSETS}
    push_z = {k: jnp.where(inside[k], PUSH[k], 0.0) for k in OFFSETS}

    first_ref[:, REACH:top_x, LIFT:top_y, :] = f_ref[...]
    reached = slice(LIFT - CORNER, top_y + CORNER)
    first_ref[:, 0:REACH, reached, :] = xlo_ref[...].astype(jnp.float32)
    first_ref[:, top_x:full_x, reached, :] = xhi_ref[...].astype(jnp.float32)
    for field in range(FIELDS):
        for low, face_ref in ((True, ylo_ref), (False, yhi_ref)):
            face = face_ref[field].astype(jnp.float32)
            for layer in range(REACH):
                line = LIFT - 1 - layer if low else top_y + layer
                first_ref[field, REACH:top_x, line, :] = face[
                    layer * wide_x : (layer + 1) * wide_x
                ]

    def clear(ref, least):
        @pl.when(edge_ref[0] == 1)
        def _():
            ref[:, least:REACH] = jnp.zeros((FIELDS, REACH - least, full_y, wide_z), jnp.float32)

        @pl.when(edge_ref[1] == 1)
        def _():
            ref[:, top_x : full_x - least] = jnp.zeros(
                (FIELDS, REACH - least, full_y, wide_z), jnp.float32
            )

        @pl.when(edge_ref[2] == 1)
        def _():
            ref[:, :, 0:LIFT] = jnp.zeros((FIELDS, full_x, LIFT, wide_z), jnp.float32)

        @pl.when(edge_ref[3] == 1)
        def _():
            ref[:, :, top_y:full_y] = jnp.zeros((FIELDS, full_x, LIFT, wide_z), jnp.float32)

    def step(src, dst, least):
        begin = LIFT - REACH + least
        end = begin + wide_y + LIFT

        def body(row, carry):
            done = one_row(src, row, own_z, push_z, begin, end)
            for field in range(FIELDS):
                dst[field, row, begin:end] = done[field]
            return carry

        lax.fori_loop(least, full_x - least, body, 0, unroll=4)
        clear(dst, least)

    def last_step(src):
        def body(row, carry):
            done = one_row(src, row, own_z, push_z, LIFT, top_y)
            for field in range(FIELDS):
                new_ref[field, row - REACH] = done[field]
            return carry

        lax.fori_loop(REACH, top_x, body, 0, unroll=4)

    z_count = wide_z // PATCH
    lane_r = lax.broadcasted_iota(jnp.int32, (wide_z, wide_z), 0)
    lane_c = lax.broadcasted_iota(jnp.int32, (wide_z, wide_z), 1)
    swap = jnp.where(
        (lane_r // PATCH == lane_c % z_count) & (lane_r % PATCH == lane_c // z_count), 1.0, 0.0
    ).astype(jnp.bfloat16)
    group = lax.broadcasted_iota(jnp.int32, (PATCH, wide_z), 1) // z_count

    def into_patches(load, store):
        for field in range(FIELDS):
            flat = load(field).reshape(wide_x * wide_y, wide_z)
            shuffle_ref[field] = jnp.dot(
                flat.astype(jnp.bfloat16), swap, preferred_element_type=jnp.float32
            ).reshape(wide_x, wide_y, wide_z)

        for field in range(FIELDS):
            tiles = [
                shuffle_ref[
                    field, px * PATCH : (px + 1) * PATCH, py * PATCH : (py + 1) * PATCH
                ]
                for px in range(wide_x // PATCH)
                for py in range(wide_y // PATCH)
            ]
            for bit in (4, 2, 1):
                low = ((group & bit) == 0)[None]
                fresh = list(tiles)
                for i in range(PATCH):
                    if i & bit:
                        continue
                    a, b = tiles[i], tiles[i | bit]
                    fresh[i] = jnp.where(low, a, pltpu.roll(b, bit * z_count, 2))
                    fresh[i | bit] = jnp.where(
                        low, pltpu.roll(a, wide_z - bit * z_count, 2), b
                    )
                tiles = fresh
            for inner_z in range(PATCH):
                natural_ref[
                    field * PATCH : (field + 1) * PATCH, pl.ds(inner_z, PATCH, stride=PATCH), :
                ] = tiles[inner_z]

        for field in range(FIELDS):
            block = natural_ref[field * PATCH : (field + 1) * PATCH]
            block = block.reshape(PATCH**3, patches).astype(jnp.bfloat16)
            store(field * PATCH**3, block)

    def keep_picked(at, block):
        both_ref[at : at + PATCH**3, 0:patches] = block

    def keep_target(at, block):
        both_ref[at : at + PATCH**3, patches : 2 * patches] = block

    def chosen(field):
        one = second_ref[field, REACH:top_x, LIFT:top_y]
        two = first_ref[field, REACH:top_x, LIFT:top_y]
        one = one.reshape(wide_x // PATCH, PATCH, wide_y, wide_z)
        two = two.reshape(wide_x // PATCH, PATCH, wide_y, wide_z)
        later = chosen_ref[...].reshape(wide_x // PATCH, 1, wide_y, wide_z)
        return jnp.where(later == 1.0, two, one)

    step(first_ref, second_ref, 2)
    step(second_ref, first_ref, 4)
    last_step(first_ref)
    store_new = pltpu.make_async_copy(new_ref, new_hbm, done.at[1])
    store_new.start()
    into_patches(chosen, keep_picked)
    into_patches(lambda field: new_ref[field], keep_target)

    half = both_ref.shape[0] // 2
    mine = pl.multiple_of(edge_ref[4] * half, half)
    lanes = slice(0, patches)
    store_keep = pltpu.make_async_copy(both_ref.at[pl.ds(mine, half), lanes], keep_hbm, done.at[2])
    store_give = pltpu.make_async_copy(
        both_ref.at[pl.ds(half - mine, half), lanes], give_hbm, done.at[3]
    )
    store_give.start()
    store_keep.start()
    load_w.wait()
    embedded = contract_rows(both_ref[...], w_ref[...]).astype(jnp.bfloat16)
    rows = send_ref.shape[0]
    pieces = 4
    stores = []
    for piece in range(pieces):
        lines = slice(piece * rows // pieces, (piece + 1) * rows // pieces)
        wanted = target_pick_ref[lines]
        filled = jnp.sum(wanted.astype(jnp.float32), axis=1, keepdims=True)
        line = lax.broadcasted_iota(jnp.int32, (rows // pieces, 1), 0)
        marker = jnp.where((line // per % 2 == 1) & (filled == 0.0), EMPTY, 0.0)
        placed = jnp.dot(
            source_pick_ref[lines], embedded[0:patches], preferred_element_type=jnp.float32
        )
        placed = placed + jnp.dot(
            wanted, embedded[patches : 2 * patches], preferred_element_type=jnp.float32
        )
        send_ref[lines] = (placed + marker).astype(jnp.bfloat16)
        store = pltpu.make_async_copy(send_ref.at[lines], send_hbm.at[lines], done.at[4 + piece])
        store.start()
        stores.append(store)
    for store in [store_new, store_keep, store_give] + stores:
        store.wait()


def trainer_kernel(
    per,
    got_ref,
    w_in_ref,
    b_in_ref,
    w_out_ref,
    b_out_ref,
    source_ref,
    hidden_ref,
    error_ref,
    pre_grad_ref,
    b_in_grad_ref,
    b_out_grad_ref,
    back_ref,
    target_ref,
    slope_ref,
):
    rows = source_ref.shape[0]
    width = back_ref.shape[1]
    small, large = 32 * per, 64 * per
    line = lax.broadcasted_iota(jnp.int32, (small, large), 0)
    taken = lax.broadcasted_iota(jnp.int32, (small, large), 1)
    first = line // per * (2 * per) + line % per
    source_pick = jnp.where(taken == first, 1.0, 0.0).astype(jnp.bfloat16)
    target_pick = jnp.where(taken == first + per, 1.0, 0.0).astype(jnp.bfloat16)
    for at in range(rows // small):
        block = got_ref[at * large : (at + 1) * large]
        lines = slice(at * small, (at + 1) * small)
        source_ref[lines] = jnp.dot(
            source_pick, block, preferred_element_type=jnp.float32
        ).astype(jnp.bfloat16)
        target_ref[lines] = jnp.dot(target_pick, block, preferred_element_type=jnp.float32)

    chunk = 512
    hidden_size = hidden_ref.shape[1]
    source = source_ref[...]
    predict = jnp.broadcast_to(b_out_ref[...], target_ref.shape)
    for start in range(0, hidden_size, chunk):
        lanes = slice(start, start + chunk)
        pre = jnp.dot(source, w_in_ref[:, lanes], preferred_element_type=jnp.float32)
        pre = pre + b_in_ref[:, lanes]
        sigma = jax.nn.sigmoid(pre)
        hidden = (pre * sigma).astype(jnp.bfloat16)
        hidden_ref[:, lanes] = hidden
        slope_ref[:, lanes] = sigma * (1.0 + pre * (1.0 - sigma))
        predict = predict + jnp.dot(
            hidden, w_out_ref[lanes], preferred_element_type=jnp.float32
        )
    wanted = target_ref[...]
    error = jnp.where(wanted < FULL_BELOW, error_weight * (predict - wanted), 0.0)
    error = error.astype(jnp.bfloat16)
    error_ref[...] = error
    b_out_grad_ref[...] = jnp.sum(error.astype(jnp.float32), axis=0, keepdims=True)
    total = jnp.zeros(target_ref.shape, jnp.float32)
    for start in range(0, hidden_size, chunk):
        lanes = slice(start, start + chunk)
        upstream = contract_cols(error, w_out_ref[lanes])
        pre_grad = (upstream * slope_ref[:, lanes]).astype(jnp.bfloat16)
        pre_grad_ref[:, lanes] = pre_grad
        b_in_grad_ref[:, lanes] = jnp.sum(
            pre_grad.astype(jnp.float32), axis=0, keepdims=True
        )
        total = total + contract_cols(pre_grad, w_in_ref[:, lanes])
    gradient = total.astype(jnp.bfloat16)
    out = lax.broadcasted_iota(jnp.int32, (large, small), 0)
    origin = lax.broadcasted_iota(jnp.int32, (large, small), 1)
    fits = origin == out // (2 * per) * per + out % per
    side = out // per % 2
    for at in range(rows // small):
        lines = slice(at * small, (at + 1) * small)
        block = jnp.zeros((large, width), jnp.float32)
        for half in range(2):
            move = jnp.where(fits & (side == half), 1.0, 0.0).astype(jnp.bfloat16)
            block = block + jnp.dot(
                move,
                gradient[lines, half * width : (half + 1) * width],
                preferred_element_type=jnp.float32,
            )
        back_ref[at * large : (at + 1) * large] = block.astype(jnp.bfloat16)


def gather_kernel(source_pick_ref, target_pick_ref, back_ref, out_ref):
    width = back_ref.shape[1]
    for half, pick_ref in enumerate((source_pick_ref, target_pick_ref)):
        out_ref[:, half * width : (half + 1) * width] = contract_rows(
            pick_ref[...], back_ref[...]
        ).astype(jnp.bfloat16)


def part_kernel(
    keep_hbm, got_hbm, own_grad_ref, other_grad_ref, part_ref, keep_ref, got_ref, loaded
):
    loads = (
        pltpu.make_async_copy(keep_hbm, keep_ref, loaded.at[0]),
        pltpu.make_async_copy(got_hbm, got_ref, loaded.at[1]),
    )
    for load in loads:
        load.start()
    half = keep_ref.shape[0]
    width = part_ref.shape[1]
    loads[0].wait()
    total = jnp.dot(keep_ref[...], own_grad_ref[...], preferred_element_type=jnp.float32)
    loads[1].wait()
    total = total + jnp.dot(
        got_ref[...], other_grad_ref[...], preferred_element_type=jnp.float32
    )
    for side in range(EMBED // width):
        part_ref[side * half : (side + 1) * half, :] = total[
            :, side * width : (side + 1) * width
        ].astype(jnp.bfloat16)


def sum_kernel(parts_ref, copies_ref):
    total = jnp.sum(parts_ref[...].astype(jnp.float32), axis=0).astype(jnp.bfloat16)
    copies_ref[...] = jnp.broadcast_to(total[None], copies_ref.shape)


def spread_kernel(other, edge_ref, half_ref, *rest):
    out_hbm, wide_ref, done = rest[-3:]
    half, width = wide_ref.shape[0], half_ref.shape[1]
    core = 1 - edge_ref[4] if other else edge_ref[4]
    begin = core * half
    pieces = 4
    stores = []
    for piece in range(pieces):
        lines = slice(piece * half // pieces, (piece + 1) * half // pieces)
        for side in range(EMBED // width):
            lanes = slice(side * width, (side + 1) * width)
            rows = slice(side * half + lines.start, side * half + lines.stop)
            wide_ref[lines, lanes] = half_ref[rows].astype(jnp.float32)
        at = pl.multiple_of(begin + lines.start, half // pieces)
        store = pltpu.make_async_copy(
            wide_ref.at[lines], out_hbm.at[pl.ds(at, half // pieces)], done.at[piece]
        )
        store.start()
        stores.append(store)
    for store in stores:
        store.wait()


def neighbours(low_piece, high_piece, axis):
    count = lax.axis_size(axis)
    up = [(i, i + 1) for i in range(count - 1)]
    down = [(b, a) for a, b in up]
    return lax.ppermute(high_piece, axis, up), lax.ppermute(low_piece, axis, down)


def contract_rows(left, right):
    return lax.dot_general(
        left, right, (((0,), (0,)), ((), ())), preferred_element_type=jnp.float32
    )


def contract_cols(left, right):
    return lax.dot_general(
        left, right, (((1,), (1,)), ((), ())), preferred_element_type=jnp.float32
    )


def per_device(fields, patch_weight, trainer_of, lag_index, w_in, b_in, w_out, b_out):
    axes = ("gx", "gy")
    n_x, n_y = lax.axis_size("gx"), lax.axis_size("gy")
    devices = n_x * n_y
    _, wide_x, wide_y, wide_z = fields.shape
    patches = (wide_x // PATCH) * (wide_y // PATCH) * (wide_z // PATCH)
    blocks = patches // BLOCK_ROWS
    slots = max(2, 2 * blocks // devices)
    per = slots * BLOCK_ROWS
    features = FIELDS * PATCH**3

    at_x, at_y = lax.axis_index("gx"), lax.axis_index("gy")
    core = at_x % 2
    edges = jnp.stack(
        [at_x == 0, at_x == n_x - 1, at_y == 0, at_y == n_y - 1, core == 1]
    ).astype(jnp.int32)
    own_patch = jnp.repeat(trainer_of[:, 0], BLOCK_ROWS)
    lag = lag_index.reshape(-1, lag_index.shape[2]).astype(jnp.float32)

    vmem = pl.BlockSpec(memory_space=pltpu.VMEM)
    smem = pl.BlockSpec(memory_space=pltpu.SMEM)
    hbm = pl.BlockSpec(memory_space=pltpu.HBM)

    def grant(mebibytes):
        return pltpu.CompilerParams(vmem_limit_bytes=mebibytes * 1024 * 1024)

    def shape(dims, kind):
        return jax.ShapeDtypeStruct(dims, kind)

    tall = wide_y + 2 * CORNER
    y_first, y_last = pl.pallas_call(
        y_faces_kernel,
        out_shape=(shape((FIELDS, REACH * wide_x, wide_z), jnp.bfloat16),) * 2,
        in_specs=[vmem],
        out_specs=(vmem,) * 2,
        scratch_shapes=[pltpu.VMEM((wide_x * LIFT, wide_z), jnp.float32)],
        compiler_params=grant(8),
        name="y_faces",
    )(fields)
    ylo, yhi = neighbours(y_first, y_last, "gy")
    x_first, x_last = pl.pallas_call(
        x_faces_kernel,
        out_shape=(shape((FIELDS, REACH, tall, wide_z), jnp.bfloat16),) * 2,
        in_specs=[vmem] * 3,
        out_specs=(vmem,) * 2,
        scratch_shapes=[pltpu.VMEM((REACH * tall, wide_z), jnp.float32)],
        compiler_params=grant(8),
        name="x_faces",
    )(fields, ylo, yhi)
    xlo, xhi = neighbours(x_first, x_last, "gx")

    send_rows = 2 * devices * per
    source_pick, target_pick, chosen = pl.pallas_call(
        functools.partial(slots_kernel, slots),
        out_shape=(
            shape((send_rows, patches), jnp.bfloat16),
            shape((send_rows, patches), jnp.bfloat16),
            shape(((wide_x // PATCH) * wide_y, wide_z), jnp.float32),
        ),
        in_specs=[vmem] * 3,
        out_specs=(vmem,) * 3,
        compiler_params=grant(8),
        name="slots",
    )(own_patch[None, :], own_patch[:, None], lag)

    full = (FIELDS, wide_x + 2 * REACH, wide_y + 2 * LIFT, wide_z)
    new_fields, keep, give, send = pl.pallas_call(
        functools.partial(window_kernel, (wide_x, wide_y, wide_z), per),
        out_shape=(
            shape(fields.shape, jnp.float32),
            shape((features // 2, patches), jnp.bfloat16),
            shape((features // 2, patches), jnp.bfloat16),
            shape((send_rows, EMBED), jnp.bfloat16),
        ),
        in_specs=[smem] + [vmem] * 8 + [hbm],
        out_specs=(hbm,) * 4,
        scratch_shapes=[
            pltpu.VMEM(full, jnp.float32),
            pltpu.VMEM(full, jnp.float32),
            pltpu.VMEM((FIELDS, wide_x, wide_y, wide_z), jnp.float32),
            pltpu.VMEM((FIELDS * PATCH, PATCH * PATCH, patches), jnp.float32),
            pltpu.VMEM((features, 2 * patches), jnp.bfloat16),
            pltpu.VMEM((features, EMBED), jnp.bfloat16),
            pltpu.VMEM((FIELDS, wide_x, wide_y, wide_z), jnp.float32),
            pltpu.VMEM((send_rows, EMBED), jnp.bfloat16),
            pltpu.SemaphoreType.DMA((8,)),
        ],
        compiler_params=grant(50),
        name="window",
    )(
        edges, fields, xlo, xhi, ylo, yhi, chosen, source_pick, target_pick, patch_weight
    )

    pairs = [(i, i ^ 1) for i in range(n_x)]
    groups = [
        [x * n_y + y for x in range(n_x) for y in range(n_y) if x % 2 == c] for c in range(2)
    ]
    members = devices // 2
    got_picked = lax.ppermute(give, "gx", pairs)
    got = lax.all_to_all(send.reshape(devices, 2 * per, EMBED), axes, 0, 0, tiled=True)
    rows = devices * per
    hidden_size = w_in.shape[2]
    width = EMBED // 2
    source, hidden, error, pre_grad, b_in_grad, b_out_grad, back = pl.pallas_call(
        functools.partial(trainer_kernel, per),
        out_shape=(
            shape((rows, EMBED), jnp.bfloat16),
            shape((rows, hidden_size), jnp.bfloat16),
            shape((rows, EMBED), jnp.bfloat16),
            shape((rows, hidden_size), jnp.bfloat16),
            shape((1, hidden_size), jnp.float32),
            shape((1, EMBED), jnp.float32),
            shape((2 * rows, width), jnp.bfloat16),
        ),
        in_specs=[vmem] * 5,
        out_specs=(vmem,) * 7,
        scratch_shapes=[
            pltpu.VMEM((rows, EMBED), jnp.float32),
            pltpu.VMEM((rows, hidden_size), jnp.float32),
        ],
        compiler_params=grant(50),
        name="trainer",
    )(got.reshape(send_rows, EMBED), w_in[0], b_in, w_out[0], b_out)
    back = lax.all_to_all(back.reshape(devices, 2 * per, width), axes, 0, 0, tiled=True)
    w_in_grad = contract_rows(source, pre_grad)
    w_out_grad = contract_rows(hidden, error)
    back, w_in_grad, w_out_grad = lax.optimization_barrier((back, w_in_grad, w_out_grad))
    own_grad = pl.pallas_call(
        gather_kernel,
        out_shape=shape((patches, EMBED), jnp.bfloat16),
        in_specs=[vmem] * 3,
        out_specs=vmem,
        compiler_params=grant(8),
        name="gather",
    )(source_pick, target_pick, back.reshape(send_rows, width))
    other_grad = lax.ppermute(own_grad, "gx", pairs)
    piece = features // members
    parts = pl.pallas_call(
        part_kernel,
        out_shape=shape((features, width), jnp.bfloat16),
        in_specs=[hbm, hbm, vmem, vmem],
        out_specs=vmem,
        scratch_shapes=[
            pltpu.VMEM((features // 2, patches), jnp.bfloat16),
            pltpu.VMEM((features // 2, patches), jnp.bfloat16),
            pltpu.SemaphoreType.DMA((2,)),
        ],
        compiler_params=grant(24),
        name="part",
    )(keep, got_picked, own_grad, other_grad)
    parts = lax.all_to_all(
        parts.reshape(members, piece, width), axes, 0, 0, axis_index_groups=groups, tiled=True
    )
    copies = pl.pallas_call(
        sum_kernel,
        out_shape=jax.ShapeDtypeStruct((members, piece, width), jnp.bfloat16),
        in_specs=[vmem],
        out_specs=vmem,
        compiler_params=grant(16),
        name="total",
    )(parts)
    own_half = lax.all_to_all(copies, axes, 0, 0, axis_index_groups=groups, tiled=True)
    own_half = own_half.reshape(features, width)
    other_half = lax.ppermute(own_half, "gx", pairs)

    def spread(other, *operands):
        return pl.pallas_call(
            functools.partial(spread_kernel, other),
            out_shape=shape((features, EMBED), jnp.float32),
            in_specs=[smem, vmem] + [hbm] * (len(operands) - 2),
            out_specs=hbm,
            scratch_shapes=[
                pltpu.VMEM((features // 2, EMBED), jnp.float32),
                pltpu.SemaphoreType.DMA((4,)),
            ],
            input_output_aliases={2: 0} if other else {},
            compiler_params=grant(8),
            name="spread_other" if other else "spread_own",
        )(*operands)

    patch_gradient = spread(False, edges, own_half)
    patch_gradient = spread(True, edges, other_half, patch_gradient)
    return (
        new_fields,
        patch_gradient,
        w_in_grad[None],
        b_in_grad,
        w_out_grad[None],
        b_out_grad,
    )


def solution(mesh):
    in_specs = (
        P(None, "gx", "gy", None),
        P(),
        P(("gx", "gy"), None),
        P("gx", "gy", None),
        P(("gx", "gy"), None, None),
        P(("gx", "gy"), None),
        P(("gx", "gy"), None, None),
        P(("gx", "gy"), None),
    )
    out_specs = (
        P(None, "gx", "gy", None),
        P(),
        P(("gx", "gy"), None, None),
        P(("gx", "gy"), None),
        P(("gx", "gy"), None, None),
        P(("gx", "gy"), None),
    )
    return jax.shard_map(
        per_device, mesh=mesh, in_specs=in_specs, out_specs=out_specs, check_vma=False
    )
```

```python
import functools

import jax
import jax.numpy as jnp
from jax import lax
from jax.experimental import pallas as pl
from jax.experimental.pallas import tpu as pltpu
from jax.sharding import PartitionSpec as P

FIELDS = 5
PATCH = 8
STEPS = 3
EMBED = 512
BLOCK_ROWS = 2
REACH = 2 * STEPS
LIFT = 8
EMPTY = 1.0e30
FULL_BELOW = 1.0e29

time_step = 0.2
viscosity = 0.5
drift_x = 0.6
drift_y = -0.4
drift_z = 0.3
error_weight = 0.0625

SLOPE = {-2: 1.0 / 12.0, -1: -8.0 / 12.0, 1: 8.0 / 12.0, 2: -1.0 / 12.0}
BEND = {-2: -1.0 / 12.0, -1: 16.0 / 12.0, 1: 16.0 / 12.0, 2: -1.0 / 12.0}
OFFSETS = (-2, -1, 1, 2)


def own_weights(drift):
    return {k: time_step * (viscosity * BEND[k] - drift * SLOPE[k]) for k in OFFSETS}


OWN_X, OWN_Y, OWN_Z = own_weights(drift_x), own_weights(drift_y), own_weights(drift_z)
MIDDLE = 1.0 - time_step * viscosity * 3.0 * 30.0 / 12.0
PUSH = {k: -time_step * SLOPE[k] for k in OFFSETS}


def rolled(value, offset, axis):
    size = value.shape[axis]
    return pltpu.roll(value, (-offset) % size, axis)


def weighted(pieces, weights):
    total = None
    for k in OFFSETS:
        term = pieces[k] * weights[k]
        total = term if total is None else total + term
    return total


def slope_of(pieces):
    return (pieces[-1] - pieces[1]) * PUSH[-1] + (pieces[2] - pieces[-2]) * PUSH[2]


def one_row(src, row, own_z, push_z, begin, end):
    def along(field):
        middle = src[field, row, begin:end]
        xs = {k: src[field, row + k, begin:end] for k in OFFSETS}
        ys = {k: src[field, row, begin + k : end + k] for k in OFFSETS}
        zs = {k: rolled(middle, k, 1) for k in OFFSETS}
        total = middle * MIDDLE + weighted(xs, OWN_X) + weighted(ys, OWN_Y)
        return total + weighted(zs, own_z), xs, ys, zs

    pressure, xs, ys, zs = along(4)
    px, py, pz = slope_of(xs), slope_of(ys), weighted(zs, push_z)
    first, xs, _, _ = along(1)
    first = first + px
    spread = slope_of(xs)
    second, _, ys, _ = along(2)
    second = second + py
    spread = spread + slope_of(ys)
    third, _, _, zs = along(3)
    third = third + pz
    spread = spread + weighted(zs, push_z)
    density = along(0)[0] + spread
    return density, first, second, third, pressure + spread


def slots_kernel(slots, own_row_ref, own_col_ref, lag_ref, source_ref, target_ref, chosen_ref):
    rows, patches = source_ref.shape
    per = slots * BLOCK_ROWS
    at_r = lax.broadcasted_iota(jnp.int32, (patches, patches), 0)
    at_c = lax.broadcasted_iota(jnp.int32, (patches, patches), 1)
    earlier = (at_r // BLOCK_ROWS < at_c // BLOCK_ROWS) & (at_r % BLOCK_ROWS == 0)
    hit = (own_row_ref[...] == own_col_ref[...]) & earlier
    rank = jnp.sum(jnp.where(hit, 1.0, 0.0), axis=0, keepdims=True).astype(jnp.int32)
    place = lax.broadcasted_iota(jnp.int32, (1, patches), 1) % BLOCK_ROWS
    at = own_row_ref[...] * (2 * per) + rank * BLOCK_ROWS + place
    row = lax.broadcasted_iota(jnp.int32, (rows, patches), 0)
    source_ref[...] = jnp.where(row == at, 1.0, 0.0).astype(jnp.bfloat16)
    target_ref[...] = jnp.where(row == at + per, 1.0, 0.0).astype(jnp.bfloat16)
    tall, wide = chosen_ref.shape
    bricks, deep = lag_ref.shape
    along = lax.broadcasted_iota(jnp.int32, (deep, wide), 0)
    cells = lax.broadcasted_iota(jnp.int32, (deep, wide), 1)
    spread = jnp.where(along == cells // PATCH, 1.0, 0.0).astype(jnp.bfloat16)
    lanes = jnp.dot(
        lag_ref[...].astype(jnp.bfloat16), spread, preferred_element_type=jnp.float32
    )
    line = lax.broadcasted_iota(jnp.int32, (tall, bricks), 0)
    brick = lax.broadcasted_iota(jnp.int32, (tall, bricks), 1)
    lift = jnp.where(line // PATCH == brick, 1.0, 0.0).astype(jnp.bfloat16)
    chosen_ref[...] = jnp.dot(
        lift, lanes.astype(jnp.bfloat16), preferred_element_type=jnp.float32
    )


CORNER = 4


def by_parity(parity, act, near_ref, far_ref):
    @pl.when(parity == 0)
    def _():
        act(far_ref, near_ref)

    @pl.when(parity == 1)
    def _():
        act(near_ref, far_ref)


def y_faces_kernel(edge_ref, f_ref, near_ref, far_ref, lines_ref):
    wide_x, wide_y = f_ref.shape[1], f_ref.shape[2]

    def write(first_ref, last_ref):
        for at, out_ref in ((0, first_ref), (wide_y - LIFT, last_ref)):
            for field in range(FIELDS):
                for row in range(wide_x):
                    lines_ref[row * LIFT : (row + 1) * LIFT] = f_ref[field, row, at : at + LIFT]
                for layer in range(REACH):
                    line = layer if at == 0 else LIFT - 1 - layer
                    out_ref[field, layer * wide_x : (layer + 1) * wide_x] = lines_ref[
                        pl.ds(line, wide_x, stride=LIFT), :
                    ].astype(jnp.bfloat16)

    by_parity(edge_ref[5], write, near_ref, far_ref)


def x_faces_kernel(edge_ref, f_ref, y_near_ref, y_far_ref, near_ref, far_ref, lines_ref):
    wide_x, wide_y = f_ref.shape[1], f_ref.shape[2]
    tall = wide_y + 2 * CORNER
    ends = (0, wide_x - REACH)

    def corners(ylo_ref, yhi_ref):
        for field in range(FIELDS):
            low = ylo_ref[field].astype(jnp.float32)
            high = yhi_ref[field].astype(jnp.float32)
            for end, at in enumerate(ends):
                for layer in range(CORNER):
                    rows = slice(layer * wide_x + at, layer * wide_x + at + REACH)
                    below, above = CORNER - 1 - layer, CORNER + wide_y + layer
                    lines_ref[field, end, pl.ds(below, REACH, stride=tall), :] = low[rows]
                    lines_ref[field, end, pl.ds(above, REACH, stride=tall), :] = high[rows]

    by_parity(edge_ref[5], corners, y_near_ref, y_far_ref)
    for field in range(FIELDS):
        for end, at in enumerate(ends):
            for row in range(REACH):
                begin = row * tall + CORNER
                lines_ref[field, end, begin : begin + wide_y] = f_ref[field, at + row]

    def write(first_ref, last_ref):
        for field in range(FIELDS):
            for end, out_ref in enumerate((first_ref, last_ref)):
                for row in range(REACH):
                    out_ref[field, row] = lines_ref[
                        field, end, row * tall : (row + 1) * tall
                    ].astype(jnp.bfloat16)

    by_parity(edge_ref[4], write, near_ref, far_ref)


def window_kernel(
    shape,
    per,
    edge_ref,
    f_ref,
    x_near_ref,
    x_far_ref,
    y_near_ref,
    y_far_ref,
    chosen_ref,
    source_pick_ref,
    target_pick_ref,
    w_hbm,
    new_hbm,
    keep_hbm,
    give_hbm,
    send_hbm,
    first_ref,
    second_ref,
    shuffle_ref,
    natural_ref,
    both_ref,
    w_ref,
    new_ref,
    send_ref,
    done,
):
    load_w = pltpu.make_async_copy(w_hbm, w_ref, done.at[0])
    load_w.start()
    wide_x, wide_y, wide_z = shape
    patches = (wide_x // PATCH) * (wide_y // PATCH) * (wide_z // PATCH)
    top_x, top_y = REACH + wide_x, LIFT + wide_y
    full_x, full_y = top_x + REACH, top_y + LIFT
    lane = lax.broadcasted_iota(jnp.int32, (1, wide_z), 1)
    inside = {k: (lane + k >= 0) & (lane + k < wide_z) for k in OFFSETS}
    own_z = {k: jnp.where(inside[k], OWN_Z[k], 0.0) for k in OFFSETS}
    push_z = {k: jnp.where(inside[k], PUSH[k], 0.0) for k in OFFSETS}

    first_ref[:, REACH:top_x, LIFT:top_y, :] = f_ref[...]
    reached = slice(LIFT - CORNER, top_y + CORNER)

    def beside_x(xlo_ref, xhi_ref):
        first_ref[:, 0:REACH, reached, :] = xlo_ref[...].astype(jnp.float32)
        first_ref[:, top_x:full_x, reached, :] = xhi_ref[...].astype(jnp.float32)

    def beside_y(ylo_ref, yhi_ref):
        for field in range(FIELDS):
            for low, face_ref in ((True, ylo_ref), (False, yhi_ref)):
                face = face_ref[field].astype(jnp.float32)
                for layer in range(REACH):
                    line = LIFT - 1 - layer if low else top_y + layer
                    first_ref[field, REACH:top_x, line, :] = face[
                        layer * wide_x : (layer + 1) * wide_x
                    ]

    by_parity(edge_ref[4], beside_x, x_near_ref, x_far_ref)
    by_parity(edge_ref[5], beside_y, y_near_ref, y_far_ref)

    def clear(ref, least):
        @pl.when(edge_ref[0] == 1)
        def _():
            ref[:, least:REACH] = jnp.zeros((FIELDS, REACH - least, full_y, wide_z), jnp.float32)

        @pl.when(edge_ref[1] == 1)
        def _():
            ref[:, top_x : full_x - least] = jnp.zeros(
                (FIELDS, REACH - least, full_y, wide_z), jnp.float32
            )

        @pl.when(edge_ref[2] == 1)
        def _():
            ref[:, :, 0:LIFT] = jnp.zeros((FIELDS, full_x, LIFT, wide_z), jnp.float32)

        @pl.when(edge_ref[3] == 1)
        def _():
            ref[:, :, top_y:full_y] = jnp.zeros((FIELDS, full_x, LIFT, wide_z), jnp.float32)

    def step(src, dst, least):
        begin = LIFT - REACH + least
        end = begin + wide_y + LIFT

        def body(row, carry):
            done = one_row(src, row, own_z, push_z, begin, end)
            for field in range(FIELDS):
                dst[field, row, begin:end] = done[field]
            return carry

        lax.fori_loop(least, full_x - least, body, 0, unroll=4)
        clear(dst, least)

    def last_step(src):
        def body(row, carry):
            done = one_row(src, row, own_z, push_z, LIFT, top_y)
            for field in range(FIELDS):
                new_ref[field, row - REACH] = done[field]
            return carry

        lax.fori_loop(REACH, top_x, body, 0, unroll=4)

    z_count = wide_z // PATCH
    lane_r = lax.broadcasted_iota(jnp.int32, (wide_z, wide_z), 0)
    lane_c = lax.broadcasted_iota(jnp.int32, (wide_z, wide_z), 1)
    swap = jnp.where(
        (lane_r // PATCH == lane_c % z_count) & (lane_r % PATCH == lane_c // z_count), 1.0, 0.0
    ).astype(jnp.bfloat16)
    group = lax.broadcasted_iota(jnp.int32, (PATCH, wide_z), 1) // z_count

    def into_patches(load, store):
        for field in range(FIELDS):
            flat = load(field).reshape(wide_x * wide_y, wide_z)
            shuffle_ref[field] = jnp.dot(
                flat.astype(jnp.bfloat16), swap, preferred_element_type=jnp.float32
            ).reshape(wide_x, wide_y, wide_z)

        for field in range(FIELDS):
            tiles = [
                shuffle_ref[
                    field, px * PATCH : (px + 1) * PATCH, py * PATCH : (py + 1) * PATCH
                ]
                for px in range(wide_x // PATCH)
                for py in range(wide_y // PATCH)
            ]
            for bit in (4, 2, 1):
                low = ((group & bit) == 0)[None]
                fresh = list(tiles)
                for i in range(PATCH):
                    if i & bit:
                        continue
                    a, b = tiles[i], tiles[i | bit]
                    fresh[i] = jnp.where(low, a, pltpu.roll(b, bit * z_count, 2))
                    fresh[i | bit] = jnp.where(
                        low, pltpu.roll(a, wide_z - bit * z_count, 2), b
                    )
                tiles = fresh
            for inner_z in range(PATCH):
                natural_ref[
                    field * PATCH : (field + 1) * PATCH, pl.ds(inner_z, PATCH, stride=PATCH), :
                ] = tiles[inner_z]

        for field in range(FIELDS):
            block = natural_ref[field * PATCH : (field + 1) * PATCH]
            block = block.reshape(PATCH**3, patches).astype(jnp.bfloat16)
            store(field * PATCH**3, block)

    def keep_picked(at, block):
        both_ref[at : at + PATCH**3, 0:patches] = block

    def keep_target(at, block):
        both_ref[at : at + PATCH**3, patches : 2 * patches] = block

    def chosen(field):
        one = second_ref[field, REACH:top_x, LIFT:top_y]
        two = first_ref[field, REACH:top_x, LIFT:top_y]
        one = one.reshape(wide_x // PATCH, PATCH, wide_y, wide_z)
        two = two.reshape(wide_x // PATCH, PATCH, wide_y, wide_z)
        later = chosen_ref[...].reshape(wide_x // PATCH, 1, wide_y, wide_z)
        return jnp.where(later == 1.0, two, one)

    step(first_ref, second_ref, 2)
    step(second_ref, first_ref, 4)
    last_step(first_ref)
    store_new = pltpu.make_async_copy(new_ref, new_hbm, done.at[1])
    store_new.start()
    into_patches(chosen, keep_picked)
    into_patches(lambda field: new_ref[field], keep_target)

    half = both_ref.shape[0] // 2
    mine = pl.multiple_of(edge_ref[4] * half, half)
    lanes = slice(0, patches)
    store_keep = pltpu.make_async_copy(both_ref.at[pl.ds(mine, half), lanes], keep_hbm, done.at[2])
    store_give = pltpu.make_async_copy(
        both_ref.at[pl.ds(half - mine, half), lanes], give_hbm, done.at[3]
    )
    store_give.start()
    store_keep.start()
    load_w.wait()
    embedded = contract_rows(both_ref[...], w_ref[...]).astype(jnp.bfloat16)
    rows = send_ref.shape[0]
    pieces = 4
    stores = []
    for piece in range(pieces):
        lines = slice(piece * rows // pieces, (piece + 1) * rows // pieces)
        wanted = target_pick_ref[lines]
        filled = jnp.sum(wanted.astype(jnp.float32), axis=1, keepdims=True)
        line = lax.broadcasted_iota(jnp.int32, (rows // pieces, 1), 0)
        marker = jnp.where((line // per % 2 == 1) & (filled == 0.0), EMPTY, 0.0)
        placed = jnp.dot(
            source_pick_ref[lines], embedded[0:patches], preferred_element_type=jnp.float32
        )
        placed = placed + jnp.dot(
            wanted, embedded[patches : 2 * patches], preferred_element_type=jnp.float32
        )
        send_ref[lines] = (placed + marker).astype(jnp.bfloat16)
        store = pltpu.make_async_copy(send_ref.at[lines], send_hbm.at[lines], done.at[4 + piece])
        store.start()
        stores.append(store)
    for store in [store_new, store_keep, store_give] + stores:
        store.wait()


def trainer_kernel(
    per,
    got_ref,
    w_in_ref,
    b_in_ref,
    w_out_ref,
    b_out_ref,
    source_ref,
    hidden_ref,
    error_ref,
    pre_grad_ref,
    b_in_grad_ref,
    b_out_grad_ref,
    back_ref,
    target_ref,
    slope_ref,
):
    rows = source_ref.shape[0]
    width = back_ref.shape[1]
    small, large = 32 * per, 64 * per
    line = lax.broadcasted_iota(jnp.int32, (small, large), 0)
    taken = lax.broadcasted_iota(jnp.int32, (small, large), 1)
    first = line // per * (2 * per) + line % per
    source_pick = jnp.where(taken == first, 1.0, 0.0).astype(jnp.bfloat16)
    target_pick = jnp.where(taken == first + per, 1.0, 0.0).astype(jnp.bfloat16)
    for at in range(rows // small):
        block = got_ref[at * large : (at + 1) * large]
        lines = slice(at * small, (at + 1) * small)
        source_ref[lines] = jnp.dot(
            source_pick, block, preferred_element_type=jnp.float32
        ).astype(jnp.bfloat16)
        target_ref[lines] = jnp.dot(target_pick, block, preferred_element_type=jnp.float32)

    chunk = 512
    hidden_size = hidden_ref.shape[1]
    source = source_ref[...]
    predict = jnp.broadcast_to(b_out_ref[...], target_ref.shape)
    for start in range(0, hidden_size, chunk):
        lanes = slice(start, start + chunk)
        pre = jnp.dot(source, w_in_ref[:, lanes], preferred_element_type=jnp.float32)
        pre = pre + b_in_ref[:, lanes]
        sigma = jax.nn.sigmoid(pre)
        hidden = (pre * sigma).astype(jnp.bfloat16)
        hidden_ref[:, lanes] = hidden
        slope_ref[:, lanes] = sigma * (1.0 + pre * (1.0 - sigma))
        predict = predict + jnp.dot(
            hidden, w_out_ref[lanes], preferred_element_type=jnp.float32
        )
    wanted = target_ref[...]
    error = jnp.where(wanted < FULL_BELOW, error_weight * (predict - wanted), 0.0)
    error = error.astype(jnp.bfloat16)
    error_ref[...] = error
    b_out_grad_ref[...] = jnp.sum(error.astype(jnp.float32), axis=0, keepdims=True)
    total = jnp.zeros(target_ref.shape, jnp.float32)
    for start in range(0, hidden_size, chunk):
        lanes = slice(start, start + chunk)
        upstream = contract_cols(error, w_out_ref[lanes])
        pre_grad = (upstream * slope_ref[:, lanes]).astype(jnp.bfloat16)
        pre_grad_ref[:, lanes] = pre_grad
        b_in_grad_ref[:, lanes] = jnp.sum(
            pre_grad.astype(jnp.float32), axis=0, keepdims=True
        )
        total = total + contract_cols(pre_grad, w_in_ref[:, lanes])
    gradient = total.astype(jnp.bfloat16)
    out = lax.broadcasted_iota(jnp.int32, (large, small), 0)
    origin = lax.broadcasted_iota(jnp.int32, (large, small), 1)
    fits = origin == out // (2 * per) * per + out % per
    side = out // per % 2
    for at in range(rows // small):
        lines = slice(at * small, (at + 1) * small)
        block = jnp.zeros((large, width), jnp.float32)
        for half in range(2):
            move = jnp.where(fits & (side == half), 1.0, 0.0).astype(jnp.bfloat16)
            block = block + jnp.dot(
                move,
                gradient[lines, half * width : (half + 1) * width],
                preferred_element_type=jnp.float32,
            )
        back_ref[at * large : (at + 1) * large] = block.astype(jnp.bfloat16)


def gather_kernel(source_pick_ref, target_pick_ref, back_ref, out_ref):
    width = back_ref.shape[1]
    for half, pick_ref in enumerate((source_pick_ref, target_pick_ref)):
        out_ref[:, half * width : (half + 1) * width] = contract_rows(
            pick_ref[...], back_ref[...]
        ).astype(jnp.bfloat16)


def part_kernel(
    keep_hbm, got_hbm, own_grad_ref, other_grad_ref, part_ref, keep_ref, got_ref, loaded
):
    loads = (
        pltpu.make_async_copy(keep_hbm, keep_ref, loaded.at[0]),
        pltpu.make_async_copy(got_hbm, got_ref, loaded.at[1]),
    )
    for load in loads:
        load.start()
    half = keep_ref.shape[0]
    width = part_ref.shape[1]
    loads[0].wait()
    total = jnp.dot(keep_ref[...], own_grad_ref[...], preferred_element_type=jnp.float32)
    loads[1].wait()
    total = total + jnp.dot(
        got_ref[...], other_grad_ref[...], preferred_element_type=jnp.float32
    )
    for side in range(EMBED // width):
        part_ref[side * half : (side + 1) * half, :] = total[
            :, side * width : (side + 1) * width
        ].astype(jnp.bfloat16)


def sum_kernel(parts_ref, copies_ref):
    total = jnp.sum(parts_ref[...].astype(jnp.float32), axis=0).astype(jnp.bfloat16)
    copies_ref[...] = jnp.broadcast_to(total[None], copies_ref.shape)


def spread_kernel(other, edge_ref, half_ref, *rest):
    out_hbm, wide_ref, done = rest[-3:]
    half, width = wide_ref.shape[0], half_ref.shape[1]
    core = 1 - edge_ref[4] if other else edge_ref[4]
    begin = core * half
    pieces = 4
    stores = []
    for piece in range(pieces):
        lines = slice(piece * half // pieces, (piece + 1) * half // pieces)
        for side in range(EMBED // width):
            lanes = slice(side * width, (side + 1) * width)
            rows = slice(side * half + lines.start, side * half + lines.stop)
            wide_ref[lines, lanes] = half_ref[rows].astype(jnp.float32)
        at = pl.multiple_of(begin + lines.start, half // pieces)
        store = pltpu.make_async_copy(
            wide_ref.at[lines], out_hbm.at[pl.ds(at, half // pieces)], done.at[piece]
        )
        store.start()
        stores.append(store)
    for store in stores:
        store.wait()


def swapped(near_piece, far_piece, axis):
    count = lax.axis_size(axis)
    near = [(i, i ^ 1) for i in range(count)]
    far = [pair for i in range(1, count - 1, 2) for pair in ((i, i + 1), (i + 1, i))]
    return lax.ppermute(near_piece, axis, near), lax.ppermute(far_piece, axis, far)


def contract_rows(left, right):
    return lax.dot_general(
        left, right, (((0,), (0,)), ((), ())), preferred_element_type=jnp.float32
    )


def contract_cols(left, right):
    return lax.dot_general(
        left, right, (((1,), (1,)), ((), ())), preferred_element_type=jnp.float32
    )


def per_device(fields, patch_weight, trainer_of, lag_index, w_in, b_in, w_out, b_out):
    axes = ("gx", "gy")
    n_x, n_y = lax.axis_size("gx"), lax.axis_size("gy")
    devices = n_x * n_y
    _, wide_x, wide_y, wide_z = fields.shape
    patches = (wide_x // PATCH) * (wide_y // PATCH) * (wide_z // PATCH)
    blocks = patches // BLOCK_ROWS
    slots = max(2, 2 * blocks // devices)
    per = slots * BLOCK_ROWS
    features = FIELDS * PATCH**3

    at_x, at_y = lax.axis_index("gx"), lax.axis_index("gy")
    edges = jnp.stack(
        [
            at_x == 0,
            at_x == n_x - 1,
            at_y == 0,
            at_y == n_y - 1,
            at_x % 2 == 1,
            at_y % 2 == 1,
        ]
    ).astype(jnp.int32)
    own_patch = jnp.repeat(trainer_of[:, 0], BLOCK_ROWS)
    lag = lag_index.reshape(-1, lag_index.shape[2]).astype(jnp.float32)

    vmem = pl.BlockSpec(memory_space=pltpu.VMEM)
    smem = pl.BlockSpec(memory_space=pltpu.SMEM)
    hbm = pl.BlockSpec(memory_space=pltpu.HBM)

    def grant(mebibytes):
        return pltpu.CompilerParams(vmem_limit_bytes=mebibytes * 1024 * 1024)

    def shape(dims, kind):
        return jax.ShapeDtypeStruct(dims, kind)

    tall = wide_y + 2 * CORNER
    y_near, y_far = pl.pallas_call(
        y_faces_kernel,
        out_shape=(shape((FIELDS, REACH * wide_x, wide_z), jnp.bfloat16),) * 2,
        in_specs=[smem, vmem],
        out_specs=(vmem,) * 2,
        scratch_shapes=[pltpu.VMEM((wide_x * LIFT, wide_z), jnp.float32)],
        compiler_params=grant(8),
        name="y_faces",
    )(edges, fields)
    y_near, y_far = swapped(y_near, y_far, "gy")
    x_near, x_far = pl.pallas_call(
        x_faces_kernel,
        out_shape=(shape((FIELDS, REACH, tall, wide_z), jnp.bfloat16),) * 2,
        in_specs=[smem] + [vmem] * 3,
        out_specs=(vmem,) * 2,
        scratch_shapes=[pltpu.VMEM((FIELDS, 2, REACH * tall, wide_z), jnp.float32)],
        compiler_params=grant(8),
        name="x_faces",
    )(edges, fields, y_near, y_far)
    x_near, x_far = swapped(x_near, x_far, "gx")

    send_rows = 2 * devices * per
    source_pick, target_pick, chosen = pl.pallas_call(
        functools.partial(slots_kernel, slots),
        out_shape=(
            shape((send_rows, patches), jnp.bfloat16),
            shape((send_rows, patches), jnp.bfloat16),
            shape(((wide_x // PATCH) * wide_y, wide_z), jnp.float32),
        ),
        in_specs=[vmem] * 3,
        out_specs=(vmem,) * 3,
        compiler_params=grant(8),
        name="slots",
    )(own_patch[None, :], own_patch[:, None], lag)

    full = (FIELDS, wide_x + 2 * REACH, wide_y + 2 * LIFT, wide_z)
    new_fields, keep, give, send = pl.pallas_call(
        functools.partial(window_kernel, (wide_x, wide_y, wide_z), per),
        out_shape=(
            shape(fields.shape, jnp.float32),
            shape((features // 2, patches), jnp.bfloat16),
            shape((features // 2, patches), jnp.bfloat16),
            shape((send_rows, EMBED), jnp.bfloat16),
        ),
        in_specs=[smem] + [vmem] * 8 + [hbm],
        out_specs=(hbm,) * 4,
        scratch_shapes=[
            pltpu.VMEM(full, jnp.float32),
            pltpu.VMEM(full, jnp.float32),
            pltpu.VMEM((FIELDS, wide_x, wide_y, wide_z), jnp.float32),
            pltpu.VMEM((FIELDS * PATCH, PATCH * PATCH, patches), jnp.float32),
            pltpu.VMEM((features, 2 * patches), jnp.bfloat16),
            pltpu.VMEM((features, EMBED), jnp.bfloat16),
            pltpu.VMEM((FIELDS, wide_x, wide_y, wide_z), jnp.float32),
            pltpu.VMEM((send_rows, EMBED), jnp.bfloat16),
            pltpu.SemaphoreType.DMA((8,)),
        ],
        compiler_params=grant(50),
        name="window",
    )(
        edges,
        fields,
        x_near,
        x_far,
        y_near,
        y_far,
        chosen,
        source_pick,
        target_pick,
        patch_weight,
    )

    pairs = [(i, i ^ 1) for i in range(n_x)]
    groups = [
        [x * n_y + y for x in range(n_x) for y in range(n_y) if x % 2 == c] for c in range(2)
    ]
    members = devices // 2
    got_picked = lax.ppermute(give, "gx", pairs)
    got = lax.all_to_all(send.reshape(devices, 2 * per, EMBED), axes, 0, 0, tiled=True)
    rows = devices * per
    hidden_size = w_in.shape[2]
    width = EMBED // 2
    source, hidden, error, pre_grad, b_in_grad, b_out_grad, back = pl.pallas_call(
        functools.partial(trainer_kernel, per),
        out_shape=(
            shape((rows, EMBED), jnp.bfloat16),
            shape((rows, hidden_size), jnp.bfloat16),
            shape((rows, EMBED), jnp.bfloat16),
            shape((rows, hidden_size), jnp.bfloat16),
            shape((1, hidden_size), jnp.float32),
            shape((1, EMBED), jnp.float32),
            shape((2 * rows, width), jnp.bfloat16),
        ),
        in_specs=[vmem] * 5,
        out_specs=(vmem,) * 7,
        scratch_shapes=[
            pltpu.VMEM((rows, EMBED), jnp.float32),
            pltpu.VMEM((rows, hidden_size), jnp.float32),
        ],
        compiler_params=grant(50),
        name="trainer",
    )(got.reshape(send_rows, EMBED), w_in[0], b_in, w_out[0], b_out)
    back = lax.all_to_all(back.reshape(devices, 2 * per, width), axes, 0, 0, tiled=True)
    w_in_grad = contract_rows(source, pre_grad)
    w_out_grad = contract_rows(hidden, error)
    back, w_in_grad, w_out_grad = lax.optimization_barrier((back, w_in_grad, w_out_grad))
    own_grad = pl.pallas_call(
        gather_kernel,
        out_shape=shape((patches, EMBED), jnp.bfloat16),
        in_specs=[vmem] * 3,
        out_specs=vmem,
        compiler_params=grant(8),
        name="gather",
    )(source_pick, target_pick, back.reshape(send_rows, width))
    other_grad = lax.ppermute(own_grad, "gx", pairs)
    piece = features // members
    parts = pl.pallas_call(
        part_kernel,
        out_shape=shape((features, width), jnp.bfloat16),
        in_specs=[hbm, hbm, vmem, vmem],
        out_specs=vmem,
        scratch_shapes=[
            pltpu.VMEM((features // 2, patches), jnp.bfloat16),
            pltpu.VMEM((features // 2, patches), jnp.bfloat16),
            pltpu.SemaphoreType.DMA((2,)),
        ],
        compiler_params=grant(24),
        name="part",
    )(keep, got_picked, own_grad, other_grad)
    parts = lax.all_to_all(
        parts.reshape(members, piece, width), axes, 0, 0, axis_index_groups=groups, tiled=True
    )
    copies = pl.pallas_call(
        sum_kernel,
        out_shape=jax.ShapeDtypeStruct((members, piece, width), jnp.bfloat16),
        in_specs=[vmem],
        out_specs=vmem,
        compiler_params=grant(16),
        name="total",
    )(parts)
    own_half = lax.all_to_all(copies, axes, 0, 0, axis_index_groups=groups, tiled=True)
    own_half = own_half.reshape(features, width)
    other_half = lax.ppermute(own_half, "gx", pairs)

    def spread(other, *operands):
        return pl.pallas_call(
            functools.partial(spread_kernel, other),
            out_shape=shape((features, EMBED), jnp.float32),
            in_specs=[smem, vmem] + [hbm] * (len(operands) - 2),
            out_specs=hbm,
            scratch_shapes=[
                pltpu.VMEM((features // 2, EMBED), jnp.float32),
                pltpu.SemaphoreType.DMA((4,)),
            ],
            input_output_aliases={2: 0} if other else {},
            compiler_params=grant(8),
            name="spread_other" if other else "spread_own",
        )(*operands)

    patch_gradient = spread(False, edges, own_half)
    patch_gradient = spread(True, edges, other_half, patch_gradient)
    return (
        new_fields,
        patch_gradient,
        w_in_grad[None],
        b_in_grad,
        w_out_grad[None],
        b_out_grad,
    )


def solution(mesh):
    in_specs = (
        P(None, "gx", "gy", None),
        P(),
        P(("gx", "gy"), None),
        P("gx", "gy", None),
        P(("gx", "gy"), None, None),
        P(("gx", "gy"), None),
        P(("gx", "gy"), None, None),
        P(("gx", "gy"), None),
    )
    out_specs = (
        P(None, "gx", "gy", None),
        P(),
        P(("gx", "gy"), None, None),
        P(("gx", "gy"), None),
        P(("gx", "gy"), None, None),
        P(("gx", "gy"), None),
    )
    return jax.shard_map(
        per_device, mesh=mesh, in_specs=in_specs, out_specs=out_specs, check_vma=False
    )
```

```python
import functools

import jax
import jax.numpy as jnp
from jax import lax
from jax.experimental import pallas as pl
from jax.experimental.pallas import tpu as pltpu
from jax.sharding import PartitionSpec as P

FIELDS = 5
PATCH = 8
STEPS = 3
EMBED = 512
BLOCK_ROWS = 2
REACH = 2 * STEPS
LIFT = 8
EMPTY = 1.0e30
FULL_BELOW = 1.0e29

time_step = 0.2
viscosity = 0.5
drift_x = 0.6
drift_y = -0.4
drift_z = 0.3
error_weight = 0.0625

SLOPE = {-2: 1.0 / 12.0, -1: -8.0 / 12.0, 1: 8.0 / 12.0, 2: -1.0 / 12.0}
BEND = {-2: -1.0 / 12.0, -1: 16.0 / 12.0, 1: 16.0 / 12.0, 2: -1.0 / 12.0}
OFFSETS = (-2, -1, 1, 2)


def own_weights(drift):
    return {k: time_step * (viscosity * BEND[k] - drift * SLOPE[k]) for k in OFFSETS}


OWN_X, OWN_Y, OWN_Z = own_weights(drift_x), own_weights(drift_y), own_weights(drift_z)
MIDDLE = 1.0 - time_step * viscosity * 3.0 * 30.0 / 12.0
PUSH = {k: -time_step * SLOPE[k] for k in OFFSETS}


def rolled(value, offset, axis):
    size = value.shape[axis]
    return pltpu.roll(value, (-offset) % size, axis)


def weighted(pieces, weights):
    total = None
    for k in OFFSETS:
        term = pieces[k] * weights[k]
        total = term if total is None else total + term
    return total


def slope_of(pieces):
    return (pieces[-1] - pieces[1]) * PUSH[-1] + (pieces[2] - pieces[-2]) * PUSH[2]


def one_row(src, row, own_z, push_z, begin, end):
    def along(field):
        middle = src[field, row, begin:end]
        xs = {k: src[field, row + k, begin:end] for k in OFFSETS}
        ys = {k: src[field, row, begin + k : end + k] for k in OFFSETS}
        zs = {k: rolled(middle, k, 1) for k in OFFSETS}
        total = middle * MIDDLE + weighted(xs, OWN_X) + weighted(ys, OWN_Y)
        return total + weighted(zs, own_z), xs, ys, zs

    pressure, xs, ys, zs = along(4)
    px, py, pz = slope_of(xs), slope_of(ys), weighted(zs, push_z)
    first, xs, _, _ = along(1)
    first = first + px
    spread = slope_of(xs)
    second, _, ys, _ = along(2)
    second = second + py
    spread = spread + slope_of(ys)
    third, _, _, zs = along(3)
    third = third + pz
    spread = spread + weighted(zs, push_z)
    density = along(0)[0] + spread
    return density, first, second, third, pressure + spread


def slots_kernel(slots, own_row_ref, own_col_ref, lag_ref, source_ref, target_ref, chosen_ref):
    rows, patches = source_ref.shape
    per = slots * BLOCK_ROWS
    at_r = lax.broadcasted_iota(jnp.int32, (patches, patches), 0)
    at_c = lax.broadcasted_iota(jnp.int32, (patches, patches), 1)
    earlier = (at_r // BLOCK_ROWS < at_c // BLOCK_ROWS) & (at_r % BLOCK_ROWS == 0)
    hit = (own_row_ref[...] == own_col_ref[...]) & earlier
    rank = jnp.sum(jnp.where(hit, 1.0, 0.0), axis=0, keepdims=True).astype(jnp.int32)
    place = lax.broadcasted_iota(jnp.int32, (1, patches), 1) % BLOCK_ROWS
    at = own_row_ref[...] * (2 * per) + rank * BLOCK_ROWS + place
    row = lax.broadcasted_iota(jnp.int32, (rows, patches), 0)
    source_ref[...] = jnp.where(row == at, 1.0, 0.0).astype(jnp.bfloat16)
    target_ref[...] = jnp.where(row == at + per, 1.0, 0.0).astype(jnp.bfloat16)
    tall, wide = chosen_ref.shape
    bricks, deep = lag_ref.shape
    along = lax.broadcasted_iota(jnp.int32, (deep, wide), 0)
    cells = lax.broadcasted_iota(jnp.int32, (deep, wide), 1)
    spread = jnp.where(along == cells // PATCH, 1.0, 0.0).astype(jnp.bfloat16)
    lanes = jnp.dot(
        lag_ref[...].astype(jnp.bfloat16), spread, preferred_element_type=jnp.float32
    )
    line = lax.broadcasted_iota(jnp.int32, (tall, bricks), 0)
    brick = lax.broadcasted_iota(jnp.int32, (tall, bricks), 1)
    lift = jnp.where(line // PATCH == brick, 1.0, 0.0).astype(jnp.bfloat16)
    chosen_ref[...] = jnp.dot(
        lift, lanes.astype(jnp.bfloat16), preferred_element_type=jnp.float32
    )


CORNER = 4


def by_parity(parity, act, near_ref, far_ref):
    @pl.when(parity == 0)
    def _():
        act(far_ref, near_ref)

    @pl.when(parity == 1)
    def _():
        act(near_ref, far_ref)


def y_faces_kernel(edge_ref, f_hbm, near_ref, far_ref, tiles_ref, loaded):
    wide_x, wide_y = f_hbm.shape[1], f_hbm.shape[2]
    loads = []
    for end, at in enumerate((0, wide_y - LIFT)):
        load = pltpu.make_async_copy(
            f_hbm.at[:, :, at : at + LIFT, :], tiles_ref.at[end], loaded.at[end]
        )
        load.start()
        loads.append(load)
    for load in loads:
        load.wait()

    def write(first_ref, last_ref):
        for end, out_ref in enumerate((first_ref, last_ref)):
            for field in range(FIELDS):
                for layer in range(REACH):
                    line = layer if end == 0 else LIFT - 1 - layer
                    out_ref[field, layer * wide_x : (layer + 1) * wide_x] = tiles_ref[
                        end, field, :, line, :
                    ].astype(jnp.bfloat16)

    by_parity(edge_ref[5], write, near_ref, far_ref)


def x_faces_kernel(edge_ref, f_ref, y_near_ref, y_far_ref, near_ref, far_ref, lines_ref):
    wide_x, wide_y = f_ref.shape[1], f_ref.shape[2]
    tall = wide_y + 2 * CORNER
    ends = (0, wide_x - REACH)

    def corners(ylo_ref, yhi_ref):
        for field in range(FIELDS):
            low = ylo_ref[field].astype(jnp.float32)
            high = yhi_ref[field].astype(jnp.float32)
            for end, at in enumerate(ends):
                for layer in range(CORNER):
                    rows = slice(layer * wide_x + at, layer * wide_x + at + REACH)
                    below, above = CORNER - 1 - layer, CORNER + wide_y + layer
                    lines_ref[field, end, pl.ds(below, REACH, stride=tall), :] = low[rows]
                    lines_ref[field, end, pl.ds(above, REACH, stride=tall), :] = high[rows]

    by_parity(edge_ref[5], corners, y_near_ref, y_far_ref)
    for field in range(FIELDS):
        for end, at in enumerate(ends):
            for row in range(REACH):
                begin = row * tall + CORNER
                lines_ref[field, end, begin : begin + wide_y] = f_ref[field, at + row]

    def write(first_ref, last_ref):
        for field in range(FIELDS):
            for end, out_ref in enumerate((first_ref, last_ref)):
                for row in range(REACH):
                    out_ref[field, row] = lines_ref[
                        field, end, row * tall : (row + 1) * tall
                    ].astype(jnp.bfloat16)

    by_parity(edge_ref[4], write, near_ref, far_ref)


def window_kernel(
    shape,
    per,
    edge_ref,
    f_ref,
    x_near_ref,
    x_far_ref,
    y_near_ref,
    y_far_ref,
    chosen_ref,
    source_pick_ref,
    target_pick_ref,
    w_hbm,
    new_hbm,
    keep_hbm,
    give_hbm,
    send_hbm,
    first_ref,
    second_ref,
    shuffle_ref,
    natural_ref,
    both_ref,
    w_ref,
    new_ref,
    send_ref,
    done,
):
    load_w = pltpu.make_async_copy(w_hbm, w_ref, done.at[0])
    load_w.start()
    wide_x, wide_y, wide_z = shape
    patches = (wide_x // PATCH) * (wide_y // PATCH) * (wide_z // PATCH)
    top_x, top_y = REACH + wide_x, LIFT + wide_y
    full_x, full_y = top_x + REACH, top_y + LIFT
    lane = lax.broadcasted_iota(jnp.int32, (1, wide_z), 1)
    inside = {k: (lane + k >= 0) & (lane + k < wide_z) for k in OFFSETS}
    own_z = {k: jnp.where(inside[k], OWN_Z[k], 0.0) for k in OFFSETS}
    push_z = {k: jnp.where(inside[k], PUSH[k], 0.0) for k in OFFSETS}

    first_ref[:, REACH:top_x, LIFT:top_y, :] = f_ref[...]
    reached = slice(LIFT - CORNER, top_y + CORNER)

    def beside_x(xlo_ref, xhi_ref):
        first_ref[:, 0:REACH, reached, :] = xlo_ref[...].astype(jnp.float32)
        first_ref[:, top_x:full_x, reached, :] = xhi_ref[...].astype(jnp.float32)

    def beside_y(ylo_ref, yhi_ref):
        for field in range(FIELDS):
            for low, face_ref in ((True, ylo_ref), (False, yhi_ref)):
                face = face_ref[field].astype(jnp.float32)
                for layer in range(REACH):
                    line = LIFT - 1 - layer if low else top_y + layer
                    first_ref[field, REACH:top_x, line, :] = face[
                        layer * wide_x : (layer + 1) * wide_x
                    ]

    by_parity(edge_ref[4], beside_x, x_near_ref, x_far_ref)
    by_parity(edge_ref[5], beside_y, y_near_ref, y_far_ref)

    def clear(ref, least):
        @pl.when(edge_ref[0] == 1)
        def _():
            ref[:, least:REACH] = jnp.zeros((FIELDS, REACH - least, full_y, wide_z), jnp.float32)

        @pl.when(edge_ref[1] == 1)
        def _():
            ref[:, top_x : full_x - least] = jnp.zeros(
                (FIELDS, REACH - least, full_y, wide_z), jnp.float32
            )

        @pl.when(edge_ref[2] == 1)
        def _():
            ref[:, :, 0:LIFT] = jnp.zeros((FIELDS, full_x, LIFT, wide_z), jnp.float32)

        @pl.when(edge_ref[3] == 1)
        def _():
            ref[:, :, top_y:full_y] = jnp.zeros((FIELDS, full_x, LIFT, wide_z), jnp.float32)

    def step(src, dst, least):
        begin = LIFT - REACH + least
        end = begin + wide_y + LIFT

        def body(row, carry):
            done = one_row(src, row, own_z, push_z, begin, end)
            for field in range(FIELDS):
                dst[field, row, begin:end] = done[field]
            return carry

        lax.fori_loop(least, full_x - least, body, 0, unroll=4)
        clear(dst, least)

    def last_step(src):
        def body(row, carry):
            done = one_row(src, row, own_z, push_z, LIFT, top_y)
            for field in range(FIELDS):
                new_ref[field, row - REACH] = done[field]
            return carry

        lax.fori_loop(REACH, top_x, body, 0, unroll=4)

    z_count = wide_z // PATCH
    lane_r = lax.broadcasted_iota(jnp.int32, (wide_z, wide_z), 0)
    lane_c = lax.broadcasted_iota(jnp.int32, (wide_z, wide_z), 1)
    swap = jnp.where(
        (lane_r // PATCH == lane_c % z_count) & (lane_r % PATCH == lane_c // z_count), 1.0, 0.0
    ).astype(jnp.bfloat16)
    group = lax.broadcasted_iota(jnp.int32, (PATCH, wide_z), 1) // z_count

    def into_patches(load, store):
        for field in range(FIELDS):
            flat = load(field).reshape(wide_x * wide_y, wide_z)
            shuffle_ref[field] = jnp.dot(
                flat.astype(jnp.bfloat16), swap, preferred_element_type=jnp.float32
            ).reshape(wide_x, wide_y, wide_z)

        for field in range(FIELDS):
            tiles = [
                shuffle_ref[
                    field, px * PATCH : (px + 1) * PATCH, py * PATCH : (py + 1) * PATCH
                ]
                for px in range(wide_x // PATCH)
                for py in range(wide_y // PATCH)
            ]
            for bit in (4, 2, 1):
                low = ((group & bit) == 0)[None]
                fresh = list(tiles)
                for i in range(PATCH):
                    if i & bit:
                        continue
                    a, b = tiles[i], tiles[i | bit]
                    fresh[i] = jnp.where(low, a, pltpu.roll(b, bit * z_count, 2))
                    fresh[i | bit] = jnp.where(
                        low, pltpu.roll(a, wide_z - bit * z_count, 2), b
                    )
                tiles = fresh
            for inner_z in range(PATCH):
                natural_ref[
                    field * PATCH : (field + 1) * PATCH, pl.ds(inner_z, PATCH, stride=PATCH), :
                ] = tiles[inner_z]

        for field in range(FIELDS):
            block = natural_ref[field * PATCH : (field + 1) * PATCH]
            block = block.reshape(PATCH**3, patches).astype(jnp.bfloat16)
            store(field * PATCH**3, block)

    def keep_picked(at, block):
        both_ref[at : at + PATCH**3, 0:patches] = block

    def keep_target(at, block):
        both_ref[at : at + PATCH**3, patches : 2 * patches] = block

    def chosen(field):
        one = second_ref[field, REACH:top_x, LIFT:top_y]
        two = first_ref[field, REACH:top_x, LIFT:top_y]
        one = one.reshape(wide_x // PATCH, PATCH, wide_y, wide_z)
        two = two.reshape(wide_x // PATCH, PATCH, wide_y, wide_z)
        later = chosen_ref[...].reshape(wide_x // PATCH, 1, wide_y, wide_z)
        return jnp.where(later == 1.0, two, one)

    step(first_ref, second_ref, 2)
    step(second_ref, first_ref, 4)
    last_step(first_ref)
    store_new = pltpu.make_async_copy(new_ref, new_hbm, done.at[1])
    store_new.start()
    into_patches(chosen, keep_picked)
    into_patches(lambda field: new_ref[field], keep_target)

    half = both_ref.shape[0] // 2
    mine = pl.multiple_of(edge_ref[4] * half, half)
    lanes = slice(0, patches)
    store_keep = pltpu.make_async_copy(both_ref.at[pl.ds(mine, half), lanes], keep_hbm, done.at[2])
    store_give = pltpu.make_async_copy(
        both_ref.at[pl.ds(half - mine, half), lanes], give_hbm, done.at[3]
    )
    store_give.start()
    store_keep.start()
    load_w.wait()
    embedded = contract_rows(both_ref[...], w_ref[...]).astype(jnp.bfloat16)
    rows = send_ref.shape[0]
    pieces = 4
    stores = []
    for piece in range(pieces):
        lines = slice(piece * rows // pieces, (piece + 1) * rows // pieces)
        wanted = target_pick_ref[lines]
        filled = jnp.sum(wanted.astype(jnp.float32), axis=1, keepdims=True)
        line = lax.broadcasted_iota(jnp.int32, (rows // pieces, 1), 0)
        marker = jnp.where((line // per % 2 == 1) & (filled == 0.0), EMPTY, 0.0)
        placed = jnp.dot(
            source_pick_ref[lines], embedded[0:patches], preferred_element_type=jnp.float32
        )
        placed = placed + jnp.dot(
            wanted, embedded[patches : 2 * patches], preferred_element_type=jnp.float32
        )
        send_ref[lines] = (placed + marker).astype(jnp.bfloat16)
        store = pltpu.make_async_copy(send_ref.at[lines], send_hbm.at[lines], done.at[4 + piece])
        store.start()
        stores.append(store)
    for store in [store_new, store_keep, store_give] + stores:
        store.wait()


def trainer_kernel(
    per,
    got_ref,
    w_in_ref,
    b_in_ref,
    w_out_ref,
    b_out_ref,
    source_ref,
    hidden_ref,
    error_ref,
    pre_grad_ref,
    b_in_grad_ref,
    b_out_grad_ref,
    back_ref,
    target_ref,
    slope_ref,
):
    rows = source_ref.shape[0]
    width = back_ref.shape[1]
    small, large = 32 * per, 64 * per
    line = lax.broadcasted_iota(jnp.int32, (small, large), 0)
    taken = lax.broadcasted_iota(jnp.int32, (small, large), 1)
    first = line // per * (2 * per) + line % per
    source_pick = jnp.where(taken == first, 1.0, 0.0).astype(jnp.bfloat16)
    target_pick = jnp.where(taken == first + per, 1.0, 0.0).astype(jnp.bfloat16)
    for at in range(rows // small):
        block = got_ref[at * large : (at + 1) * large]
        lines = slice(at * small, (at + 1) * small)
        source_ref[lines] = jnp.dot(
            source_pick, block, preferred_element_type=jnp.float32
        ).astype(jnp.bfloat16)
        target_ref[lines] = jnp.dot(target_pick, block, preferred_element_type=jnp.float32)

    chunk = 512
    hidden_size = hidden_ref.shape[1]
    source = source_ref[...]
    predict = jnp.broadcast_to(b_out_ref[...], target_ref.shape)
    for start in range(0, hidden_size, chunk):
        lanes = slice(start, start + chunk)
        pre = jnp.dot(source, w_in_ref[:, lanes], preferred_element_type=jnp.float32)
        pre = pre + b_in_ref[:, lanes]
        sigma = jax.nn.sigmoid(pre)
        hidden = (pre * sigma).astype(jnp.bfloat16)
        hidden_ref[:, lanes] = hidden
        slope_ref[:, lanes] = sigma * (1.0 + pre * (1.0 - sigma))
        predict = predict + jnp.dot(
            hidden, w_out_ref[lanes], preferred_element_type=jnp.float32
        )
    wanted = target_ref[...]
    error = jnp.where(wanted < FULL_BELOW, error_weight * (predict - wanted), 0.0)
    error = error.astype(jnp.bfloat16)
    error_ref[...] = error
    b_out_grad_ref[...] = jnp.sum(error.astype(jnp.float32), axis=0, keepdims=True)
    total = jnp.zeros(target_ref.shape, jnp.float32)
    for start in range(0, hidden_size, chunk):
        lanes = slice(start, start + chunk)
        upstream = contract_cols(error, w_out_ref[lanes])
        pre_grad = (upstream * slope_ref[:, lanes]).astype(jnp.bfloat16)
        pre_grad_ref[:, lanes] = pre_grad
        b_in_grad_ref[:, lanes] = jnp.sum(
            pre_grad.astype(jnp.float32), axis=0, keepdims=True
        )
        total = total + contract_cols(pre_grad, w_in_ref[:, lanes])
    gradient = total.astype(jnp.bfloat16)
    out = lax.broadcasted_iota(jnp.int32, (large, small), 0)
    origin = lax.broadcasted_iota(jnp.int32, (large, small), 1)
    fits = origin == out // (2 * per) * per + out % per
    side = out // per % 2
    for at in range(rows // small):
        lines = slice(at * small, (at + 1) * small)
        block = jnp.zeros((large, width), jnp.float32)
        for half in range(2):
            move = jnp.where(fits & (side == half), 1.0, 0.0).astype(jnp.bfloat16)
            block = block + jnp.dot(
                move,
                gradient[lines, half * width : (half + 1) * width],
                preferred_element_type=jnp.float32,
            )
        back_ref[at * large : (at + 1) * large] = block.astype(jnp.bfloat16)


def gather_kernel(source_pick_ref, target_pick_ref, back_ref, out_ref):
    width = back_ref.shape[1]
    for half, pick_ref in enumerate((source_pick_ref, target_pick_ref)):
        out_ref[:, half * width : (half + 1) * width] = contract_rows(
            pick_ref[...], back_ref[...]
        ).astype(jnp.bfloat16)


def part_kernel(
    keep_hbm, got_hbm, own_grad_ref, other_grad_ref, part_ref, keep_ref, got_ref, loaded
):
    loads = (
        pltpu.make_async_copy(keep_hbm, keep_ref, loaded.at[0]),
        pltpu.make_async_copy(got_hbm, got_ref, loaded.at[1]),
    )
    for load in loads:
        load.start()
    half = keep_ref.shape[0]
    width = part_ref.shape[1]
    loads[0].wait()
    total = jnp.dot(keep_ref[...], own_grad_ref[...], preferred_element_type=jnp.float32)
    loads[1].wait()
    total = total + jnp.dot(
        got_ref[...], other_grad_ref[...], preferred_element_type=jnp.float32
    )
    for side in range(EMBED // width):
        part_ref[side * half : (side + 1) * half, :] = total[
            :, side * width : (side + 1) * width
        ].astype(jnp.bfloat16)


def sum_kernel(parts_ref, copies_ref):
    total = jnp.sum(parts_ref[...].astype(jnp.float32), axis=0).astype(jnp.bfloat16)
    copies_ref[...] = jnp.broadcast_to(total[None], copies_ref.shape)


def spread_kernel(other, edge_ref, half_ref, *rest):
    out_hbm, wide_ref, done = rest[-3:]
    half, width = wide_ref.shape[0], half_ref.shape[1]
    core = 1 - edge_ref[4] if other else edge_ref[4]
    begin = core * half
    pieces = 8
    stores = []
    for piece in range(pieces):
        lines = slice(piece * half // pieces, (piece + 1) * half // pieces)
        for side in range(EMBED // width):
            lanes = slice(side * width, (side + 1) * width)
            rows = slice(side * half + lines.start, side * half + lines.stop)
            wide_ref[lines, lanes] = half_ref[rows].astype(jnp.float32)
        at = pl.multiple_of(begin + lines.start, half // pieces)
        store = pltpu.make_async_copy(
            wide_ref.at[lines], out_hbm.at[pl.ds(at, half // pieces)], done.at[piece]
        )
        store.start()
        stores.append(store)
    for store in stores:
        store.wait()


def swapped(near_piece, far_piece, axis):
    count = lax.axis_size(axis)
    near = [(i, i ^ 1) for i in range(count)]
    far = [pair for i in range(1, count - 1, 2) for pair in ((i, i + 1), (i + 1, i))]
    return lax.ppermute(near_piece, axis, near), lax.ppermute(far_piece, axis, far)


def contract_rows(left, right):
    return lax.dot_general(
        left, right, (((0,), (0,)), ((), ())), preferred_element_type=jnp.float32
    )


def contract_cols(left, right):
    return lax.dot_general(
        left, right, (((1,), (1,)), ((), ())), preferred_element_type=jnp.float32
    )


def per_device(fields, patch_weight, trainer_of, lag_index, w_in, b_in, w_out, b_out):
    axes = ("gx", "gy")
    n_x, n_y = lax.axis_size("gx"), lax.axis_size("gy")
    devices = n_x * n_y
    _, wide_x, wide_y, wide_z = fields.shape
    patches = (wide_x // PATCH) * (wide_y // PATCH) * (wide_z // PATCH)
    blocks = patches // BLOCK_ROWS
    slots = max(2, 2 * blocks // devices)
    per = slots * BLOCK_ROWS
    features = FIELDS * PATCH**3

    at_x, at_y = lax.axis_index("gx"), lax.axis_index("gy")
    edges = jnp.stack(
        [
            at_x == 0,
            at_x == n_x - 1,
            at_y == 0,
            at_y == n_y - 1,
            at_x % 2 == 1,
            at_y % 2 == 1,
        ]
    ).astype(jnp.int32)
    own_patch = jnp.repeat(trainer_of[:, 0], BLOCK_ROWS)
    lag = lag_index.reshape(-1, lag_index.shape[2]).astype(jnp.float32)

    vmem = pl.BlockSpec(memory_space=pltpu.VMEM)
    smem = pl.BlockSpec(memory_space=pltpu.SMEM)
    hbm = pl.BlockSpec(memory_space=pltpu.HBM)

    def grant(mebibytes):
        return pltpu.CompilerParams(vmem_limit_bytes=mebibytes * 1024 * 1024)

    def shape(dims, kind):
        return jax.ShapeDtypeStruct(dims, kind)

    tall = wide_y + 2 * CORNER
    y_near, y_far = pl.pallas_call(
        y_faces_kernel,
        out_shape=(shape((FIELDS, REACH * wide_x, wide_z), jnp.bfloat16),) * 2,
        in_specs=[smem, hbm],
        out_specs=(vmem,) * 2,
        scratch_shapes=[
            pltpu.VMEM((2, FIELDS, wide_x, LIFT, wide_z), jnp.float32),
            pltpu.SemaphoreType.DMA((2,)),
        ],
        compiler_params=grant(61),
        name="y_faces",
    )(edges, fields)
    y_near, y_far = swapped(y_near, y_far, "gy")
    x_near, x_far = pl.pallas_call(
        x_faces_kernel,
        out_shape=(shape((FIELDS, REACH, tall, wide_z), jnp.bfloat16),) * 2,
        in_specs=[smem] + [vmem] * 3,
        out_specs=(vmem,) * 2,
        scratch_shapes=[pltpu.VMEM((FIELDS, 2, REACH * tall, wide_z), jnp.float32)],
        compiler_params=grant(8),
        name="x_faces",
    )(edges, fields, y_near, y_far)
    x_near, x_far = swapped(x_near, x_far, "gx")

    send_rows = 2 * devices * per
    source_pick, target_pick, chosen = pl.pallas_call(
        functools.partial(slots_kernel, slots),
        out_shape=(
            shape((send_rows, patches), jnp.bfloat16),
            shape((send_rows, patches), jnp.bfloat16),
            shape(((wide_x // PATCH) * wide_y, wide_z), jnp.float32),
        ),
        in_specs=[vmem] * 3,
        out_specs=(vmem,) * 3,
        compiler_params=grant(8),
        name="slots",
    )(own_patch[None, :], own_patch[:, None], lag)

    full = (FIELDS, wide_x + 2 * REACH, wide_y + 2 * LIFT, wide_z)
    new_fields, keep, give, send = pl.pallas_call(
        functools.partial(window_kernel, (wide_x, wide_y, wide_z), per),
        out_shape=(
            shape(fields.shape, jnp.float32),
            shape((features // 2, patches), jnp.bfloat16),
            shape((features // 2, patches), jnp.bfloat16),
            shape((send_rows, EMBED), jnp.bfloat16),
        ),
        in_specs=[smem] + [vmem] * 8 + [hbm],
        out_specs=(hbm,) * 4,
        scratch_shapes=[
            pltpu.VMEM(full, jnp.float32),
            pltpu.VMEM(full, jnp.float32),
            pltpu.VMEM((FIELDS, wide_x, wide_y, wide_z), jnp.float32),
            pltpu.VMEM((FIELDS * PATCH, PATCH * PATCH, patches), jnp.float32),
            pltpu.VMEM((features, 2 * patches), jnp.bfloat16),
            pltpu.VMEM((features, EMBED), jnp.bfloat16),
            pltpu.VMEM((FIELDS, wide_x, wide_y, wide_z), jnp.float32),
            pltpu.VMEM((send_rows, EMBED), jnp.bfloat16),
            pltpu.SemaphoreType.DMA((8,)),
        ],
        compiler_params=grant(50),
        name="window",
    )(
        edges,
        fields,
        x_near,
        x_far,
        y_near,
        y_far,
        chosen,
        source_pick,
        target_pick,
        patch_weight,
    )

    pairs = [(i, i ^ 1) for i in range(n_x)]
    groups = [
        [x * n_y + y for x in range(n_x) for y in range(n_y) if x % 2 == c] for c in range(2)
    ]
    members = devices // 2
    got_picked = lax.ppermute(give, "gx", pairs)
    got = lax.all_to_all(send.reshape(devices, 2 * per, EMBED), axes, 0, 0, tiled=True)
    rows = devices * per
    hidden_size = w_in.shape[2]
    width = EMBED // 2
    source, hidden, error, pre_grad, b_in_grad, b_out_grad, back = pl.pallas_call(
        functools.partial(trainer_kernel, per),
        out_shape=(
            shape((rows, EMBED), jnp.bfloat16),
            shape((rows, hidden_size), jnp.bfloat16),
            shape((rows, EMBED), jnp.bfloat16),
            shape((rows, hidden_size), jnp.bfloat16),
            shape((1, hidden_size), jnp.float32),
            shape((1, EMBED), jnp.float32),
            shape((2 * rows, width), jnp.bfloat16),
        ),
        in_specs=[vmem] * 5,
        out_specs=(vmem,) * 7,
        scratch_shapes=[
            pltpu.VMEM((rows, EMBED), jnp.float32),
            pltpu.VMEM((rows, hidden_size), jnp.float32),
        ],
        compiler_params=grant(50),
        name="trainer",
    )(got.reshape(send_rows, EMBED), w_in[0], b_in, w_out[0], b_out)
    back = lax.all_to_all(back.reshape(devices, 2 * per, width), axes, 0, 0, tiled=True)
    w_in_grad = contract_rows(source, pre_grad)
    w_out_grad = contract_rows(hidden, error)
    back, w_in_grad, w_out_grad = lax.optimization_barrier((back, w_in_grad, w_out_grad))
    own_grad = pl.pallas_call(
        gather_kernel,
        out_shape=shape((patches, EMBED), jnp.bfloat16),
        in_specs=[vmem] * 3,
        out_specs=vmem,
        compiler_params=grant(8),
        name="gather",
    )(source_pick, target_pick, back.reshape(send_rows, width))
    other_grad = lax.ppermute(own_grad, "gx", pairs)
    piece = features // members
    parts = pl.pallas_call(
        part_kernel,
        out_shape=shape((features, width), jnp.bfloat16),
        in_specs=[hbm, hbm, vmem, vmem],
        out_specs=vmem,
        scratch_shapes=[
            pltpu.VMEM((features // 2, patches), jnp.bfloat16),
            pltpu.VMEM((features // 2, patches), jnp.bfloat16),
            pltpu.SemaphoreType.DMA((2,)),
        ],
        compiler_params=grant(24),
        name="part",
    )(keep, got_picked, own_grad, other_grad)
    parts = lax.all_to_all(
        parts.reshape(members, piece, width), axes, 0, 0, axis_index_groups=groups, tiled=True
    )
    copies = pl.pallas_call(
        sum_kernel,
        out_shape=jax.ShapeDtypeStruct((members, piece, width), jnp.bfloat16),
        in_specs=[vmem],
        out_specs=vmem,
        compiler_params=grant(16),
        name="total",
    )(parts)
    own_half = lax.all_to_all(copies, axes, 0, 0, axis_index_groups=groups, tiled=True)
    own_half = own_half.reshape(features, width)
    other_half = lax.ppermute(own_half, "gx", pairs)

    def spread(other, *operands):
        return pl.pallas_call(
            functools.partial(spread_kernel, other),
            out_shape=shape((features, EMBED), jnp.float32),
            in_specs=[smem, vmem] + [hbm] * (len(operands) - 2),
            out_specs=hbm,
            scratch_shapes=[
                pltpu.VMEM((features // 2, EMBED), jnp.float32),
                pltpu.SemaphoreType.DMA((8,)),
            ],
            input_output_aliases={2: 0} if other else {},
            compiler_params=grant(8),
            name="spread_other" if other else "spread_own",
        )(*operands)

    patch_gradient = spread(False, edges, own_half)
    patch_gradient = spread(True, edges, other_half, patch_gradient)
    return (
        new_fields,
        patch_gradient,
        w_in_grad[None],
        b_in_grad,
        w_out_grad[None],
        b_out_grad,
    )


def solution(mesh):
    in_specs = (
        P(None, "gx", "gy", None),
        P(),
        P(("gx", "gy"), None),
        P("gx", "gy", None),
        P(("gx", "gy"), None, None),
        P(("gx", "gy"), None),
        P(("gx", "gy"), None, None),
        P(("gx", "gy"), None),
    )
    out_specs = (
        P(None, "gx", "gy", None),
        P(),
        P(("gx", "gy"), None, None),
        P(("gx", "gy"), None),
        P(("gx", "gy"), None, None),
        P(("gx", "gy"), None),
    )
    return jax.shard_map(
        per_device, mesh=mesh, in_specs=in_specs, out_specs=out_specs, check_vma=False
    )
```

```python
import functools

import jax
import jax.numpy as jnp
from jax import lax
from jax.experimental import pallas as pl
from jax.experimental.pallas import tpu as pltpu
from jax.sharding import PartitionSpec as P

FIELDS = 5
PATCH = 8
STEPS = 3
EMBED = 512
BLOCK_ROWS = 2
REACH = 2 * STEPS
LIFT = 8
EMPTY = 1.0e30
FULL_BELOW = 1.0e29

time_step = 0.2
viscosity = 0.5
drift_x = 0.6
drift_y = -0.4
drift_z = 0.3
error_weight = 0.0625

SLOPE = {-2: 1.0 / 12.0, -1: -8.0 / 12.0, 1: 8.0 / 12.0, 2: -1.0 / 12.0}
BEND = {-2: -1.0 / 12.0, -1: 16.0 / 12.0, 1: 16.0 / 12.0, 2: -1.0 / 12.0}
OFFSETS = (-2, -1, 1, 2)


def own_weights(drift):
    return {k: time_step * (viscosity * BEND[k] - drift * SLOPE[k]) for k in OFFSETS}


OWN_X, OWN_Y, OWN_Z = own_weights(drift_x), own_weights(drift_y), own_weights(drift_z)
MIDDLE = 1.0 - time_step * viscosity * 3.0 * 30.0 / 12.0
PUSH = {k: -time_step * SLOPE[k] for k in OFFSETS}


def rolled(value, offset, axis):
    size = value.shape[axis]
    return pltpu.roll(value, (-offset) % size, axis)


def weighted(pieces, weights):
    total = None
    for k in OFFSETS:
        term = pieces[k] * weights[k]
        total = term if total is None else total + term
    return total


def slope_of(pieces):
    return (pieces[-1] - pieces[1]) * PUSH[-1] + (pieces[2] - pieces[-2]) * PUSH[2]


def one_row(src, row, own_z, push_z, begin, end):
    def along(field):
        middle = src[field, row, begin:end]
        xs = {k: src[field, row + k, begin:end] for k in OFFSETS}
        ys = {k: src[field, row, begin + k : end + k] for k in OFFSETS}
        zs = {k: rolled(middle, k, 1) for k in OFFSETS}
        total = middle * MIDDLE + weighted(xs, OWN_X) + weighted(ys, OWN_Y)
        return total + weighted(zs, own_z), xs, ys, zs

    pressure, xs, ys, zs = along(4)
    px, py, pz = slope_of(xs), slope_of(ys), weighted(zs, push_z)
    first, xs, _, _ = along(1)
    first = first + px
    spread = slope_of(xs)
    second, _, ys, _ = along(2)
    second = second + py
    spread = spread + slope_of(ys)
    third, _, _, zs = along(3)
    third = third + pz
    spread = spread + weighted(zs, push_z)
    density = along(0)[0] + spread
    return density, first, second, third, pressure + spread


def slots_kernel(slots, own_row_ref, own_col_ref, lag_ref, source_ref, target_ref, chosen_ref):
    rows, patches = source_ref.shape
    per = slots * BLOCK_ROWS
    at_r = lax.broadcasted_iota(jnp.int32, (patches, patches), 0)
    at_c = lax.broadcasted_iota(jnp.int32, (patches, patches), 1)
    earlier = (at_r // BLOCK_ROWS < at_c // BLOCK_ROWS) & (at_r % BLOCK_ROWS == 0)
    hit = (own_row_ref[...] == own_col_ref[...]) & earlier
    rank = jnp.sum(jnp.where(hit, 1.0, 0.0), axis=0, keepdims=True).astype(jnp.int32)
    place = lax.broadcasted_iota(jnp.int32, (1, patches), 1) % BLOCK_ROWS
    at = own_row_ref[...] * (2 * per) + rank * BLOCK_ROWS + place
    row = lax.broadcasted_iota(jnp.int32, (rows, patches), 0)
    source_ref[...] = jnp.where(row == at, 1.0, 0.0).astype(jnp.bfloat16)
    target_ref[...] = jnp.where(row == at + per, 1.0, 0.0).astype(jnp.bfloat16)
    tall, wide = chosen_ref.shape
    bricks, deep = lag_ref.shape
    along = lax.broadcasted_iota(jnp.int32, (deep, wide), 0)
    cells = lax.broadcasted_iota(jnp.int32, (deep, wide), 1)
    spread = jnp.where(along == cells // PATCH, 1.0, 0.0).astype(jnp.bfloat16)
    lanes = jnp.dot(
        lag_ref[...].astype(jnp.bfloat16), spread, preferred_element_type=jnp.float32
    )
    line = lax.broadcasted_iota(jnp.int32, (tall, bricks), 0)
    brick = lax.broadcasted_iota(jnp.int32, (tall, bricks), 1)
    lift = jnp.where(line // PATCH == brick, 1.0, 0.0).astype(jnp.bfloat16)
    chosen_ref[...] = jnp.dot(
        lift, lanes.astype(jnp.bfloat16), preferred_element_type=jnp.float32
    )


CORNER = 4


def by_parity(parity, act, near_ref, far_ref):
    @pl.when(parity == 0)
    def _():
        act(far_ref, near_ref)

    @pl.when(parity == 1)
    def _():
        act(near_ref, far_ref)


def y_faces_kernel(edge_ref, f_ref, near_ref, far_ref, lines_ref):
    wide_x, wide_y = f_ref.shape[1], f_ref.shape[2]

    def write(first_ref, last_ref):
        for at, out_ref in ((0, first_ref), (wide_y - LIFT, last_ref)):
            for field in range(FIELDS):
                for row in range(wide_x):
                    lines_ref[row * LIFT : (row + 1) * LIFT] = f_ref[field, row, at : at + LIFT]
                for layer in range(REACH):
                    line = layer if at == 0 else LIFT - 1 - layer
                    out_ref[field, layer * wide_x : (layer + 1) * wide_x] = lines_ref[
                        pl.ds(line, wide_x, stride=LIFT), :
                    ].astype(jnp.bfloat16)

    by_parity(edge_ref[5], write, near_ref, far_ref)


def x_faces_kernel(edge_ref, f_ref, y_near_ref, y_far_ref, near_ref, far_ref, lines_ref):
    wide_x, wide_y = f_ref.shape[1], f_ref.shape[2]
    tall = wide_y + 2 * CORNER
    ends = (0, wide_x - REACH)

    def corners(ylo_ref, yhi_ref):
        for field in range(FIELDS):
            low = ylo_ref[field].astype(jnp.float32)
            high = yhi_ref[field].astype(jnp.float32)
            for end, at in enumerate(ends):
                for layer in range(CORNER):
                    rows = slice(layer * wide_x + at, layer * wide_x + at + REACH)
                    below, above = CORNER - 1 - layer, CORNER + wide_y + layer
                    lines_ref[field, end, pl.ds(below, REACH, stride=tall), :] = low[rows]
                    lines_ref[field, end, pl.ds(above, REACH, stride=tall), :] = high[rows]

    by_parity(edge_ref[5], corners, y_near_ref, y_far_ref)
    for field in range(FIELDS):
        for end, at in enumerate(ends):
            for row in range(REACH):
                begin = row * tall + CORNER
                lines_ref[field, end, begin : begin + wide_y] = f_ref[field, at + row]

    def write(first_ref, last_ref):
        for field in range(FIELDS):
            for end, out_ref in enumerate((first_ref, last_ref)):
                for row in range(REACH):
                    out_ref[field, row] = lines_ref[
                        field, end, row * tall : (row + 1) * tall
                    ].astype(jnp.bfloat16)

    by_parity(edge_ref[4], write, near_ref, far_ref)


def window_kernel(
    shape,
    per,
    edge_ref,
    f_ref,
    x_near_ref,
    x_far_ref,
    y_near_ref,
    y_far_ref,
    chosen_ref,
    source_pick_ref,
    target_pick_ref,
    w_hbm,
    new_hbm,
    keep_hbm,
    give_hbm,
    send_hbm,
    first_ref,
    second_ref,
    shuffle_ref,
    natural_ref,
    both_ref,
    w_ref,
    new_ref,
    send_ref,
    done,
):
    load_w = pltpu.make_async_copy(w_hbm, w_ref, done.at[0])
    load_w.start()
    wide_x, wide_y, wide_z = shape
    patches = (wide_x // PATCH) * (wide_y // PATCH) * (wide_z // PATCH)
    top_x, top_y = REACH + wide_x, LIFT + wide_y
    full_x, full_y = top_x + REACH, top_y + LIFT
    lane = lax.broadcasted_iota(jnp.int32, (1, wide_z), 1)
    inside = {k: (lane + k >= 0) & (lane + k < wide_z) for k in OFFSETS}
    own_z = {k: jnp.where(inside[k], OWN_Z[k], 0.0) for k in OFFSETS}
    push_z = {k: jnp.where(inside[k], PUSH[k], 0.0) for k in OFFSETS}

    first_ref[:, REACH:top_x, LIFT:top_y, :] = f_ref[...]
    reached = slice(LIFT - CORNER, top_y + CORNER)

    def beside_x(xlo_ref, xhi_ref):
        first_ref[:, 0:REACH, reached, :] = xlo_ref[...].astype(jnp.float32)
        first_ref[:, top_x:full_x, reached, :] = xhi_ref[...].astype(jnp.float32)

    def beside_y(ylo_ref, yhi_ref):
        for field in range(FIELDS):
            for low, face_ref in ((True, ylo_ref), (False, yhi_ref)):
                face = face_ref[field].astype(jnp.float32)
                for layer in range(REACH):
                    line = LIFT - 1 - layer if low else top_y + layer
                    first_ref[field, REACH:top_x, line, :] = face[
                        layer * wide_x : (layer + 1) * wide_x
                    ]

    by_parity(edge_ref[4], beside_x, x_near_ref, x_far_ref)
    by_parity(edge_ref[5], beside_y, y_near_ref, y_far_ref)

    def clear(ref, least):
        @pl.when(edge_ref[0] == 1)
        def _():
            ref[:, least:REACH] = jnp.zeros((FIELDS, REACH - least, full_y, wide_z), jnp.float32)

        @pl.when(edge_ref[1] == 1)
        def _():
            ref[:, top_x : full_x - least] = jnp.zeros(
                (FIELDS, REACH - least, full_y, wide_z), jnp.float32
            )

        @pl.when(edge_ref[2] == 1)
        def _():
            ref[:, :, 0:LIFT] = jnp.zeros((FIELDS, full_x, LIFT, wide_z), jnp.float32)

        @pl.when(edge_ref[3] == 1)
        def _():
            ref[:, :, top_y:full_y] = jnp.zeros((FIELDS, full_x, LIFT, wide_z), jnp.float32)

    def step(src, dst, least):
        begin = LIFT - REACH + least
        end = begin + wide_y + LIFT

        def body(row, carry):
            done = one_row(src, row, own_z, push_z, begin, end)
            for field in range(FIELDS):
                dst[field, row, begin:end] = done[field]
            return carry

        lax.fori_loop(least, full_x - least, body, 0, unroll=8 if least == 2 else 4)
        clear(dst, least)

    def last_step(src):
        def body(row, carry):
            done = one_row(src, row, own_z, push_z, LIFT, top_y)
            for field in range(FIELDS):
                new_ref[field, row - REACH] = done[field]
            return carry

        lax.fori_loop(REACH, top_x, body, 0, unroll=8)

    z_count = wide_z // PATCH
    lane_r = lax.broadcasted_iota(jnp.int32, (wide_z, wide_z), 0)
    lane_c = lax.broadcasted_iota(jnp.int32, (wide_z, wide_z), 1)
    swap = jnp.where(
        (lane_r // PATCH == lane_c % z_count) & (lane_r % PATCH == lane_c // z_count), 1.0, 0.0
    ).astype(jnp.bfloat16)
    group = lax.broadcasted_iota(jnp.int32, (PATCH, wide_z), 1) // z_count

    def into_patches(load, store):
        for field in range(FIELDS):
            flat = load(field).reshape(wide_x * wide_y, wide_z)
            shuffle_ref[field] = jnp.dot(
                flat.astype(jnp.bfloat16), swap, preferred_element_type=jnp.float32
            ).reshape(wide_x, wide_y, wide_z)

        for field in range(FIELDS):
            tiles = [
                shuffle_ref[
                    field, px * PATCH : (px + 1) * PATCH, py * PATCH : (py + 1) * PATCH
                ]
                for px in range(wide_x // PATCH)
                for py in range(wide_y // PATCH)
            ]
            for bit in (4, 2, 1):
                low = ((group & bit) == 0)[None]
                fresh = list(tiles)
                for i in range(PATCH):
                    if i & bit:
                        continue
                    a, b = tiles[i], tiles[i | bit]
                    fresh[i] = jnp.where(low, a, pltpu.roll(b, bit * z_count, 2))
                    fresh[i | bit] = jnp.where(
                        low, pltpu.roll(a, wide_z - bit * z_count, 2), b
                    )
                tiles = fresh
            for inner_z in range(PATCH):
                natural_ref[
                    field * PATCH : (field + 1) * PATCH, pl.ds(inner_z, PATCH, stride=PATCH), :
                ] = tiles[inner_z]

        for field in range(FIELDS):
            block = natural_ref[field * PATCH : (field + 1) * PATCH]
            block = block.reshape(PATCH**3, patches).astype(jnp.bfloat16)
            store(field * PATCH**3, block)

    def keep_picked(at, block):
        both_ref[at : at + PATCH**3, 0:patches] = block

    def keep_target(at, block):
        both_ref[at : at + PATCH**3, patches : 2 * patches] = block

    def chosen(field):
        one = second_ref[field, REACH:top_x, LIFT:top_y]
        two = first_ref[field, REACH:top_x, LIFT:top_y]
        one = one.reshape(wide_x // PATCH, PATCH, wide_y, wide_z)
        two = two.reshape(wide_x // PATCH, PATCH, wide_y, wide_z)
        later = chosen_ref[...].reshape(wide_x // PATCH, 1, wide_y, wide_z)
        return jnp.where(later == 1.0, two, one)

    step(first_ref, second_ref, 2)
    step(second_ref, first_ref, 4)
    last_step(first_ref)
    store_new = pltpu.make_async_copy(new_ref, new_hbm, done.at[1])
    store_new.start()
    into_patches(chosen, keep_picked)
    into_patches(lambda field: new_ref[field], keep_target)

    half = both_ref.shape[0] // 2
    mine = pl.multiple_of(edge_ref[4] * half, half)
    lanes = slice(0, patches)
    store_keep = pltpu.make_async_copy(both_ref.at[pl.ds(mine, half), lanes], keep_hbm, done.at[2])
    store_give = pltpu.make_async_copy(
        both_ref.at[pl.ds(half - mine, half), lanes], give_hbm, done.at[3]
    )
    store_give.start()
    store_keep.start()
    load_w.wait()
    embedded = contract_rows(both_ref[...], w_ref[...]).astype(jnp.bfloat16)
    rows = send_ref.shape[0]
    pieces = 4
    stores = []
    for piece in range(pieces):
        lines = slice(piece * rows // pieces, (piece + 1) * rows // pieces)
        wanted = target_pick_ref[lines]
        filled = jnp.sum(wanted.astype(jnp.float32), axis=1, keepdims=True)
        line = lax.broadcasted_iota(jnp.int32, (rows // pieces, 1), 0)
        marker = jnp.where((line // per % 2 == 1) & (filled == 0.0), EMPTY, 0.0)
        placed = jnp.dot(
            source_pick_ref[lines], embedded[0:patches], preferred_element_type=jnp.float32
        )
        placed = placed + jnp.dot(
            wanted, embedded[patches : 2 * patches], preferred_element_type=jnp.float32
        )
        send_ref[lines] = (placed + marker).astype(jnp.bfloat16)
        store = pltpu.make_async_copy(send_ref.at[lines], send_hbm.at[lines], done.at[4 + piece])
        store.start()
        stores.append(store)
    for store in [store_new, store_keep, store_give] + stores:
        store.wait()


def trainer_kernel(
    per,
    got_ref,
    w_in_ref,
    b_in_ref,
    w_out_ref,
    b_out_ref,
    source_ref,
    hidden_ref,
    error_ref,
    pre_grad_ref,
    b_in_grad_ref,
    b_out_grad_ref,
    back_ref,
    target_ref,
    slope_ref,
):
    rows = source_ref.shape[0]
    width = back_ref.shape[1]
    small, large = 32 * per, 64 * per
    line = lax.broadcasted_iota(jnp.int32, (small, large), 0)
    taken = lax.broadcasted_iota(jnp.int32, (small, large), 1)
    first = line // per * (2 * per) + line % per
    source_pick = jnp.where(taken == first, 1.0, 0.0).astype(jnp.bfloat16)
    target_pick = jnp.where(taken == first + per, 1.0, 0.0).astype(jnp.bfloat16)
    for at in range(rows // small):
        block = got_ref[at * large : (at + 1) * large]
        lines = slice(at * small, (at + 1) * small)
        source_ref[lines] = jnp.dot(
            source_pick, block, preferred_element_type=jnp.float32
        ).astype(jnp.bfloat16)
        target_ref[lines] = jnp.dot(target_pick, block, preferred_element_type=jnp.float32)

    chunk = 512
    hidden_size = hidden_ref.shape[1]
    source = source_ref[...]
    predict = jnp.broadcast_to(b_out_ref[...], target_ref.shape)
    for start in range(0, hidden_size, chunk):
        lanes = slice(start, start + chunk)
        pre = jnp.dot(source, w_in_ref[:, lanes], preferred_element_type=jnp.float32)
        pre = pre + b_in_ref[:, lanes]
        sigma = jax.nn.sigmoid(pre)
        hidden = (pre * sigma).astype(jnp.bfloat16)
        hidden_ref[:, lanes] = hidden
        slope_ref[:, lanes] = sigma * (1.0 + pre * (1.0 - sigma))
        predict = predict + jnp.dot(
            hidden, w_out_ref[lanes], preferred_element_type=jnp.float32
        )
    wanted = target_ref[...]
    error = jnp.where(wanted < FULL_BELOW, error_weight * (predict - wanted), 0.0)
    error = error.astype(jnp.bfloat16)
    error_ref[...] = error
    b_out_grad_ref[...] = jnp.sum(error.astype(jnp.float32), axis=0, keepdims=True)
    total = jnp.zeros(target_ref.shape, jnp.float32)
    for start in range(0, hidden_size, chunk):
        lanes = slice(start, start + chunk)
        upstream = contract_cols(error, w_out_ref[lanes])
        pre_grad = (upstream * slope_ref[:, lanes]).astype(jnp.bfloat16)
        pre_grad_ref[:, lanes] = pre_grad
        b_in_grad_ref[:, lanes] = jnp.sum(
            pre_grad.astype(jnp.float32), axis=0, keepdims=True
        )
        total = total + contract_cols(pre_grad, w_in_ref[:, lanes])
    gradient = total.astype(jnp.bfloat16)
    out = lax.broadcasted_iota(jnp.int32, (large, small), 0)
    origin = lax.broadcasted_iota(jnp.int32, (large, small), 1)
    fits = origin == out // (2 * per) * per + out % per
    side = out // per % 2
    for at in range(rows // small):
        lines = slice(at * small, (at + 1) * small)
        block = jnp.zeros((large, width), jnp.float32)
        for half in range(2):
            move = jnp.where(fits & (side == half), 1.0, 0.0).astype(jnp.bfloat16)
            block = block + jnp.dot(
                move,
                gradient[lines, half * width : (half + 1) * width],
                preferred_element_type=jnp.float32,
            )
        back_ref[at * large : (at + 1) * large] = block.astype(jnp.bfloat16)


def gather_kernel(source_pick_ref, target_pick_ref, back_ref, out_ref):
    width = back_ref.shape[1]
    for half, pick_ref in enumerate((source_pick_ref, target_pick_ref)):
        out_ref[:, half * width : (half + 1) * width] = contract_rows(
            pick_ref[...], back_ref[...]
        ).astype(jnp.bfloat16)


def part_kernel(
    keep_hbm, got_hbm, own_grad_ref, other_grad_ref, part_ref, keep_ref, got_ref, loaded
):
    loads = (
        pltpu.make_async_copy(keep_hbm, keep_ref, loaded.at[0]),
        pltpu.make_async_copy(got_hbm, got_ref, loaded.at[1]),
    )
    for load in loads:
        load.start()
    half = keep_ref.shape[0]
    width = part_ref.shape[1]
    loads[0].wait()
    total = jnp.dot(keep_ref[...], own_grad_ref[...], preferred_element_type=jnp.float32)
    loads[1].wait()
    total = total + jnp.dot(
        got_ref[...], other_grad_ref[...], preferred_element_type=jnp.float32
    )
    for side in range(EMBED // width):
        part_ref[side * half : (side + 1) * half, :] = total[
            :, side * width : (side + 1) * width
        ].astype(jnp.bfloat16)


def sum_kernel(parts_ref, copies_ref):
    total = jnp.sum(parts_ref[...].astype(jnp.float32), axis=0).astype(jnp.bfloat16)
    copies_ref[...] = jnp.broadcast_to(total[None], copies_ref.shape)


def spread_kernel(other, edge_ref, half_ref, *rest):
    out_hbm, wide_ref, done = rest[-3:]
    half, width = wide_ref.shape[0], half_ref.shape[1]
    core = 1 - edge_ref[4] if other else edge_ref[4]
    begin = core * half
    pieces = 4
    stores = []
    for piece in range(pieces):
        lines = slice(piece * half // pieces, (piece + 1) * half // pieces)
        for side in range(EMBED // width):
            lanes = slice(side * width, (side + 1) * width)
            rows = slice(side * half + lines.start, side * half + lines.stop)
            wide_ref[lines, lanes] = half_ref[rows].astype(jnp.float32)
        at = pl.multiple_of(begin + lines.start, half // pieces)
        store = pltpu.make_async_copy(
            wide_ref.at[lines], out_hbm.at[pl.ds(at, half // pieces)], done.at[piece]
        )
        store.start()
        stores.append(store)
    for store in stores:
        store.wait()


def swapped(near_piece, far_piece, axis):
    count = lax.axis_size(axis)
    near = [(i, i ^ 1) for i in range(count)]
    far = [pair for i in range(1, count - 1, 2) for pair in ((i, i + 1), (i + 1, i))]
    return lax.ppermute(near_piece, axis, near), lax.ppermute(far_piece, axis, far)


def contract_rows(left, right):
    return lax.dot_general(
        left, right, (((0,), (0,)), ((), ())), preferred_element_type=jnp.float32
    )


def contract_cols(left, right):
    return lax.dot_general(
        left, right, (((1,), (1,)), ((), ())), preferred_element_type=jnp.float32
    )


def per_device(fields, patch_weight, trainer_of, lag_index, w_in, b_in, w_out, b_out):
    axes = ("gx", "gy")
    n_x, n_y = lax.axis_size("gx"), lax.axis_size("gy")
    devices = n_x * n_y
    _, wide_x, wide_y, wide_z = fields.shape
    patches = (wide_x // PATCH) * (wide_y // PATCH) * (wide_z // PATCH)
    blocks = patches // BLOCK_ROWS
    slots = max(2, 2 * blocks // devices)
    per = slots * BLOCK_ROWS
    features = FIELDS * PATCH**3

    at_x, at_y = lax.axis_index("gx"), lax.axis_index("gy")
    edges = jnp.stack(
        [
            at_x == 0,
            at_x == n_x - 1,
            at_y == 0,
            at_y == n_y - 1,
            at_x % 2 == 1,
            at_y % 2 == 1,
        ]
    ).astype(jnp.int32)
    own_patch = jnp.repeat(trainer_of[:, 0], BLOCK_ROWS)
    lag = lag_index.reshape(-1, lag_index.shape[2]).astype(jnp.float32)

    vmem = pl.BlockSpec(memory_space=pltpu.VMEM)
    smem = pl.BlockSpec(memory_space=pltpu.SMEM)
    hbm = pl.BlockSpec(memory_space=pltpu.HBM)

    def grant(mebibytes):
        return pltpu.CompilerParams(vmem_limit_bytes=mebibytes * 1024 * 1024)

    def shape(dims, kind):
        return jax.ShapeDtypeStruct(dims, kind)

    tall = wide_y + 2 * CORNER
    y_near, y_far = pl.pallas_call(
        y_faces_kernel,
        out_shape=(shape((FIELDS, REACH * wide_x, wide_z), jnp.bfloat16),) * 2,
        in_specs=[smem, vmem],
        out_specs=(vmem,) * 2,
        scratch_shapes=[pltpu.VMEM((wide_x * LIFT, wide_z), jnp.float32)],
        compiler_params=grant(8),
        name="y_faces",
    )(edges, fields)
    y_near, y_far = swapped(y_near, y_far, "gy")
    x_near, x_far = pl.pallas_call(
        x_faces_kernel,
        out_shape=(shape((FIELDS, REACH, tall, wide_z), jnp.bfloat16),) * 2,
        in_specs=[smem] + [vmem] * 3,
        out_specs=(vmem,) * 2,
        scratch_shapes=[pltpu.VMEM((FIELDS, 2, REACH * tall, wide_z), jnp.float32)],
        compiler_params=grant(8),
        name="x_faces",
    )(edges, fields, y_near, y_far)
    x_near, x_far = swapped(x_near, x_far, "gx")

    send_rows = 2 * devices * per
    source_pick, target_pick, chosen = pl.pallas_call(
        functools.partial(slots_kernel, slots),
        out_shape=(
            shape((send_rows, patches), jnp.bfloat16),
            shape((send_rows, patches), jnp.bfloat16),
            shape(((wide_x // PATCH) * wide_y, wide_z), jnp.float32),
        ),
        in_specs=[vmem] * 3,
        out_specs=(vmem,) * 3,
        compiler_params=grant(8),
        name="slots",
    )(own_patch[None, :], own_patch[:, None], lag)

    full = (FIELDS, wide_x + 2 * REACH, wide_y + 2 * LIFT, wide_z)
    new_fields, keep, give, send = pl.pallas_call(
        functools.partial(window_kernel, (wide_x, wide_y, wide_z), per),
        out_shape=(
            shape(fields.shape, jnp.float32),
            shape((features // 2, patches), jnp.bfloat16),
            shape((features // 2, patches), jnp.bfloat16),
            shape((send_rows, EMBED), jnp.bfloat16),
        ),
        in_specs=[smem] + [vmem] * 8 + [hbm],
        out_specs=(hbm,) * 4,
        scratch_shapes=[
            pltpu.VMEM(full, jnp.float32),
            pltpu.VMEM(full, jnp.float32),
            pltpu.VMEM((FIELDS, wide_x, wide_y, wide_z), jnp.float32),
            pltpu.VMEM((FIELDS * PATCH, PATCH * PATCH, patches), jnp.float32),
            pltpu.VMEM((features, 2 * patches), jnp.bfloat16),
            pltpu.VMEM((features, EMBED), jnp.bfloat16),
            pltpu.VMEM((FIELDS, wide_x, wide_y, wide_z), jnp.float32),
            pltpu.VMEM((send_rows, EMBED), jnp.bfloat16),
            pltpu.SemaphoreType.DMA((8,)),
        ],
        compiler_params=grant(50),
        name="window",
    )(
        edges,
        fields,
        x_near,
        x_far,
        y_near,
        y_far,
        chosen,
        source_pick,
        target_pick,
        patch_weight,
    )

    pairs = [(i, i ^ 1) for i in range(n_x)]
    groups = [
        [x * n_y + y for x in range(n_x) for y in range(n_y) if x % 2 == c] for c in range(2)
    ]
    members = devices // 2
    got_picked = lax.ppermute(give, "gx", pairs)
    got = lax.all_to_all(send.reshape(devices, 2 * per, EMBED), axes, 0, 0, tiled=True)
    rows = devices * per
    hidden_size = w_in.shape[2]
    width = EMBED // 2
    source, hidden, error, pre_grad, b_in_grad, b_out_grad, back = pl.pallas_call(
        functools.partial(trainer_kernel, per),
        out_shape=(
            shape((rows, EMBED), jnp.bfloat16),
            shape((rows, hidden_size), jnp.bfloat16),
            shape((rows, EMBED), jnp.bfloat16),
            shape((rows, hidden_size), jnp.bfloat16),
            shape((1, hidden_size), jnp.float32),
            shape((1, EMBED), jnp.float32),
            shape((2 * rows, width), jnp.bfloat16),
        ),
        in_specs=[vmem] * 5,
        out_specs=(vmem,) * 7,
        scratch_shapes=[
            pltpu.VMEM((rows, EMBED), jnp.float32),
            pltpu.VMEM((rows, hidden_size), jnp.float32),
        ],
        compiler_params=grant(50),
        name="trainer",
    )(got.reshape(send_rows, EMBED), w_in[0], b_in, w_out[0], b_out)
    back = lax.all_to_all(back.reshape(devices, 2 * per, width), axes, 0, 0, tiled=True)
    w_in_grad = contract_rows(source, pre_grad)
    w_out_grad = contract_rows(hidden, error)
    back, w_in_grad, w_out_grad = lax.optimization_barrier((back, w_in_grad, w_out_grad))
    own_grad = pl.pallas_call(
        gather_kernel,
        out_shape=shape((patches, EMBED), jnp.bfloat16),
        in_specs=[vmem] * 3,
        out_specs=vmem,
        compiler_params=grant(8),
        name="gather",
    )(source_pick, target_pick, back.reshape(send_rows, width))
    other_grad = lax.ppermute(own_grad, "gx", pairs)
    piece = features // members
    parts = pl.pallas_call(
        part_kernel,
        out_shape=shape((features, width), jnp.bfloat16),
        in_specs=[hbm, hbm, vmem, vmem],
        out_specs=vmem,
        scratch_shapes=[
            pltpu.VMEM((features // 2, patches), jnp.bfloat16),
            pltpu.VMEM((features // 2, patches), jnp.bfloat16),
            pltpu.SemaphoreType.DMA((2,)),
        ],
        compiler_params=grant(24),
        name="part",
    )(keep, got_picked, own_grad, other_grad)
    parts = lax.all_to_all(
        parts.reshape(members, piece, width), axes, 0, 0, axis_index_groups=groups, tiled=True
    )
    copies = pl.pallas_call(
        sum_kernel,
        out_shape=jax.ShapeDtypeStruct((members, piece, width), jnp.bfloat16),
        in_specs=[vmem],
        out_specs=vmem,
        compiler_params=grant(16),
        name="total",
    )(parts)
    own_half = lax.all_to_all(copies, axes, 0, 0, axis_index_groups=groups, tiled=True)
    own_half = own_half.reshape(features, width)
    other_half = lax.ppermute(own_half, "gx", pairs)

    def spread(other, *operands):
        return pl.pallas_call(
            functools.partial(spread_kernel, other),
            out_shape=shape((features, EMBED), jnp.float32),
            in_specs=[smem, vmem] + [hbm] * (len(operands) - 2),
            out_specs=hbm,
            scratch_shapes=[
                pltpu.VMEM((features // 2, EMBED), jnp.float32),
                pltpu.SemaphoreType.DMA((4,)),
            ],
            input_output_aliases={2: 0} if other else {},
            compiler_params=grant(8),
            name="spread_other" if other else "spread_own",
        )(*operands)

    patch_gradient = spread(False, edges, own_half)
    patch_gradient = spread(True, edges, other_half, patch_gradient)
    return (
        new_fields,
        patch_gradient,
        w_in_grad[None],
        b_in_grad,
        w_out_grad[None],
        b_out_grad,
    )


def solution(mesh):
    in_specs = (
        P(None, "gx", "gy", None),
        P(),
        P(("gx", "gy"), None),
        P("gx", "gy", None),
        P(("gx", "gy"), None, None),
        P(("gx", "gy"), None),
        P(("gx", "gy"), None, None),
        P(("gx", "gy"), None),
    )
    out_specs = (
        P(None, "gx", "gy", None),
        P(),
        P(("gx", "gy"), None, None),
        P(("gx", "gy"), None),
        P(("gx", "gy"), None, None),
        P(("gx", "gy"), None),
    )
    return jax.shard_map(
        per_device, mesh=mesh, in_specs=in_specs, out_specs=out_specs, check_vma=False
    )
```
